128 devices in a mesh: seq: 32 (over x, y, core), chan: 4 (over z).
Axes of the slice: x: 4, y: 4, z: 4, core: 2. Of those that a mesh axis runs over, the one named last changes fastest.
Arguments:
- tokens: bfloat16 [16384, 8192], P('seq'), may hold values from -6 to 6
- proj_weight: bfloat16 [8192, 3, 2048], P('seq', None, 'chan'), may hold values from -0.0625 to 0.0625
- residues: float32 [16, 2048], P(None, 'chan'), may hold values from -1.5 to 1.5
- decay_rates: float32 [16, 2048], P(None, 'chan'), may hold values from 3.0517578e-05 to 0.05
- skip_gain: float32 [2048], P('chan'), may hold values from -3 to 3
- grad_out: bfloat16 [16384, 2048], P('seq', 'chan'), may hold values from -6 to 6
Outputs:
- gated_output: bfloat16 [16384, 2048], P('seq', 'chan')
- grad_tokens: bfloat16 [16384, 8192], P('seq', 'chan')
The draws below stay inside these ranges and needn't reach their ends.
All inputs are finite; a program needn't handle non-finite values.
Results may differ from the reference program's by a relative error of at most 0.022.
Values may be sent and summed in bfloat16 or wider, within the bound.
A program may use at most 128 MiB of HBM per device.

```python
import jax
import jax.numpy as jnp
from jax import lax

D = 8192
C = 2048
MODES = 16
TOKENS = 16384
N_CHAN = 4


def draw_decay_rates(key, part):
    lowest = 0.5 / TOKENS
    highest = 0.05
    spread = jax.random.uniform(key, (MODES, C), jnp.float32)
    return lowest * jnp.exp(spread * jnp.log(highest / lowest))


def shard_levels(rng, dims, cuts, smallest, top_value):
    def one(axis_at, blocks):
        steps = jax.random.uniform(jax.random.fold_in(jax.random.fold_in(rng, 6), axis_at), (blocks,), jnp.float32, smallest / len(cuts), top_value / len(cuts))
        return jnp.repeat(jnp.exp(steps), dims[axis_at] // blocks).reshape((-1,) + (1,) * (len(dims) - axis_at - 1))

    level = one(*cuts[0])
    for cut in cuts[1:]:
        level = level * one(*cut)
    return level


def gaussian(rng, shape, deviation, most, pieces=(), kind=jnp.bfloat16):
    entries = deviation * jax.random.normal(rng, shape, jnp.float32)
    if pieces:
        entries = entries * shard_levels(rng, shape, pieces, -0.22, 0.18)
    return jnp.clip(entries, -most, most).astype(kind)


def setup_inputs(seed: int = 0) -> dict:
    keys = jax.random.split(jax.random.key(seed), 7)
    return {
        "tokens": gaussian(keys[0], (TOKENS, D), 1.0, 6.0, ((0, 32),)),
        "proj_weight": gaussian(keys[1], (D, 3, C), D ** -0.5, 0.0625, ((0, 32), (2, 4))),
        "residues": gaussian(keys[2], (MODES, C), 0.25, 1.5, ((1, 4),), jnp.float32),
        "decay_rates": draw_decay_rates(jax.random.fold_in(keys[6], 71), 0),
        "skip_gain": gaussian(keys[4], (C,), 0.5, 3.0, ((0, 4),), jnp.float32),
        "grad_out": gaussian(keys[5], (TOKENS, C), 1.0, 6.0, ((0, 32), (1, 4))),
    }


def modal_scan(signal, decay_step, mode_gain, backward):

    def advance(mode_state, token_row):
        mode_state = decay_step * mode_state + token_row[None, :]
        return (mode_state, lax.optimization_barrier(jnp.sum(mode_gain * mode_state, axis=0)))
    _, outputs = lax.scan(advance, jnp.zeros(decay_step.shape, jnp.float32), signal, reverse=backward)
    return outputs

def reference(tokens, proj_weight, residues, decay_rates, skip_gain, grad_out):
    flat_w = proj_weight.reshape(D, 3 * C)
    projected = jnp.dot(tokens, flat_w, preferred_element_type=jnp.float32)
    proj_vals = lax.optimization_barrier(projected.astype(jnp.bfloat16)).astype(jnp.float32).reshape(TOKENS, 3, C)
    query_in = proj_vals[:, 0]
    key_in = proj_vals[:, 1]
    value_in = proj_vals[:, 2]
    decay_step = jnp.exp(-decay_rates)
    mode_gain = residues * jnp.sqrt(-jnp.expm1(-2.0 * decay_rates))
    mixed_in = key_in * value_in
    filtered = modal_scan(mixed_in, decay_step, mode_gain, False) + skip_gain[None, :] * mixed_in
    gated_output = (query_in * filtered).astype(jnp.bfloat16)
    grad_gate = grad_out.astype(jnp.float32)
    grad_mix = grad_gate * query_in
    grad_query = grad_gate * filtered
    grad_conv = modal_scan(grad_mix, decay_step, mode_gain, True) + skip_gain[None, :] * grad_mix
    grad_proj = jnp.stack([grad_query, grad_conv * value_in, grad_conv * key_in], axis=1).astype(jnp.bfloat16)
    group_width = C // N_CHAN
    grouped = grad_proj.reshape(TOKENS, 3, N_CHAN, group_width)
    w_grouped = proj_weight.reshape(D, 3, N_CHAN, group_width)

    def add_group(group_id, running):
        grad_slab = lax.dynamic_index_in_dim(grouped, group_id, 2, keepdims=False).reshape(TOKENS, 3 * group_width)
        weight_slab = lax.dynamic_index_in_dim(w_grouped, group_id, 2, keepdims=False).reshape(D, 3 * group_width)
        slab_term = lax.dot_general(grad_slab, weight_slab, (((1,), (1,)), ((), ())), preferred_element_type=jnp.float32)
        return running + lax.optimization_barrier(slab_term.astype(jnp.bfloat16)).astype(jnp.float32)
    summed = lax.fori_loop(0, N_CHAN, add_group, jnp.zeros((TOKENS, D), jnp.float32))
    return (gated_output, summed.astype(jnp.bfloat16))
```

```python
import math

import jax
import jax.numpy as jnp
from jax import lax
from jax.sharding import PartitionSpec as P

f32 = jnp.float32
bf16 = jnp.bfloat16


def dft_tables(block_len):
    n_len = 2 * block_len
    k = jnp.arange(block_len, dtype=jnp.int32)[:, None]
    n = jnp.arange(block_len, dtype=jnp.int32)[None, :]
    phase = (k * n) % n_len
    angle = (2.0 * math.pi / n_len) * phase.astype(f32)
    cos_rows = jnp.cos(angle)
    sin_rows = jnp.sin(angle)
    nyquist = jnp.where(n % 2 == 0, 1.0, -1.0).astype(f32)
    sin_rows = jnp.where(k == 0, nyquist, sin_rows)
    fwd = jnp.concatenate([cos_rows, sin_rows], axis=0)
    weight = jnp.where(k == 0, 1.0, 2.0).astype(f32) / n_len
    inv = (jnp.concatenate([cos_rows * weight, sin_rows * weight], axis=0)).T
    return fwd, inv


def spectral_conv(signal, fwd, inv, h_a, h_a2, h_b):
    block_len = signal.shape[0]
    spec = jnp.dot(fwd, signal.astype(bf16), preferred_element_type=f32)
    xc = spec[:block_len]
    xs = spec[block_len:]
    pr = xc * h_a - xs * h_b
    pi = xc * h_b + xs * h_a2
    prod = jnp.concatenate([pr, pi], axis=0).astype(bf16)
    return jnp.dot(inv, prod, preferred_element_type=f32)


def local(tokens, proj_weight, residues, decay_rates, skip_gain, grad_out):
    tok_rows = tokens.shape[0]
    chan_count = skip_gain.shape[0]
    seq_count = lax.axis_size("seq")
    me = lax.axis_index("seq")
    flat_w = proj_weight.reshape(proj_weight.shape[0], 3 * chan_count)
    whole_w = lax.all_gather(flat_w, "seq", axis=0, tiled=True)
    projected = jnp.dot(tokens, whole_w, preferred_element_type=f32)
    proj_vals = (
        lax.optimization_barrier(projected.astype(bf16))
        .astype(f32)
        .reshape(tok_rows, 3, chan_count)
    )
    query_in = proj_vals[:, 0]
    key_in = proj_vals[:, 1]
    value_in = proj_vals[:, 2]
    mixed_in = key_in * value_in
    grad_gate = grad_out.astype(f32)
    grad_mix = grad_gate * query_in

    rates = decay_rates
    mode_gain = residues * jnp.sqrt(-jnp.expm1(-2.0 * rates))
    steps = jnp.arange(tok_rows, dtype=f32)

    fwd_w = jnp.exp(-rates[:, None, :] * (tok_rows - 1 - steps)[None, :, None])
    bwd_w = jnp.exp(-rates[:, None, :] * steps[None, :, None])
    end_fwd = jnp.sum(fwd_w * mixed_in[None], axis=1)
    end_bwd = jnp.sum(bwd_w * grad_mix[None], axis=1)
    states = jnp.stack([end_fwd, end_bwd])
    every = lax.all_gather(states, "seq")

    others = jnp.arange(seq_count, dtype=jnp.int32)
    gap_f = me - 1 - others
    gap_b = others - me - 1
    span = rates[None] * float(tok_rows)
    w_f = jnp.where(
        (gap_f >= 0)[:, None, None],
        jnp.exp(-span * jnp.maximum(gap_f, 0).astype(f32)[:, None, None]),
        0.0,
    )
    w_b = jnp.where(
        (gap_b >= 0)[:, None, None],
        jnp.exp(-span * jnp.maximum(gap_b, 0).astype(f32)[:, None, None]),
        0.0,
    )
    into_f = jnp.sum(w_f * every[:, 0], axis=0) * mode_gain
    into_b = jnp.sum(w_b * every[:, 1], axis=0) * mode_gain

    taps = jnp.sum(mode_gain[:, None, :] * bwd_w, axis=0)
    fwd, inv = dft_tables(tok_rows)
    fwd_b = fwd.astype(bf16)
    inv_b = inv.astype(bf16)
    spec = jnp.dot(fwd, taps, precision=lax.Precision.HIGHEST)
    row0 = (jnp.arange(tok_rows) == 0)[:, None]
    h_a = spec[:tok_rows]
    h_a2 = jnp.where(row0, spec[tok_rows:tok_rows + 1], h_a)
    h_b = jnp.where(row0, 0.0, spec[tok_rows:])

    local_f = spectral_conv(mixed_in, fwd_b, inv_b, h_a, h_a2, h_b)
    carry_f = jnp.sum(into_f[:, None, :] * jnp.exp(-rates[:, None, :] * (steps + 1.0)[None, :, None]), axis=0)
    filtered = local_f + carry_f + skip_gain[None, :] * mixed_in
    gated_output = (query_in * filtered).astype(bf16)
    grad_query = grad_gate * filtered

    local_b = spectral_conv(grad_mix, fwd_b[:, ::-1], inv_b[::-1, :], h_a, h_a2, h_b)
    carry_b = jnp.sum(
        into_b[:, None, :] * jnp.exp(-rates[:, None, :] * (tok_rows - steps)[None, :, None]), axis=0
    )
    grad_conv = local_b + carry_b + skip_gain[None, :] * grad_mix

    grad_proj = jnp.stack([grad_query, grad_conv * value_in, grad_conv * key_in], axis=1).astype(bf16)
    grad_proj = grad_proj.reshape(tok_rows, 3 * chan_count)
    contract = (((1,), (1,)), ((), ()))
    dx_terms = lax.dot_general(grad_proj, whole_w, contract, preferred_element_type=f32)
    grad_tokens = lax.psum_scatter(dx_terms.astype(bf16), "chan", scatter_dimension=1, tiled=True)
    return (gated_output, grad_tokens)


def solution(mesh):
    placed = (
        P("seq", None),
        P("seq", None, "chan"),
        P(None, "chan"),
        P(None, "chan"),
        P("chan"),
        P("seq", "chan"),
    )
    return jax.shard_map(
        local,
        mesh=mesh,
        in_specs=placed,
        out_specs=(P("seq", "chan"), P("seq", "chan")),
        check_vma=False,
    )
```

```python
import math

import jax
import jax.numpy as jnp
from jax import lax
from jax.sharding import PartitionSpec as P

f32 = jnp.float32
bf16 = jnp.bfloat16


def dft_tables(block_len, flip=False):
    n_len = 2 * block_len
    k = jnp.arange(block_len, dtype=jnp.int32)[:, None]
    n = jnp.arange(block_len, dtype=jnp.int32)[None, :]
    if flip:
        n = block_len - 1 - n
    phase = (k * n) % n_len
    angle = (2.0 * math.pi / n_len) * phase.astype(f32)
    cos_rows = jnp.cos(angle)
    sin_rows = jnp.sin(angle)
    nyquist = jnp.where(n % 2 == 0, 1.0, -1.0).astype(f32)
    sin_rows = jnp.where(k == 0, nyquist, sin_rows)
    fwd = jnp.concatenate([cos_rows, sin_rows], axis=0)
    weight = jnp.where(k == 0, 1.0, 2.0).astype(f32) / n_len
    inv = (jnp.concatenate([cos_rows * weight, sin_rows * weight], axis=0)).T
    return fwd, inv


def spectral_conv(signal, fwd, inv, h_a, h_a2, h_b):
    block_len = signal.shape[0]
    spec = jnp.dot(fwd, signal.astype(bf16), preferred_element_type=f32)
    xc = spec[:block_len]
    xs = spec[block_len:]
    pr = xc * h_a - xs * h_b
    pi = xc * h_b + xs * h_a2
    prod = jnp.concatenate([pr, pi], axis=0).astype(bf16)
    return jnp.dot(inv, prod, preferred_element_type=f32)


def local(tokens, proj_weight, residues, decay_rates, skip_gain, grad_out):
    tok_rows = tokens.shape[0]
    chan_count = skip_gain.shape[0]
    seq_count = lax.axis_size(SEQ)
    me = lax.axis_index(SEQ)
    flat_w = proj_weight.reshape(proj_weight.shape[0], 3 * chan_count)
    half = 3 * chan_count // 2
    pair_w = lax.all_gather(flat_w, "core", axis=0, tiled=True)
    mine_w = lax.dynamic_slice_in_dim(pair_w, lax.axis_index("core") * half, half, axis=1)
    plane_w = lax.all_gather(mine_w, "xy", axis=0, tiled=True)
    whole_w = lax.all_gather(plane_w, "core", axis=1, tiled=True)
    projected = jnp.dot(tokens, whole_w, preferred_element_type=f32)
    proj_vals = (
        lax.optimization_barrier(projected.astype(bf16))
        .astype(f32)
        .reshape(tok_rows, 3, chan_count)
    )
    query_in = proj_vals[:, 0]
    key_in = proj_vals[:, 1]
    value_in = proj_vals[:, 2]
    mixed_in = key_in * value_in
    grad_gate = grad_out.astype(f32)
    grad_mix = grad_gate * query_in

    rates = decay_rates
    mode_gain = residues * jnp.sqrt(-jnp.expm1(-2.0 * rates))
    steps = jnp.arange(tok_rows, dtype=f32)

    fwd_w = jnp.exp(-rates[:, None, :] * (tok_rows - 1 - steps)[None, :, None])
    bwd_w = jnp.exp(-rates[:, None, :] * steps[None, :, None])
    end_fwd = jnp.sum(fwd_w * mixed_in[None], axis=1)
    end_bwd = jnp.sum(bwd_w * grad_mix[None], axis=1)
    states = jnp.stack([end_fwd, end_bwd])
    every = lax.all_gather(states, SEQ)

    others = jnp.arange(seq_count, dtype=jnp.int32)
    gap_f = me - 1 - others
    gap_b = others - me - 1
    span = rates[None] * float(tok_rows)
    w_f = jnp.where(
        (gap_f >= 0)[:, None, None],
        jnp.exp(-span * jnp.maximum(gap_f, 0).astype(f32)[:, None, None]),
        0.0,
    )
    w_b = jnp.where(
        (gap_b >= 0)[:, None, None],
        jnp.exp(-span * jnp.maximum(gap_b, 0).astype(f32)[:, None, None]),
        0.0,
    )
    into_f = jnp.sum(w_f * every[:, 0], axis=0) * mode_gain
    into_b = jnp.sum(w_b * every[:, 1], axis=0) * mode_gain

    taps = jnp.sum(mode_gain[:, None, :] * bwd_w, axis=0)
    fwd, inv = dft_tables(tok_rows)
    fwd_b = fwd.astype(bf16)
    inv_b = inv.astype(bf16)
    fwd_r, inv_r = dft_tables(tok_rows, flip=True)
    spec = jnp.dot(fwd, taps, precision=lax.Precision.HIGHEST)
    row0 = (jnp.arange(tok_rows) == 0)[:, None]
    h_a = spec[:tok_rows]
    h_a2 = jnp.where(row0, spec[tok_rows:tok_rows + 1], h_a)
    h_b = jnp.where(row0, 0.0, spec[tok_rows:])

    local_f = spectral_conv(mixed_in, fwd_b, inv_b, h_a, h_a2, h_b)
    carry_f = jnp.sum(into_f[:, None, :] * jnp.exp(-rates[:, None, :] * (steps + 1.0)[None, :, None]), axis=0)
    filtered = local_f + carry_f + skip_gain[None, :] * mixed_in
    gated_output = (query_in * filtered).astype(bf16)
    grad_query = grad_gate * filtered

    local_b = spectral_conv(grad_mix, fwd_r.astype(bf16), inv_r.astype(bf16), h_a, h_a2, h_b)
    carry_b = jnp.sum(
        into_b[:, None, :] * jnp.exp(-rates[:, None, :] * (tok_rows - steps)[None, :, None]), axis=0
    )
    grad_conv = local_b + carry_b + skip_gain[None, :] * grad_mix

    grad_proj = jnp.stack([grad_query, grad_conv * value_in, grad_conv * key_in], axis=1).astype(bf16)
    grad_proj = grad_proj.reshape(tok_rows, 3 * chan_count)
    contract = (((1,), (1,)), ((), ()))
    dx_terms = lax.dot_general(grad_proj, whole_w, contract, preferred_element_type=f32)
    grad_tokens = lax.psum_scatter(dx_terms.astype(bf16), "chan", scatter_dimension=1, tiled=True)
    return (gated_output, grad_tokens)


SEQ = ("xy", "core")


def solution(mesh):
    cores = 2
    split = jax.sharding.Mesh(
        mesh.devices.reshape(mesh.shape["seq"] // cores, cores, mesh.shape["chan"]),
        ("xy", "core", "chan"),
    )
    placed = (
        P(SEQ, None),
        P(SEQ, None, "chan"),
        P(None, "chan"),
        P(None, "chan"),
        P("chan"),
        P(SEQ, "chan"),
    )
    return jax.shard_map(
        local,
        mesh=split,
        in_specs=placed,
        out_specs=(P(SEQ, "chan"), P(SEQ, "chan")),
        check_vma=False,
    )
```

```python
import math

import jax
import jax.numpy as jnp
from jax import lax
from jax.sharding import PartitionSpec as P

f32 = jnp.float32
bf16 = jnp.bfloat16


def dft_tables(block_len, flip=False):
    n_len = 2 * block_len
    k = jnp.arange(block_len, dtype=jnp.int32)[:, None]
    n = jnp.arange(block_len, dtype=jnp.int32)[None, :]
    if flip:
        n = block_len - 1 - n
    phase = (k * n) % n_len
    angle = (2.0 * math.pi / n_len) * phase.astype(f32)
    cos_rows = jnp.cos(angle)
    sin_rows = jnp.sin(angle)
    nyquist = jnp.where(n % 2 == 0, 1.0, -1.0).astype(f32)
    sin_rows = jnp.where(k == 0, nyquist, sin_rows)
    fwd = jnp.concatenate([cos_rows, sin_rows], axis=0)
    weight = jnp.where(k == 0, 1.0, 2.0).astype(f32) / n_len
    inv = (jnp.concatenate([cos_rows * weight, sin_rows * weight], axis=0)).T
    return fwd, inv


def spectral_conv(signal, fwd, inv, h_a, h_a2, h_b):
    block_len = signal.shape[0]
    spec = jnp.dot(fwd, signal.astype(bf16), preferred_element_type=f32)
    xc = spec[:block_len]
    xs = spec[block_len:]
    pr = xc * h_a - xs * h_b
    pi = xc * h_b + xs * h_a2
    prod = jnp.concatenate([pr, pi], axis=0).astype(bf16)
    return jnp.dot(inv, prod, preferred_element_type=f32)


def mode_sum(amp, rates, lag):
    total = amp[0] * jnp.exp(-rates[0] * lag)
    for r in range(1, rates.shape[0]):
        total = total + amp[r] * jnp.exp(-rates[r] * lag)
    return total


def local(tokens, proj_weight, residues, decay_rates, skip_gain, grad_out):
    tok_rows = tokens.shape[0]
    chan_count = skip_gain.shape[0]
    seq_count = lax.axis_size(SEQ)
    me = lax.axis_index(SEQ)
    flat_w = proj_weight.reshape(proj_weight.shape[0], 3 * chan_count)
    whole_w = lax.all_gather(flat_w, SEQ, axis=0, tiled=True)
    projected = jnp.dot(tokens, whole_w, preferred_element_type=f32)
    proj_vals = (
        lax.optimization_barrier(projected.astype(bf16))
        .astype(f32)
        .reshape(tok_rows, 3, chan_count)
    )
    query_in = proj_vals[:, 0]
    key_in = proj_vals[:, 1]
    value_in = proj_vals[:, 2]
    mixed_in = key_in * value_in
    grad_gate = grad_out.astype(f32)
    grad_mix = grad_gate * query_in

    rates = decay_rates
    modes = rates.shape[0]
    mode_gain = residues * jnp.sqrt(-jnp.expm1(-2.0 * rates))
    steps = jnp.arange(tok_rows, dtype=f32)

    col = steps[:, None]
    end_fwd = jnp.stack(
        [jnp.sum(jnp.exp(-rates[r] * (tok_rows - 1 - col)) * mixed_in, axis=0) for r in range(modes)]
    )
    end_bwd = jnp.stack(
        [jnp.sum(jnp.exp(-rates[r] * col) * grad_mix, axis=0) for r in range(modes)]
    )
    states = jnp.stack([end_fwd, end_bwd])
    every = lax.all_gather(states, SEQ)

    others = jnp.arange(seq_count, dtype=jnp.int32)
    gap_f = me - 1 - others
    gap_b = others - me - 1
    span = rates[None] * float(tok_rows)
    w_f = jnp.where(
        (gap_f >= 0)[:, None, None],
        jnp.exp(-span * jnp.maximum(gap_f, 0).astype(f32)[:, None, None]),
        0.0,
    )
    w_b = jnp.where(
        (gap_b >= 0)[:, None, None],
        jnp.exp(-span * jnp.maximum(gap_b, 0).astype(f32)[:, None, None]),
        0.0,
    )
    into_f = jnp.sum(w_f * every[:, 0], axis=0) * mode_gain
    into_b = jnp.sum(w_b * every[:, 1], axis=0) * mode_gain

    taps = mode_sum(mode_gain, rates, col)
    fwd, inv = dft_tables(tok_rows)
    fwd_b = fwd.astype(bf16)
    inv_b = inv.astype(bf16)
    fwd_r, inv_r = dft_tables(tok_rows, flip=True)
    spec = jnp.dot(fwd, taps, precision=lax.Precision.HIGHEST)
    row0 = (jnp.arange(tok_rows) == 0)[:, None]
    h_a = spec[:tok_rows]
    h_a2 = jnp.where(row0, spec[tok_rows:tok_rows + 1], h_a)
    h_b = jnp.where(row0, 0.0, spec[tok_rows:])

    local_f = spectral_conv(mixed_in, fwd_b, inv_b, h_a, h_a2, h_b)
    carry_f = mode_sum(into_f, rates, col + 1.0)
    filtered = local_f + carry_f + skip_gain[None, :] * mixed_in
    gated_output = (query_in * filtered).astype(bf16)
    grad_query = grad_gate * filtered

    local_b = spectral_conv(grad_mix, fwd_r.astype(bf16), inv_r.astype(bf16), h_a, h_a2, h_b)
    carry_b = mode_sum(into_b, rates, tok_rows - col)
    grad_conv = local_b + carry_b + skip_gain[None, :] * grad_mix

    grad_proj = jnp.stack([grad_query, grad_conv * value_in, grad_conv * key_in], axis=1).astype(bf16)
    grad_proj = grad_proj.reshape(tok_rows, 3 * chan_count)
    contract = (((1,), (1,)), ((), ()))
    dx_terms = lax.dot_general(grad_proj, whole_w, contract, preferred_element_type=f32)
    grad_tokens = lax.psum_scatter(dx_terms.astype(bf16), "chan", scatter_dimension=1, tiled=True)
    return (gated_output, grad_tokens)


SEQ = ("xy", "core")


def solution(mesh):
    cores = 2
    split = jax.sharding.Mesh(
        mesh.devices.reshape(mesh.shape["seq"] // cores, cores, mesh.shape["chan"]),
        ("xy", "core", "chan"),
    )
    placed = (
        P(SEQ, None),
        P(SEQ, None, "chan"),
        P(None, "chan"),
        P(None, "chan"),
        P("chan"),
        P(SEQ, "chan"),
    )
    return jax.shard_map(
        local,
        mesh=split,
        in_specs=placed,
        out_specs=(P(SEQ, "chan"), P(SEQ, "chan")),
        check_vma=False,
    )
```

```python
import functools
import math

import jax
import jax.numpy as jnp
from jax import lax
from jax.experimental import pallas as pl
from jax.experimental.pallas import tpu as pltpu
from jax.sharding import PartitionSpec as P

MESH = pl.DeviceIdType.MESH

f32 = jnp.float32
bf16 = jnp.bfloat16


def dft_tables(block_len, flip=False):
    n_len = 2 * block_len
    k = jnp.arange(block_len, dtype=jnp.int32)[:, None]
    n = jnp.arange(block_len, dtype=jnp.int32)[None, :]
    if flip:
        n = block_len - 1 - n
    phase = (k * n) % n_len
    angle = (2.0 * math.pi / n_len) * phase.astype(f32)
    cos_rows = jnp.cos(angle)
    sin_rows = jnp.sin(angle)
    nyquist = jnp.where(n % 2 == 0, 1.0, -1.0).astype(f32)
    sin_rows = jnp.where(k == 0, nyquist, sin_rows)
    fwd = jnp.concatenate([cos_rows, sin_rows], axis=0)
    weight = jnp.where(k == 0, 1.0, 2.0).astype(f32) / n_len
    inv = (jnp.concatenate([cos_rows * weight, sin_rows * weight], axis=0)).T
    return fwd, inv


def spectral_conv(signal, fwd, inv, h_a, h_a2, h_b):
    block_len = signal.shape[0]
    spec = jnp.dot(fwd, signal.astype(bf16), preferred_element_type=f32)
    xc = spec[:block_len]
    xs = spec[block_len:]
    pr = xc * h_a - xs * h_b
    pi = xc * h_b + xs * h_a2
    prod = jnp.concatenate([pr, pi], axis=0).astype(bf16)
    return jnp.dot(inv, prod, preferred_element_type=f32)


def ring_kernel(n, gp_ref, w_hbm, out_ref, wbuf, acc, snd, rcv, wsem, send_sem, recv_sem):
    me = lax.axis_index("chan")
    right = lax.rem(me + 1, n)
    left = lax.rem(me + n - 1, n)
    half = out_ref.shape[1] // 2
    block = 2 * half
    tile = min(256, half)

    barrier = pltpu.get_barrier_semaphore()
    for neighbour in (left, right):
        pl.semaphore_signal(barrier, inc=1, device_id={"chan": neighbour}, device_id_type=MESH)
    pl.semaphore_wait(barrier, 2)

    def load(d, dest):
        first = pl.multiple_of(dest * block + d * half, 8)
        cp = pltpu.make_async_copy(w_hbm.at[pl.ds(first, half)], wbuf.at[d], wsem.at[d])
        cp.start()
        return cp

    def product(d):
        def body(j, carry):
            rows = pl.ds(pl.multiple_of(j * tile, tile), tile)
            acc[d, :, rows] = lax.dot_general(
                gp_ref[...], wbuf[d, rows, :], (((1,), (1,)), ((), ())),
                preferred_element_type=jnp.float32,
            )
            return carry

        lax.fori_loop(0, half // tile, body, 0)

    targets = (right, left)
    copies = [None, None]
    for step in range(n - 1):
        dests = (lax.rem(me + 2 * n - 1 - step, n), lax.rem(me + 1 + step, n))
        loads = [load(d, dests[d]) for d in (0, 1)]
        for d in (0, 1):
            loads[d].wait()
            product(d)
            if copies[d] is not None:
                copies[d].wait_recv()
                copies[d].wait_send()
                snd[d] = (acc[d] + rcv[d, step - 1].astype(jnp.float32)).astype(snd.dtype)
            else:
                snd[d] = acc[d].astype(snd.dtype)
            copies[d] = pltpu.make_async_remote_copy(
                src_ref=snd.at[d],
                dst_ref=rcv.at[d, step],
                send_sem=send_sem.at[d],
                recv_sem=recv_sem.at[d, step],
                device_id={"chan": targets[d]},
                device_id_type=MESH,
            )
            copies[d].start()
    loads = [load(d, me) for d in (0, 1)]
    for d in (0, 1):
        loads[d].wait()
        product(d)
        copies[d].wait_recv()
        copies[d].wait_send()
        out_ref[:, pl.ds(d * half, half)] = (
            acc[d] + rcv[d, n - 2].astype(jnp.float32)
        ).astype(out_ref.dtype)


def ring_reduce(grad_proj, whole_w, n):
    rows, width = grad_proj.shape
    block = whole_w.shape[0] // n
    half = block // 2
    return pl.pallas_call(
        functools.partial(ring_kernel, n),
        out_shape=jax.ShapeDtypeStruct((rows, block), jnp.bfloat16),
        in_specs=[pl.BlockSpec(memory_space=pltpu.VMEM), pl.BlockSpec(memory_space=pl.ANY)],
        out_specs=pl.BlockSpec(memory_space=pltpu.VMEM),
        scratch_shapes=[
            pltpu.VMEM((2, half, width), jnp.bfloat16),
            pltpu.VMEM((2, rows, half), jnp.float32),
            pltpu.VMEM((2, rows, half), jnp.bfloat16),
            pltpu.VMEM((2, n - 1, rows, half), jnp.bfloat16),
            pltpu.SemaphoreType.DMA((2,)),
            pltpu.SemaphoreType.DMA((2,)),
            pltpu.SemaphoreType.DMA((2, n - 1)),
        ],
        compiler_params=pltpu.CompilerParams(
            collective_id=0, has_side_effects=True, vmem_limit_bytes=60 * 1024 * 1024
        ),
        cost_estimate=pl.CostEstimate(
            flops=2 * rows * width * whole_w.shape[0],
            bytes_accessed=2 * (whole_w.size + grad_proj.size + rows * block),
            transcendentals=0,
        ),
    )(grad_proj, whole_w)


def mode_sum(amp, rates, lag):
    total = amp[0] * jnp.exp(-rates[0] * lag)
    for r in range(1, rates.shape[0]):
        total = total + amp[r] * jnp.exp(-rates[r] * lag)
    return total


def local(tokens, proj_weight, residues, decay_rates, skip_gain, grad_out):
    tok_rows = tokens.shape[0]
    chan_count = skip_gain.shape[0]
    seq_count = lax.axis_size(SEQ)
    me = lax.axis_index(SEQ)
    flat_w = proj_weight.reshape(proj_weight.shape[0], 3 * chan_count)
    whole_w = lax.all_gather(flat_w, SEQ, axis=0, tiled=True)
    projected = jnp.dot(tokens, whole_w, preferred_element_type=f32)
    proj_vals = (
        lax.optimization_barrier(projected.astype(bf16))
        .astype(f32)
        .reshape(tok_rows, 3, chan_count)
    )
    query_in = proj_vals[:, 0]
    key_in = proj_vals[:, 1]
    value_in = proj_vals[:, 2]
    mixed_in = key_in * value_in
    grad_gate = grad_out.astype(f32)
    grad_mix = grad_gate * query_in

    rates = decay_rates
    modes = rates.shape[0]
    mode_gain = residues * jnp.sqrt(-jnp.expm1(-2.0 * rates))
    steps = jnp.arange(tok_rows, dtype=f32)

    col = steps[:, None]
    end_fwd = jnp.stack(
        [jnp.sum(jnp.exp(-rates[r] * (tok_rows - 1 - col)) * mixed_in, axis=0) for r in range(modes)]
    )
    end_bwd = jnp.stack(
        [jnp.sum(jnp.exp(-rates[r] * col) * grad_mix, axis=0) for r in range(modes)]
    )
    states = jnp.stack([end_fwd, end_bwd])
    every = lax.all_gather(states, SEQ)

    others = jnp.arange(seq_count, dtype=jnp.int32)
    gap_f = me - 1 - others
    gap_b = others - me - 1
    span = rates[None] * float(tok_rows)
    w_f = jnp.where(
        (gap_f >= 0)[:, None, None],
        jnp.exp(-span * jnp.maximum(gap_f, 0).astype(f32)[:, None, None]),
        0.0,
    )
    w_b = jnp.where(
        (gap_b >= 0)[:, None, None],
        jnp.exp(-span * jnp.maximum(gap_b, 0).astype(f32)[:, None, None]),
        0.0,
    )
    into_f = jnp.sum(w_f * every[:, 0], axis=0) * mode_gain
    into_b = jnp.sum(w_b * every[:, 1], axis=0) * mode_gain

    taps = mode_sum(mode_gain, rates, col)
    fwd, inv = dft_tables(tok_rows)
    fwd_b = fwd.astype(bf16)
    inv_b = inv.astype(bf16)
    fwd_r, inv_r = dft_tables(tok_rows, flip=True)
    spec = jnp.dot(fwd, taps, precision=lax.Precision.HIGHEST)
    row0 = (jnp.arange(tok_rows) == 0)[:, None]
    h_a = spec[:tok_rows]
    h_a2 = jnp.where(row0, spec[tok_rows:tok_rows + 1], h_a)
    h_b = jnp.where(row0, 0.0, spec[tok_rows:])

    local_f = spectral_conv(mixed_in, fwd_b, inv_b, h_a, h_a2, h_b)
    carry_f = mode_sum(into_f, rates, col + 1.0)
    filtered = local_f + carry_f + skip_gain[None, :] * mixed_in
    gated_output = (query_in * filtered).astype(bf16)
    grad_query = grad_gate * filtered

    local_b = spectral_conv(grad_mix, fwd_r.astype(bf16), inv_r.astype(bf16), h_a, h_a2, h_b)
    carry_b = mode_sum(into_b, rates, tok_rows - col)
    grad_conv = local_b + carry_b + skip_gain[None, :] * grad_mix

    grad_proj = jnp.stack([grad_query, grad_conv * value_in, grad_conv * key_in], axis=1).astype(bf16)
    grad_proj = grad_proj.reshape(tok_rows, 3 * chan_count)
    grad_tokens = ring_reduce(grad_proj, whole_w, lax.axis_size("chan"))
    return (gated_output, grad_tokens)


SEQ = ("xy", "core")


def solution(mesh):
    cores = 2
    split = jax.sharding.Mesh(
        mesh.devices.reshape(mesh.shape["seq"] // cores, cores, mesh.shape["chan"]),
        ("xy", "core", "chan"),
    )
    placed = (
        P(SEQ, None),
        P(SEQ, None, "chan"),
        P(None, "chan"),
        P(None, "chan"),
        P("chan"),
        P(SEQ, "chan"),
    )
    return jax.shard_map(
        local,
        mesh=split,
        in_specs=placed,
        out_specs=(P(SEQ, "chan"), P(SEQ, "chan")),
        check_vma=False,
    )
```

```python
import functools
import math

import jax
import jax.numpy as jnp
from jax import lax
from jax.experimental import pallas as pl
from jax.experimental.pallas import tpu as pltpu
from jax.sharding import PartitionSpec as P

MESH = pl.DeviceIdType.MESH

f32 = jnp.float32
bf16 = jnp.bfloat16


def dft_tables(block_len, flip=False):
    n_len = 2 * block_len
    k = jnp.arange(block_len, dtype=jnp.int32)[:, None]
    n = jnp.arange(block_len, dtype=jnp.int32)[None, :]
    if flip:
        n = block_len - 1 - n
    phase = (k * n) % n_len
    angle = (2.0 * math.pi / n_len) * phase.astype(f32)
    cos_rows = jnp.cos(angle)
    sin_rows = jnp.sin(angle)
    nyquist = jnp.where(n % 2 == 0, 1.0, -1.0).astype(f32)
    sin_rows = jnp.where(k == 0, nyquist, sin_rows)
    fwd = jnp.concatenate([cos_rows, sin_rows], axis=0)
    weight = jnp.where(k == 0, 1.0, 2.0).astype(f32) / n_len
    inv = (jnp.concatenate([cos_rows * weight, sin_rows * weight], axis=0)).T
    return fwd, inv


def spectral_conv(signal, fwd, inv, h_a, h_a2, h_b):
    block_len = signal.shape[0]
    spec = jnp.dot(fwd, signal.astype(bf16), preferred_element_type=f32)
    xc = spec[:block_len]
    xs = spec[block_len:]
    pr = xc * h_a - xs * h_b
    pi = xc * h_b + xs * h_a2
    prod = jnp.concatenate([pr, pi], axis=0).astype(bf16)
    return jnp.dot(inv, prod, preferred_element_type=f32)


def gather_kernel(shard_ref, out_hbm, send_sem, recv_sem, local_sem):
    rows = shard_ref.shape[0]
    side = 4
    x = lax.axis_index("x")
    y = lax.axis_index("y")
    core = lax.axis_index("core")
    other = 1 - core
    a0 = x * other + y * core
    b0 = y * other + x * core

    def coords(a, b):
        a = lax.rem(a + 2 * side, side)
        b = lax.rem(b + 2 * side, side)
        return a * other + b * core, b * other + a * core

    def slot(a, b, c):
        xx, yy = coords(a, b)
        return out_hbm.at[pl.ds(pl.multiple_of(((xx * side + yy) * 2 + c) * rows, rows), rows)]

    def device(a, b, c):
        xx, yy = coords(a, b)
        return {"x": xx, "y": yy, "core": c}

    peers = [device(a0 + 1, b0, core), device(a0 - 1, b0, core), device(a0, b0 + 1, core),
             device(a0, b0 - 1, core), device(a0, b0, other)]
    barrier = pltpu.get_barrier_semaphore()
    for peer in peers:
        pl.semaphore_signal(barrier, inc=1, device_id=peer, device_id_type=MESH)
    pl.semaphore_wait(barrier, len(peers))

    sent = []

    def push(src, dst, target, index):
        cp = pltpu.make_async_remote_copy(
            src_ref=src, dst_ref=dst, send_sem=send_sem.at[index], recv_sem=recv_sem.at[index],
            device_id=target, device_id_type=MESH,
        )
        cp.start()
        sent.append(cp)
        return cp

    mine = slot(a0, b0, core)
    own = pltpu.make_async_copy(shard_ref, mine, local_sem.at[0])
    own.start()
    partner = device(a0, b0, other)
    up = push(shard_ref, mine, device(a0 + 1, b0, core), 0)
    down = push(shard_ref, mine, device(a0 - 1, b0, core), 1)
    own.wait()
    push(mine, mine, partner, 15)
    up.wait_recv()
    fwd = push(slot(a0 - 1, b0, core), slot(a0 - 1, b0, core), device(a0 + 1, b0, core), 2)
    push(slot(a0 - 1, b0, core), slot(a0 - 1, b0, core), partner, 16)
    down.wait_recv()
    push(slot(a0 + 1, b0, core), slot(a0 + 1, b0, core), partner, 17)
    fwd.wait_recv()
    push(slot(a0 + 2, b0, core), slot(a0 + 2, b0, core), partner, 18)
    outs = []
    for j in range(side):
        src = slot(a0 + j, b0, core)
        outs.append(push(src, src, device(a0, b0 + 1, core), 3 + j))
    for j in range(side):
        src = slot(a0 + j, b0, core)
        outs.append(push(src, src, device(a0, b0 - 1, core), 7 + j))
    later = []
    for j in range(side):
        outs[j].wait_recv()
        src = slot(a0 + j, b0 - 1, core)
        if j < 2:
            later.append(push(src, src, device(a0, b0 + 1, core), 11 + j))
        push(src, src, partner, 19 + j)
    for j in range(side):
        outs[side + j].wait_recv()
        src = slot(a0 + j, b0 + 1, core)
        if j >= 2:
            later.append(push(src, src, device(a0, b0 - 1, core), 11 + j))
        push(src, src, partner, 23 + j)
    for j in range(side):
        later[j].wait_recv()
        src = slot(a0 + j, b0 + 2, core)
        push(src, src, partner, 27 + j)
    for cp in sent:
        cp.wait_send()
    for index in range(15, 31):
        pltpu.make_async_remote_copy(
            src_ref=mine, dst_ref=mine, send_sem=send_sem.at[index], recv_sem=recv_sem.at[index],
            device_id=partner, device_id_type=MESH,
        ).wait_recv()


def gather_rows(shard):
    rows, width = shard.shape
    total = rows * lax.axis_size(SEQ)
    return pl.pallas_call(
        gather_kernel,
        out_shape=jax.ShapeDtypeStruct((total, width), shard.dtype),
        in_specs=[pl.BlockSpec(memory_space=pltpu.VMEM)],
        out_specs=pl.BlockSpec(memory_space=pl.ANY),
        scratch_shapes=[
            pltpu.SemaphoreType.DMA((31,)),
            pltpu.SemaphoreType.DMA((31,)),
            pltpu.SemaphoreType.DMA((1,)),
        ],
        compiler_params=pltpu.CompilerParams(collective_id=1, has_side_effects=True),
        cost_estimate=pl.CostEstimate(flops=0, bytes_accessed=2 * total * width * 2, transcendentals=0),
    )(shard)


def ring_kernel(n, gp_ref, w_hbm, out_ref, wbuf, acc, snd, rcv, wsem, send_sem, recv_sem):
    me = lax.axis_index("chan")
    right = lax.rem(me + 1, n)
    left = lax.rem(me + n - 1, n)
    half = out_ref.shape[1] // 2
    block = 2 * half
    tile = min(256, half)

    barrier = pltpu.get_barrier_semaphore()
    for neighbour in (left, right):
        pl.semaphore_signal(barrier, inc=1, device_id={"chan": neighbour}, device_id_type=MESH)
    pl.semaphore_wait(barrier, 2)

    def load(d, dest):
        first = pl.multiple_of(dest * block + d * half, 8)
        cp = pltpu.make_async_copy(w_hbm.at[pl.ds(first, half)], wbuf.at[d], wsem.at[d])
        cp.start()
        return cp

    def product(d):
        def body(j, carry):
            rows = pl.ds(pl.multiple_of(j * tile, tile), tile)
            acc[d, :, rows] = lax.dot_general(
                gp_ref[...], wbuf[d, rows, :], (((1,), (1,)), ((), ())),
                preferred_element_type=jnp.float32,
            )
            return carry

        lax.fori_loop(0, half // tile, body, 0)

    targets = (right, left)
    copies = [None, None]
    for step in range(n - 1):
        dests = (lax.rem(me + 2 * n - 1 - step, n), lax.rem(me + 1 + step, n))
        loads = [load(d, dests[d]) for d in (0, 1)]
        for d in (0, 1):
            loads[d].wait()
            product(d)
            if copies[d] is not None:
                copies[d].wait_recv()
                copies[d].wait_send()
                snd[d] = (acc[d] + rcv[d, step - 1].astype(jnp.float32)).astype(snd.dtype)
            else:
                snd[d] = acc[d].astype(snd.dtype)
            copies[d] = pltpu.make_async_remote_copy(
                src_ref=snd.at[d],
                dst_ref=rcv.at[d, step],
                send_sem=send_sem.at[d],
                recv_sem=recv_sem.at[d, step],
                device_id={"chan": targets[d]},
                device_id_type=MESH,
            )
            copies[d].start()
    loads = [load(d, me) for d in (0, 1)]
    for d in (0, 1):
        loads[d].wait()
        product(d)
        copies[d].wait_recv()
        copies[d].wait_send()
        out_ref[:, pl.ds(d * half, half)] = (
            acc[d] + rcv[d, n - 2].astype(jnp.float32)
        ).astype(out_ref.dtype)


def ring_reduce(grad_proj, whole_w, n):
    rows, width = grad_proj.shape
    block = whole_w.shape[0] // n
    half = block // 2
    return pl.pallas_call(
        functools.partial(ring_kernel, n),
        out_shape=jax.ShapeDtypeStruct((rows, block), jnp.bfloat16),
        in_specs=[pl.BlockSpec(memory_space=pltpu.VMEM), pl.BlockSpec(memory_space=pl.ANY)],
        out_specs=pl.BlockSpec(memory_space=pltpu.VMEM),
        scratch_shapes=[
            pltpu.VMEM((2, half, width), jnp.bfloat16),
            pltpu.VMEM((2, rows, half), jnp.float32),
            pltpu.VMEM((2, rows, half), jnp.bfloat16),
            pltpu.VMEM((2, n - 1, rows, half), jnp.bfloat16),
            pltpu.SemaphoreType.DMA((2,)),
            pltpu.SemaphoreType.DMA((2,)),
            pltpu.SemaphoreType.DMA((2, n - 1)),
        ],
        compiler_params=pltpu.CompilerParams(
            collective_id=0, has_side_effects=True, vmem_limit_bytes=60 * 1024 * 1024
        ),
        cost_estimate=pl.CostEstimate(
            flops=2 * rows * width * whole_w.shape[0],
            bytes_accessed=2 * (whole_w.size + grad_proj.size + rows * block),
            transcendentals=0,
        ),
    )(grad_proj, whole_w)


def mode_sum(amp, rates, lag):
    total = amp[0] * jnp.exp(-rates[0] * lag)
    for r in range(1, rates.shape[0]):
        total = total + amp[r] * jnp.exp(-rates[r] * lag)
    return total


def local(tokens, proj_weight, residues, decay_rates, skip_gain, grad_out):
    tok_rows = tokens.shape[0]
    chan_count = skip_gain.shape[0]
    seq_count = lax.axis_size(SEQ)
    me = lax.axis_index(SEQ)
    flat_w = proj_weight.reshape(proj_weight.shape[0], 3 * chan_count)
    whole_w = gather_rows(flat_w)
    projected = jnp.dot(tokens, whole_w, preferred_element_type=f32)
    proj_vals = (
        lax.optimization_barrier(projected.astype(bf16))
        .astype(f32)
        .reshape(tok_rows, 3, chan_count)
    )
    query_in = proj_vals[:, 0]
    key_in = proj_vals[:, 1]
    value_in = proj_vals[:, 2]
    mixed_in = key_in * value_in
    grad_gate = grad_out.astype(f32)
    grad_mix = grad_gate * query_in

    rates = decay_rates
    modes = rates.shape[0]
    mode_gain = residues * jnp.sqrt(-jnp.expm1(-2.0 * rates))
    steps = jnp.arange(tok_rows, dtype=f32)

    col = steps[:, None]
    end_fwd = jnp.stack(
        [jnp.sum(jnp.exp(-rates[r] * (tok_rows - 1 - col)) * mixed_in, axis=0) for r in range(modes)]
    )
    end_bwd = jnp.stack(
        [jnp.sum(jnp.exp(-rates[r] * col) * grad_mix, axis=0) for r in range(modes)]
    )
    states = jnp.stack([end_fwd, end_bwd])
    every = lax.all_gather(states, SEQ)

    others = jnp.arange(seq_count, dtype=jnp.int32)
    gap_f = me - 1 - others
    gap_b = others - me - 1
    span = rates[None] * float(tok_rows)
    w_f = jnp.where(
        (gap_f >= 0)[:, None, None],
        jnp.exp(-span * jnp.maximum(gap_f, 0).astype(f32)[:, None, None]),
        0.0,
    )
    w_b = jnp.where(
        (gap_b >= 0)[:, None, None],
        jnp.exp(-span * jnp.maximum(gap_b, 0).astype(f32)[:, None, None]),
        0.0,
    )
    into_f = jnp.sum(w_f * every[:, 0], axis=0) * mode_gain
    into_b = jnp.sum(w_b * every[:, 1], axis=0) * mode_gain

    taps = mode_sum(mode_gain, rates, col)
    fwd, inv = dft_tables(tok_rows)
    fwd_b = fwd.astype(bf16)
    inv_b = inv.astype(bf16)
    fwd_r, inv_r = dft_tables(tok_rows, flip=True)
    spec = jnp.dot(fwd, taps, precision=lax.Precision.HIGHEST)
    row0 = (jnp.arange(tok_rows) == 0)[:, None]
    h_a = spec[:tok_rows]
    h_a2 = jnp.where(row0, spec[tok_rows:tok_rows + 1], h_a)
    h_b = jnp.where(row0, 0.0, spec[tok_rows:])

    local_f = spectral_conv(mixed_in, fwd_b, inv_b, h_a, h_a2, h_b)
    carry_f = mode_sum(into_f, rates, col + 1.0)
    filtered = local_f + carry_f + skip_gain[None, :] * mixed_in
    gated_output = (query_in * filtered).astype(bf16)
    grad_query = grad_gate * filtered

    local_b = spectral_conv(grad_mix, fwd_r.astype(bf16), inv_r.astype(bf16), h_a, h_a2, h_b)
    carry_b = mode_sum(into_b, rates, tok_rows - col)
    grad_conv = local_b + carry_b + skip_gain[None, :] * grad_mix

    grad_proj = jnp.stack([grad_query, grad_conv * value_in, grad_conv * key_in], axis=1).astype(bf16)
    grad_proj = grad_proj.reshape(tok_rows, 3 * chan_count)
    grad_tokens = ring_reduce(grad_proj, whole_w, lax.axis_size("chan"))
    return (gated_output, grad_tokens)


SEQ = ("x", "y", "core")


def solution(mesh):
    side, cores = 4, 2
    split = jax.sharding.Mesh(
        mesh.devices.reshape(side, mesh.shape["seq"] // (side * cores), cores, mesh.shape["chan"]),
        ("x", "y", "core", "chan"),
    )
    placed = (
        P(SEQ, None),
        P(SEQ, None, "chan"),
        P(None, "chan"),
        P(None, "chan"),
        P("chan"),
        P(SEQ, "chan"),
    )
    return jax.shard_map(
        local,
        mesh=split,
        in_specs=placed,
        out_specs=(P(SEQ, "chan"), P(SEQ, "chan")),
        check_vma=False,
    )
```

```python
import functools
import math

import jax
import jax.numpy as jnp
from jax import lax
from jax.experimental import pallas as pl
from jax.experimental.pallas import tpu as pltpu
from jax.sharding import PartitionSpec as P

MESH = pl.DeviceIdType.MESH

f32 = jnp.float32
bf16 = jnp.bfloat16


def dft_tables(block_len, flip=False):
    n_len = 2 * block_len
    k = jnp.arange(block_len, dtype=jnp.int32)[:, None]
    n = jnp.arange(block_len, dtype=jnp.int32)[None, :]
    if flip:
        n = block_len - 1 - n
    phase = (k * n) % n_len
    angle = (2.0 * math.pi / n_len) * phase.astype(f32)
    cos_rows = jnp.cos(angle)
    sin_rows = jnp.sin(angle)
    nyquist = jnp.where(n % 2 == 0, 1.0, -1.0).astype(f32)
    sin_rows = jnp.where(k == 0, nyquist, sin_rows)
    fwd = jnp.concatenate([cos_rows, sin_rows], axis=0)
    weight = jnp.where(k == 0, 1.0, 2.0).astype(f32) / n_len
    inv = (jnp.concatenate([cos_rows * weight, sin_rows * weight], axis=0)).T
    return fwd, inv


def spectral_conv(signal, fwd, inv, h_a, h_a2, h_b):
    block_len = signal.shape[0]
    spec = jnp.dot(fwd, signal.astype(bf16), preferred_element_type=f32)
    xc = spec[:block_len]
    xs = spec[block_len:]
    pr = xc * h_a - xs * h_b
    pi = xc * h_b + xs * h_a2
    prod = jnp.concatenate([pr, pi], axis=0).astype(bf16)
    return jnp.dot(inv, prod, preferred_element_type=f32)


def gather_kernel(shard_ref, out_hbm, send_sem, recv_sem, local_sem):
    rows = shard_ref.shape[0]
    side = 4
    x = lax.axis_index("x")
    y = lax.axis_index("y")
    core = lax.axis_index("core")
    other = 1 - core
    a0 = x * other + y * core
    b0 = y * other + x * core

    def coords(a, b):
        a = lax.rem(a + 2 * side, side)
        b = lax.rem(b + 2 * side, side)
        return a * other + b * core, b * other + a * core

    def slot(a, b, c):
        xx, yy = coords(a, b)
        return out_hbm.at[pl.ds(pl.multiple_of(((xx * side + yy) * 2 + c) * rows, rows), rows)]

    def device(a, b, c):
        xx, yy = coords(a, b)
        return {"x": xx, "y": yy, "core": c}

    peers = [device(a0 + 1, b0, core), device(a0 - 1, b0, core), device(a0, b0 + 1, core),
             device(a0, b0 - 1, core), device(a0, b0, other)]
    barrier = pltpu.get_barrier_semaphore()
    for peer in peers:
        pl.semaphore_signal(barrier, inc=1, device_id=peer, device_id_type=MESH)
    pl.semaphore_wait(barrier, len(peers))

    sent = []

    def push(src, dst, target, index):
        cp = pltpu.make_async_remote_copy(
            src_ref=src, dst_ref=dst, send_sem=send_sem.at[index], recv_sem=recv_sem.at[index],
            device_id=target, device_id_type=MESH,
        )
        cp.start()
        sent.append(cp)
        return cp

    mine = slot(a0, b0, core)
    own = pltpu.make_async_copy(shard_ref, mine, local_sem.at[0])
    own.start()
    partner = device(a0, b0, other)
    up = push(shard_ref, mine, device(a0 + 1, b0, core), 0)
    down = push(shard_ref, mine, device(a0 - 1, b0, core), 1)
    own.wait()
    push(mine, mine, partner, 15)
    up.wait_recv()
    fwd = push(slot(a0 - 1, b0, core), slot(a0 - 1, b0, core), device(a0 + 1, b0, core), 2)
    push(slot(a0 - 1, b0, core), slot(a0 - 1, b0, core), partner, 16)
    down.wait_recv()
    push(slot(a0 + 1, b0, core), slot(a0 + 1, b0, core), partner, 17)
    fwd.wait_recv()
    push(slot(a0 + 2, b0, core), slot(a0 + 2, b0, core), partner, 18)
    outs = []
    for j in range(side):
        src = slot(a0 + j, b0, core)
        outs.append(push(src, src, device(a0, b0 + 1, core), 3 + j))
    for j in range(side):
        src = slot(a0 + j, b0, core)
        outs.append(push(src, src, device(a0, b0 - 1, core), 7 + j))
    later = []
    for j in range(side):
        outs[j].wait_recv()
        src = slot(a0 + j, b0 - 1, core)
        if j < 2:
            later.append(push(src, src, device(a0, b0 + 1, core), 11 + j))
        push(src, src, partner, 19 + j)
    for j in range(side):
        outs[side + j].wait_recv()
        src = slot(a0 + j, b0 + 1, core)
        if j >= 2:
            later.append(push(src, src, device(a0, b0 - 1, core), 11 + j))
        push(src, src, partner, 23 + j)
    for j in range(side):
        later[j].wait_recv()
        src = slot(a0 + j, b0 + 2, core)
        push(src, src, partner, 27 + j)
    for cp in sent:
        cp.wait_send()
    for index in range(15, 31):
        pltpu.make_async_remote_copy(
            src_ref=mine, dst_ref=mine, send_sem=send_sem.at[index], recv_sem=recv_sem.at[index],
            device_id=partner, device_id_type=MESH,
        ).wait_recv()


def gather_rows(shard, collective):
    rows, width = shard.shape
    total = rows * lax.axis_size(SEQ)
    return pl.pallas_call(
        gather_kernel,
        out_shape=jax.ShapeDtypeStruct((total, width), shard.dtype),
        in_specs=[pl.BlockSpec(memory_space=pltpu.VMEM)],
        out_specs=pl.BlockSpec(memory_space=pl.ANY),
        scratch_shapes=[
            pltpu.SemaphoreType.DMA((31,)),
            pltpu.SemaphoreType.DMA((31,)),
            pltpu.SemaphoreType.DMA((1,)),
        ],
        compiler_params=pltpu.CompilerParams(collective_id=collective, has_side_effects=True),
        cost_estimate=pl.CostEstimate(flops=0, bytes_accessed=2 * total * width * 2, transcendentals=0),
    )(shard)


def ring_kernel(n, gp_ref, w_hbm, out_ref, wbuf, acc, snd, rcv, wsem, send_sem, recv_sem):
    me = lax.axis_index("chan")
    right = lax.rem(me + 1, n)
    left = lax.rem(me + n - 1, n)
    half = out_ref.shape[1] // 2
    block = 2 * half
    tile = min(256, half)

    barrier = pltpu.get_barrier_semaphore()
    for neighbour in (left, right):
        pl.semaphore_signal(barrier, inc=1, device_id={"chan": neighbour}, device_id_type=MESH)
    pl.semaphore_wait(barrier, 2)

    def load(d, dest):
        first = pl.multiple_of(dest * block + d * half, 8)
        cp = pltpu.make_async_copy(w_hbm.at[pl.ds(first, half)], wbuf.at[d], wsem.at[d])
        cp.start()
        return cp

    def product(d):
        def body(j, carry):
            rows = pl.ds(pl.multiple_of(j * tile, tile), tile)
            acc[d, :, rows] = lax.dot_general(
                gp_ref[...], wbuf[d, rows, :], (((1,), (1,)), ((), ())),
                preferred_element_type=jnp.float32,
            )
            return carry

        lax.fori_loop(0, half // tile, body, 0)

    targets = (right, left)
    copies = [None, None]
    for step in range(n - 1):
        dests = (lax.rem(me + 2 * n - 1 - step, n), lax.rem(me + 1 + step, n))
        loads = [load(d, dests[d]) for d in (0, 1)]
        for d in (0, 1):
            loads[d].wait()
            product(d)
            if copies[d] is not None:
                copies[d].wait_recv()
                copies[d].wait_send()
                snd[d] = (acc[d] + rcv[d, step - 1].astype(jnp.float32)).astype(snd.dtype)
            else:
                snd[d] = acc[d].astype(snd.dtype)
            copies[d] = pltpu.make_async_remote_copy(
                src_ref=snd.at[d],
                dst_ref=rcv.at[d, step],
                send_sem=send_sem.at[d],
                recv_sem=recv_sem.at[d, step],
                device_id={"chan": targets[d]},
                device_id_type=MESH,
            )
            copies[d].start()
    loads = [load(d, me) for d in (0, 1)]
    for d in (0, 1):
        loads[d].wait()
        product(d)
        copies[d].wait_recv()
        copies[d].wait_send()
        out_ref[:, pl.ds(d * half, half)] = (
            acc[d] + rcv[d, n - 2].astype(jnp.float32)
        ).astype(out_ref.dtype)


def ring_reduce(grad_proj, whole_w, n):
    rows, width = grad_proj.shape
    block = whole_w.shape[0] // n
    half = block // 2
    return pl.pallas_call(
        functools.partial(ring_kernel, n),
        out_shape=jax.ShapeDtypeStruct((rows, block), jnp.bfloat16),
        in_specs=[pl.BlockSpec(memory_space=pltpu.VMEM), pl.BlockSpec(memory_space=pl.ANY)],
        out_specs=pl.BlockSpec(memory_space=pltpu.VMEM),
        scratch_shapes=[
            pltpu.VMEM((2, half, width), jnp.bfloat16),
            pltpu.VMEM((2, rows, half), jnp.float32),
            pltpu.VMEM((2, rows, half), jnp.bfloat16),
            pltpu.VMEM((2, n - 1, rows, half), jnp.bfloat16),
            pltpu.SemaphoreType.DMA((2,)),
            pltpu.SemaphoreType.DMA((2,)),
            pltpu.SemaphoreType.DMA((2, n - 1)),
        ],
        compiler_params=pltpu.CompilerParams(
            collective_id=0, has_side_effects=True, vmem_limit_bytes=60 * 1024 * 1024
        ),
        cost_estimate=pl.CostEstimate(
            flops=2 * rows * width * whole_w.shape[0],
            bytes_accessed=2 * (whole_w.size + grad_proj.size + rows * block),
            transcendentals=0,
        ),
    )(grad_proj, whole_w)


def mode_sum(amp, rates, lag):
    total = amp[0] * jnp.exp(-rates[0] * lag)
    for r in range(1, rates.shape[0]):
        total = total + amp[r] * jnp.exp(-rates[r] * lag)
    return total


def local(tokens, proj_weight, residues, decay_rates, skip_gain, grad_out):
    tok_rows = tokens.shape[0]
    chan_count = skip_gain.shape[0]
    seq_count = lax.axis_size(SEQ)
    me = lax.axis_index(SEQ)
    flat_w = proj_weight.reshape(proj_weight.shape[0], 3 * chan_count)
    whole_w = gather_rows(flat_w, 1)
    projected = jnp.dot(tokens, whole_w, preferred_element_type=f32)
    proj_vals = (
        lax.optimization_barrier(projected.astype(bf16))
        .astype(f32)
        .reshape(tok_rows, 3, chan_count)
    )
    query_in = proj_vals[:, 0]
    key_in = proj_vals[:, 1]
    value_in = proj_vals[:, 2]
    mixed_in = key_in * value_in
    grad_gate = grad_out.astype(f32)
    grad_mix = grad_gate * query_in

    rates = decay_rates
    modes = rates.shape[0]
    mode_gain = residues * jnp.sqrt(-jnp.expm1(-2.0 * rates))
    steps = jnp.arange(tok_rows, dtype=f32)

    col = steps[:, None]
    end_fwd = jnp.stack(
        [jnp.sum(jnp.exp(-rates[r] * (tok_rows - 1 - col)) * mixed_in, axis=0) for r in range(modes)]
    )
    end_bwd = jnp.stack(
        [jnp.sum(jnp.exp(-rates[r] * col) * grad_mix, axis=0) for r in range(modes)]
    )
    states = jnp.stack([end_fwd, end_bwd])
    every = gather_rows(states.reshape(2 * modes, chan_count), 2).reshape(seq_count, 2, modes, chan_count)

    others = jnp.arange(seq_count, dtype=jnp.int32)
    gap_f = me - 1 - others
    gap_b = others - me - 1
    span = rates[None] * float(tok_rows)
    w_f = jnp.where(
        (gap_f >= 0)[:, None, None],
        jnp.exp(-span * jnp.maximum(gap_f, 0).astype(f32)[:, None, None]),
        0.0,
    )
    w_b = jnp.where(
        (gap_b >= 0)[:, None, None],
        jnp.exp(-span * jnp.maximum(gap_b, 0).astype(f32)[:, None, None]),
        0.0,
    )
    into_f = jnp.sum(w_f * every[:, 0], axis=0) * mode_gain
    into_b = jnp.sum(w_b * every[:, 1], axis=0) * mode_gain

    taps = mode_sum(mode_gain, rates, col)
    fwd, inv = dft_tables(tok_rows)
    fwd_b = fwd.astype(bf16)
    inv_b = inv.astype(bf16)
    fwd_r, inv_r = dft_tables(tok_rows, flip=True)
    spec = jnp.dot(fwd, taps, precision=lax.Precision.HIGHEST)
    row0 = (jnp.arange(tok_rows) == 0)[:, None]
    h_a = spec[:tok_rows]
    h_a2 = jnp.where(row0, spec[tok_rows:tok_rows + 1], h_a)
    h_b = jnp.where(row0, 0.0, spec[tok_rows:])

    local_f = spectral_conv(mixed_in, fwd_b, inv_b, h_a, h_a2, h_b)
    carry_f = mode_sum(into_f, rates, col + 1.0)
    filtered = local_f + carry_f + skip_gain[None, :] * mixed_in
    gated_output = (query_in * filtered).astype(bf16)
    grad_query = grad_gate * filtered

    local_b = spectral_conv(grad_mix, fwd_r.astype(bf16), inv_r.astype(bf16), h_a, h_a2, h_b)
    carry_b = mode_sum(into_b, rates, tok_rows - col)
    grad_conv = local_b + carry_b + skip_gain[None, :] * grad_mix

    grad_proj = jnp.stack([grad_query, grad_conv * value_in, grad_conv * key_in], axis=1).astype(bf16)
    grad_proj = grad_proj.reshape(tok_rows, 3 * chan_count)
    grad_tokens = ring_reduce(grad_proj, whole_w, lax.axis_size("chan"))
    return (gated_output, grad_tokens)


SEQ = ("x", "y", "core")


def solution(mesh):
    side, cores = 4, 2
    split = jax.sharding.Mesh(
        mesh.devices.reshape(side, mesh.shape["seq"] // (side * cores), cores, mesh.shape["chan"]),
        ("x", "y", "core", "chan"),
    )
    placed = (
        P(SEQ, None),
        P(SEQ, None, "chan"),
        P(None, "chan"),
        P(None, "chan"),
        P("chan"),
        P(SEQ, "chan"),
    )
    return jax.shard_map(
        local,
        mesh=split,
        in_specs=placed,
        out_specs=(P(SEQ, "chan"), P(SEQ, "chan")),
        check_vma=False,
    )
```

```python
import functools
import math

import jax
import jax.numpy as jnp
from jax import lax
from jax.experimental import pallas as pl
from jax.experimental.pallas import tpu as pltpu
from jax.sharding import PartitionSpec as P

MESH = pl.DeviceIdType.MESH

f32 = jnp.float32
bf16 = jnp.bfloat16


def dft_tables(block_len, flip=False):
    n_len = 2 * block_len
    k = jnp.arange(block_len, dtype=jnp.int32)[:, None]
    n = jnp.arange(block_len, dtype=jnp.int32)[None, :]
    if flip:
        n = block_len - 1 - n
    phase = (k * n) % n_len
    angle = (2.0 * math.pi / n_len) * phase.astype(f32)
    cos_rows = jnp.cos(angle)
    sin_rows = jnp.sin(angle)
    nyquist = jnp.where(n % 2 == 0, 1.0, -1.0).astype(f32)
    sin_rows = jnp.where(k == 0, nyquist, sin_rows)
    fwd = jnp.concatenate([cos_rows, sin_rows], axis=0)
    weight = jnp.where(k == 0, 1.0, 2.0).astype(f32) / n_len
    inv = (jnp.concatenate([cos_rows * weight, sin_rows * weight], axis=0)).T
    return fwd, inv


def spectral_conv(signal, fwd, inv, h_a, h_a2, h_b):
    block_len = signal.shape[0]
    spec = jnp.dot(fwd, signal.astype(bf16), preferred_element_type=f32)
    xc = spec[:block_len]
    xs = spec[block_len:]
    pr = xc * h_a - xs * h_b
    pi = xc * h_b + xs * h_a2
    prod = jnp.concatenate([pr, pi], axis=0).astype(bf16)
    return jnp.dot(inv, prod, preferred_element_type=f32)


def gather_kernel(shard_ref, *refs, project):
    if project:
        tok_ref, out_hbm, prod_ref, vbuf, send_sem, recv_sem, local_sem = refs
    else:
        out_hbm, send_sem, recv_sem, local_sem = refs
    rows = shard_ref.shape[0]
    side = 4
    x = lax.axis_index("x")
    y = lax.axis_index("y")
    core = lax.axis_index("core")
    other = 1 - core
    a0 = x * other + y * core
    b0 = y * other + x * core

    def coords(a, b):
        a = lax.rem(a + 2 * side, side)
        b = lax.rem(b + 2 * side, side)
        return a * other + b * core, b * other + a * core

    def first_row(a, b, c):
        xx, yy = coords(a, b)
        return pl.multiple_of(((xx * side + yy) * 2 + c) * rows, rows)

    def slot(a, b, c):
        return out_hbm.at[pl.ds(first_row(a, b, c), rows)]

    def consume(a, b, c):
        xx, yy = coords(a, b)
        consume_xy(xx, yy, c)

    def consume_xy(xx, yy, c):
        if not project:
            return
        start = pl.multiple_of(((xx * side + yy) * 2 + c) * rows, rows)
        cp = pltpu.make_async_copy(out_hbm.at[pl.ds(start, rows)], vbuf, local_sem.at[1])
        cp.start()
        cp.wait()
        width = vbuf.shape[1]
        tile = 256

        def body(j, carry):
            cols = pl.ds(pl.multiple_of(j * tile, tile), tile)
            prod_ref[:, cols] += jnp.dot(
                tok_ref[:, pl.ds(start, rows)], vbuf[:, cols], preferred_element_type=jnp.float32
            )
            return carry

        lax.fori_loop(0, width // tile, body, 0)

    def device(a, b, c):
        xx, yy = coords(a, b)
        return {"x": xx, "y": yy, "core": c}

    peers = [device(a0 + 1, b0, core), device(a0 - 1, b0, core), device(a0, b0 + 1, core),
             device(a0, b0 - 1, core), device(a0, b0, other)]
    barrier = pltpu.get_barrier_semaphore()
    for peer in peers:
        pl.semaphore_signal(barrier, inc=1, device_id=peer, device_id_type=MESH)
    pl.semaphore_wait(barrier, len(peers))

    sent = []

    def push(src, dst, target, index):
        cp = pltpu.make_async_remote_copy(
            src_ref=src, dst_ref=dst, send_sem=send_sem.at[index], recv_sem=recv_sem.at[index],
            device_id=target, device_id_type=MESH,
        )
        cp.start()
        sent.append(cp)
        return cp

    mine = slot(a0, b0, core)
    own = pltpu.make_async_copy(shard_ref, mine, local_sem.at[0])
    own.start()
    partner = device(a0, b0, other)
    if project:
        prod_ref[...] = jnp.zeros_like(prod_ref)
    up = push(shard_ref, mine, device(a0 + 1, b0, core), 0)
    down = push(shard_ref, mine, device(a0 - 1, b0, core), 1)
    own.wait()
    push(mine, mine, partner, 15)
    consume(a0, b0, core)
    up.wait_recv()
    fwd = push(slot(a0 - 1, b0, core), slot(a0 - 1, b0, core), device(a0 + 1, b0, core), 2)
    push(slot(a0 - 1, b0, core), slot(a0 - 1, b0, core), partner, 16)
    consume(a0 - 1, b0, core)
    down.wait_recv()
    push(slot(a0 + 1, b0, core), slot(a0 + 1, b0, core), partner, 17)
    consume(a0 + 1, b0, core)
    fwd.wait_recv()
    push(slot(a0 + 2, b0, core), slot(a0 + 2, b0, core), partner, 18)
    consume(a0 + 2, b0, core)
    outs = []
    for j in range(side):
        src = slot(a0 + j, b0, core)
        outs.append(push(src, src, device(a0, b0 + 1, core), 3 + j))
    for j in range(side):
        src = slot(a0 + j, b0, core)
        outs.append(push(src, src, device(a0, b0 - 1, core), 7 + j))
    later = []
    for j in range(side):
        outs[j].wait_recv()
        src = slot(a0 + j, b0 - 1, core)
        if j < 2:
            later.append(push(src, src, device(a0, b0 + 1, core), 11 + j))
        push(src, src, partner, 19 + j)
        consume(a0 + j, b0 - 1, core)
    for j in range(side):
        outs[side + j].wait_recv()
        src = slot(a0 + j, b0 + 1, core)
        if j >= 2:
            later.append(push(src, src, device(a0, b0 - 1, core), 11 + j))
        push(src, src, partner, 23 + j)
        consume(a0 + j, b0 + 1, core)
    for j in range(side):
        later[j].wait_recv()
        src = slot(a0 + j, b0 + 2, core)
        push(src, src, partner, 27 + j)
        consume(a0 + j, b0 + 2, core)
    p_a = x * core + y * other
    p_b = y * core + x * other
    offsets = [(0, 0), (-1, 0), (1, 0), (2, 0)] + [(j, -1) for j in range(side)]
    offsets += [(j, 1) for j in range(side)] + [(j, 2) for j in range(side)]
    for index, (da, db) in enumerate(offsets):
        pltpu.make_async_remote_copy(
            src_ref=mine, dst_ref=mine, send_sem=send_sem.at[15 + index],
            recv_sem=recv_sem.at[15 + index], device_id=partner, device_id_type=MESH,
        ).wait_recv()
        pa = lax.rem(p_a + da + 2 * side, side)
        pb = lax.rem(p_b + db + 2 * side, side)
        xx = pa * core + pb * other
        yy = pb * core + pa * other
        if project:
            consume_xy(xx, yy, other)
    for cp in sent:
        cp.wait_send()


def gather_rows(shard, collective, tokens=None):
    rows, width = shard.shape
    total = rows * lax.axis_size(SEQ)
    sems = [
        pltpu.SemaphoreType.DMA((31,)),
        pltpu.SemaphoreType.DMA((31,)),
        pltpu.SemaphoreType.DMA((2,)),
    ]
    gathered = jax.ShapeDtypeStruct((total, width), shard.dtype)
    vmem = pl.BlockSpec(memory_space=pltpu.VMEM)
    if tokens is None:
        return pl.pallas_call(
            functools.partial(gather_kernel, project=False),
            out_shape=gathered,
            in_specs=[vmem],
            out_specs=pl.BlockSpec(memory_space=pl.ANY),
            scratch_shapes=sems,
            compiler_params=pltpu.CompilerParams(collective_id=collective, has_side_effects=True),
            cost_estimate=pl.CostEstimate(flops=0, bytes_accessed=4 * total * width, transcendentals=0),
        )(shard)
    tok_rows = tokens.shape[0]
    return pl.pallas_call(
        functools.partial(gather_kernel, project=True),
        out_shape=(gathered, jax.ShapeDtypeStruct((tok_rows, width), jnp.float32)),
        in_specs=[vmem, vmem],
        out_specs=(pl.BlockSpec(memory_space=pl.ANY), vmem),
        scratch_shapes=[pltpu.VMEM((rows, width), shard.dtype)] + sems,
        compiler_params=pltpu.CompilerParams(
            collective_id=collective, has_side_effects=True, vmem_limit_bytes=60 * 1024 * 1024
        ),
        cost_estimate=pl.CostEstimate(
            flops=2 * tok_rows * total * width,
            bytes_accessed=4 * total * width + tokens.size * 2,
            transcendentals=0,
        ),
    )(shard, tokens)


def ring_kernel(n, gp_ref, w_hbm, out_ref, wbuf, acc, snd, rcv, wsem, send_sem, recv_sem):
    me = lax.axis_index("chan")
    right = lax.rem(me + 1, n)
    left = lax.rem(me + n - 1, n)
    half = out_ref.shape[1] // 2
    block = 2 * half
    tile = min(256, half)

    barrier = pltpu.get_barrier_semaphore()
    for neighbour in (left, right):
        pl.semaphore_signal(barrier, inc=1, device_id={"chan": neighbour}, device_id_type=MESH)
    pl.semaphore_wait(barrier, 2)

    def load(d, dest):
        first = pl.multiple_of(dest * block + d * half, 8)
        cp = pltpu.make_async_copy(w_hbm.at[pl.ds(first, half)], wbuf.at[d], wsem.at[d])
        cp.start()
        return cp

    def product(d):
        def body(j, carry):
            rows = pl.ds(pl.multiple_of(j * tile, tile), tile)
            acc[d, :, rows] = lax.dot_general(
                gp_ref[...], wbuf[d, rows, :], (((1,), (1,)), ((), ())),
                preferred_element_type=jnp.float32,
            )
            return carry

        lax.fori_loop(0, half // tile, body, 0)

    targets = (right, left)
    copies = [None, None]
    for step in range(n - 1):
        dests = (lax.rem(me + 2 * n - 1 - step, n), lax.rem(me + 1 + step, n))
        loads = [load(d, dests[d]) for d in (0, 1)]
        for d in (0, 1):
            loads[d].wait()
            product(d)
            if copies[d] is not None:
                copies[d].wait_recv()
                copies[d].wait_send()
                snd[d] = (acc[d] + rcv[d, step - 1].astype(jnp.float32)).astype(snd.dtype)
            else:
                snd[d] = acc[d].astype(snd.dtype)
            copies[d] = pltpu.make_async_remote_copy(
                src_ref=snd.at[d],
                dst_ref=rcv.at[d, step],
                send_sem=send_sem.at[d],
                recv_sem=recv_sem.at[d, step],
                device_id={"chan": targets[d]},
                device_id_type=MESH,
            )
            copies[d].start()
    loads = [load(d, me) for d in (0, 1)]
    for d in (0, 1):
        loads[d].wait()
        product(d)
        copies[d].wait_recv()
        copies[d].wait_send()
        out_ref[:, pl.ds(d * half, half)] = (
            acc[d] + rcv[d, n - 2].astype(jnp.float32)
        ).astype(out_ref.dtype)


def ring_reduce(grad_proj, whole_w, n):
    rows, width = grad_proj.shape
    block = whole_w.shape[0] // n
    half = block // 2
    return pl.pallas_call(
        functools.partial(ring_kernel, n),
        out_shape=jax.ShapeDtypeStruct((rows, block), jnp.bfloat16),
        in_specs=[pl.BlockSpec(memory_space=pltpu.VMEM), pl.BlockSpec(memory_space=pl.ANY)],
        out_specs=pl.BlockSpec(memory_space=pltpu.VMEM),
        scratch_shapes=[
            pltpu.VMEM((2, half, width), jnp.bfloat16),
            pltpu.VMEM((2, rows, half), jnp.float32),
            pltpu.VMEM((2, rows, half), jnp.bfloat16),
            pltpu.VMEM((2, n - 1, rows, half), jnp.bfloat16),
            pltpu.SemaphoreType.DMA((2,)),
            pltpu.SemaphoreType.DMA((2,)),
            pltpu.SemaphoreType.DMA((2, n - 1)),
        ],
        compiler_params=pltpu.CompilerParams(
            collective_id=0, has_side_effects=True, vmem_limit_bytes=60 * 1024 * 1024
        ),
        cost_estimate=pl.CostEstimate(
            flops=2 * rows * width * whole_w.shape[0],
            bytes_accessed=2 * (whole_w.size + grad_proj.size + rows * block),
            transcendentals=0,
        ),
    )(grad_proj, whole_w)


def mode_sum(amp, rates, lag):
    total = amp[0] * jnp.exp(-rates[0] * lag)
    for r in range(1, rates.shape[0]):
        total = total + amp[r] * jnp.exp(-rates[r] * lag)
    return total


def local(tokens, proj_weight, residues, decay_rates, skip_gain, grad_out):
    tok_rows = tokens.shape[0]
    chan_count = skip_gain.shape[0]
    seq_count = lax.axis_size(SEQ)
    me = lax.axis_index(SEQ)
    flat_w = proj_weight.reshape(proj_weight.shape[0], 3 * chan_count)
    whole_w, projected = gather_rows(flat_w, 1, tokens)
    proj_vals = (
        lax.optimization_barrier(projected.astype(bf16))
        .astype(f32)
        .reshape(tok_rows, 3, chan_count)
    )
    query_in = proj_vals[:, 0]
    key_in = proj_vals[:, 1]
    value_in = proj_vals[:, 2]
    mixed_in = key_in * value_in
    grad_gate = grad_out.astype(f32)
    grad_mix = grad_gate * query_in

    rates = decay_rates
    modes = rates.shape[0]
    mode_gain = residues * jnp.sqrt(-jnp.expm1(-2.0 * rates))
    steps = jnp.arange(tok_rows, dtype=f32)

    col = steps[:, None]
    end_fwd = jnp.stack(
        [jnp.sum(jnp.exp(-rates[r] * (tok_rows - 1 - col)) * mixed_in, axis=0) for r in range(modes)]
    )
    end_bwd = jnp.stack(
        [jnp.sum(jnp.exp(-rates[r] * col) * grad_mix, axis=0) for r in range(modes)]
    )
    states = jnp.stack([end_fwd, end_bwd])
    every = gather_rows(states.reshape(2 * modes, chan_count), 2).reshape(seq_count, 2, modes, chan_count)

    others = jnp.arange(seq_count, dtype=jnp.int32)
    gap_f = me - 1 - others
    gap_b = others - me - 1
    span = rates[None] * float(tok_rows)
    w_f = jnp.where(
        (gap_f >= 0)[:, None, None],
        jnp.exp(-span * jnp.maximum(gap_f, 0).astype(f32)[:, None, None]),
        0.0,
    )
    w_b = jnp.where(
        (gap_b >= 0)[:, None, None],
        jnp.exp(-span * jnp.maximum(gap_b, 0).astype(f32)[:, None, None]),
        0.0,
    )
    into_f = jnp.sum(w_f * every[:, 0], axis=0) * mode_gain
    into_b = jnp.sum(w_b * every[:, 1], axis=0) * mode_gain

    taps = mode_sum(mode_gain, rates, col)
    fwd, inv = dft_tables(tok_rows)
    fwd_b = fwd.astype(bf16)
    inv_b = inv.astype(bf16)
    fwd_r, inv_r = dft_tables(tok_rows, flip=True)
    spec = jnp.dot(fwd, taps, precision=lax.Precision.HIGHEST)
    row0 = (jnp.arange(tok_rows) == 0)[:, None]
    h_a = spec[:tok_rows]
    h_a2 = jnp.where(row0, spec[tok_rows:tok_rows + 1], h_a)
    h_b = jnp.where(row0, 0.0, spec[tok_rows:])

    local_f = spectral_conv(mixed_in, fwd_b, inv_b, h_a, h_a2, h_b)
    carry_f = mode_sum(into_f, rates, col + 1.0)
    filtered = local_f + carry_f + skip_gain[None, :] * mixed_in
    gated_output = (query_in * filtered).astype(bf16)
    grad_query = grad_gate * filtered

    local_b = spectral_conv(grad_mix, fwd_r.astype(bf16), inv_r.astype(bf16), h_a, h_a2, h_b)
    carry_b = mode_sum(into_b, rates, tok_rows - col)
    grad_conv = local_b + carry_b + skip_gain[None, :] * grad_mix

    grad_proj = jnp.stack([grad_query, grad_conv * value_in, grad_conv * key_in], axis=1).astype(bf16)
    grad_proj = grad_proj.reshape(tok_rows, 3 * chan_count)
    grad_tokens = ring_reduce(grad_proj, whole_w, lax.axis_size("chan"))
    return (gated_output, grad_tokens)


SEQ = ("x", "y", "core")


def solution(mesh):
    side, cores = 4, 2
    split = jax.sharding.Mesh(
        mesh.devices.reshape(side, mesh.shape["seq"] // (side * cores), cores, mesh.shape["chan"]),
        ("x", "y", "core", "chan"),
    )
    placed = (
        P(SEQ, None),
        P(SEQ, None, "chan"),
        P(None, "chan"),
        P(None, "chan"),
        P("chan"),
        P(SEQ, "chan"),
    )
    return jax.shard_map(
        local,
        mesh=split,
        in_specs=placed,
        out_specs=(P(SEQ, "chan"), P(SEQ, "chan")),
        check_vma=False,
    )
```

```python
import functools
import math

import jax
import jax.numpy as jnp
from jax import lax
from jax.experimental import pallas as pl
from jax.experimental.pallas import tpu as pltpu
from jax.sharding import PartitionSpec as P

MESH = pl.DeviceIdType.MESH

f32 = jnp.float32
bf16 = jnp.bfloat16


def dft_tables(block_len, flip=False):
    n_len = 2 * block_len
    low = 32
    high = block_len // low
    n = jnp.arange(block_len, dtype=jnp.int32)
    if flip:
        n = block_len - 1 - n

    def trig(mult):
        phase = (mult[:, None] * n[None, :]) % n_len
        angle = (2.0 * math.pi / n_len) * phase.astype(f32)
        return jnp.cos(angle), jnp.sin(angle)

    ca, sa = trig(jnp.arange(high, dtype=jnp.int32) * low)
    cb, sb = trig(jnp.arange(low, dtype=jnp.int32))
    nyquist = jnp.where(n % 2 == 0, 1.0, -1.0).astype(f32)
    first = (jnp.arange(block_len) == 0)[:, None]
    weight = jnp.where(jnp.arange(block_len) == 0, 1.0, 2.0).astype(f32) / n_len

    cos_rows = (ca[:, None, :] * cb[None] - sa[:, None, :] * sb[None]).reshape(block_len, block_len)
    sin_rows = (sa[:, None, :] * cb[None] + ca[:, None, :] * sb[None]).reshape(block_len, block_len)
    sin_rows = jnp.where(first, nyquist[None, :], sin_rows)
    fwd = jnp.concatenate([cos_rows, sin_rows], axis=0)

    cos_t = (ca.T[:, :, None] * cb.T[:, None, :] - sa.T[:, :, None] * sb.T[:, None, :]).reshape(
        block_len, block_len
    )
    sin_t = (sa.T[:, :, None] * cb.T[:, None, :] + ca.T[:, :, None] * sb.T[:, None, :]).reshape(
        block_len, block_len
    )
    sin_t = jnp.where(first.T, nyquist[:, None], sin_t)
    inv = jnp.concatenate([cos_t * weight[None, :], sin_t * weight[None, :]], axis=1)
    return fwd, inv


def spectral_conv(signal, fwd, inv, h_a, h_a2, h_b):
    block_len = signal.shape[0]
    spec = jnp.dot(fwd, signal.astype(bf16), preferred_element_type=f32)
    xc = spec[:block_len]
    xs = spec[block_len:]
    pr = xc * h_a - xs * h_b
    pi = xc * h_b + xs * h_a2
    prod = jnp.concatenate([pr, pi], axis=0).astype(bf16)
    return jnp.dot(inv, prod, preferred_element_type=f32)


def gather_kernel(shard_ref, out_hbm, send_sem, recv_sem, local_sem):
    rows = shard_ref.shape[0]
    side = 4
    x = lax.axis_index("x")
    y = lax.axis_index("y")
    core = lax.axis_index("core")
    other = 1 - core
    a0 = x * other + y * core
    b0 = y * other + x * core

    def coords(a, b):
        a = lax.rem(a + 2 * side, side)
        b = lax.rem(b + 2 * side, side)
        return a * other + b * core, b * other + a * core

    def slot(a, b, c):
        xx, yy = coords(a, b)
        return out_hbm.at[pl.ds(pl.multiple_of(((xx * side + yy) * 2 + c) * rows, rows), rows)]

    def device(a, b, c):
        xx, yy = coords(a, b)
        return {"x": xx, "y": yy, "core": c}

    peers = [device(a0 + 1, b0, core), device(a0 - 1, b0, core), device(a0, b0 + 1, core),
             device(a0, b0 - 1, core), device(a0, b0, other)]
    barrier = pltpu.get_barrier_semaphore()
    for peer in peers:
        pl.semaphore_signal(barrier, inc=1, device_id=peer, device_id_type=MESH)
    pl.semaphore_wait(barrier, len(peers))

    sent = []

    def push(src, dst, target, index):
        cp = pltpu.make_async_remote_copy(
            src_ref=src, dst_ref=dst, send_sem=send_sem.at[index], recv_sem=recv_sem.at[index],
            device_id=target, device_id_type=MESH,
        )
        cp.start()
        sent.append(cp)
        return cp

    mine = slot(a0, b0, core)
    own = pltpu.make_async_copy(shard_ref, mine, local_sem.at[0])
    own.start()
    partner = device(a0, b0, other)
    up = push(shard_ref, mine, device(a0 + 1, b0, core), 0)
    down = push(shard_ref, mine, device(a0 - 1, b0, core), 1)
    own.wait()
    push(mine, mine, partner, 15)
    up.wait_recv()
    fwd = push(slot(a0 - 1, b0, core), slot(a0 - 1, b0, core), device(a0 + 1, b0, core), 2)
    push(slot(a0 - 1, b0, core), slot(a0 - 1, b0, core), partner, 16)
    down.wait_recv()
    push(slot(a0 + 1, b0, core), slot(a0 + 1, b0, core), partner, 17)
    fwd.wait_recv()
    push(slot(a0 + 2, b0, core), slot(a0 + 2, b0, core), partner, 18)
    outs = []
    for j in range(side):
        src = slot(a0 + j, b0, core)
        outs.append(push(src, src, device(a0, b0 + 1, core), 3 + j))
    for j in range(side):
        src = slot(a0 + j, b0, core)
        outs.append(push(src, src, device(a0, b0 - 1, core), 7 + j))
    later = []
    for j in range(side):
        outs[j].wait_recv()
        src = slot(a0 + j, b0 - 1, core)
        if j < 2:
            later.append(push(src, src, device(a0, b0 + 1, core), 11 + j))
        push(src, src, partner, 19 + j)
    for j in range(side):
        outs[side + j].wait_recv()
        src = slot(a0 + j, b0 + 1, core)
        if j >= 2:
            later.append(push(src, src, device(a0, b0 - 1, core), 11 + j))
        push(src, src, partner, 23 + j)
    for j in range(side):
        later[j].wait_recv()
        src = slot(a0 + j, b0 + 2, core)
        push(src, src, partner, 27 + j)
    for cp in sent:
        cp.wait_send()
    for index in range(15, 31):
        pltpu.make_async_remote_copy(
            src_ref=mine, dst_ref=mine, send_sem=send_sem.at[index], recv_sem=recv_sem.at[index],
            device_id=partner, device_id_type=MESH,
        ).wait_recv()


def gather_rows(shard, collective):
    rows, width = shard.shape
    total = rows * lax.axis_size(SEQ)
    return pl.pallas_call(
        gather_kernel,
        out_shape=jax.ShapeDtypeStruct((total, width), shard.dtype),
        in_specs=[pl.BlockSpec(memory_space=pltpu.VMEM)],
        out_specs=pl.BlockSpec(memory_space=pl.ANY),
        scratch_shapes=[
            pltpu.SemaphoreType.DMA((31,)),
            pltpu.SemaphoreType.DMA((31,)),
            pltpu.SemaphoreType.DMA((1,)),
        ],
        compiler_params=pltpu.CompilerParams(collective_id=collective, has_side_effects=True),
        cost_estimate=pl.CostEstimate(flops=0, bytes_accessed=2 * total * width * 2, transcendentals=0),
    )(shard)


def ring_kernel(n, gp_ref, w_hbm, out_ref, wbuf, acc, snd, rcv, wsem, send_sem, recv_sem):
    me = lax.axis_index("chan")
    right = lax.rem(me + 1, n)
    left = lax.rem(me + n - 1, n)
    half = out_ref.shape[1] // 2
    block = 2 * half
    tile = min(256, half)

    barrier = pltpu.get_barrier_semaphore()
    for neighbour in (left, right):
        pl.semaphore_signal(barrier, inc=1, device_id={"chan": neighbour}, device_id_type=MESH)
    pl.semaphore_wait(barrier, 2)

    def load(d, dest):
        first = pl.multiple_of(dest * block + d * half, 8)
        cp = pltpu.make_async_copy(w_hbm.at[pl.ds(first, half)], wbuf.at[d], wsem.at[d])
        cp.start()
        return cp

    def product(d):
        def body(j, carry):
            rows = pl.ds(pl.multiple_of(j * tile, tile), tile)
            acc[d, :, rows] = lax.dot_general(
                gp_ref[...], wbuf[d, rows, :], (((1,), (1,)), ((), ())),
                preferred_element_type=jnp.float32,
            )
            return carry

        lax.fori_loop(0, half // tile, body, 0)

    targets = (right, left)
    copies = [None, None]
    for step in range(n - 1):
        dests = (lax.rem(me + 2 * n - 1 - step, n), lax.rem(me + 1 + step, n))
        loads = [load(d, dests[d]) for d in (0, 1)]
        for d in (0, 1):
            loads[d].wait()
            product(d)
            if copies[d] is not None:
                copies[d].wait_recv()
                copies[d].wait_send()
                snd[d] = (acc[d] + rcv[d, step - 1].astype(jnp.float32)).astype(snd.dtype)
            else:
                snd[d] = acc[d].astype(snd.dtype)
            copies[d] = pltpu.make_async_remote_copy(
                src_ref=snd.at[d],
                dst_ref=rcv.at[d, step],
                send_sem=send_sem.at[d],
                recv_sem=recv_sem.at[d, step],
                device_id={"chan": targets[d]},
                device_id_type=MESH,
            )
            copies[d].start()
    loads = [load(d, me) for d in (0, 1)]
    for d in (0, 1):
        loads[d].wait()
        product(d)
        copies[d].wait_recv()
        copies[d].wait_send()
        out_ref[:, pl.ds(d * half, half)] = (
            acc[d] + rcv[d, n - 2].astype(jnp.float32)
        ).astype(out_ref.dtype)


def ring_reduce(grad_proj, whole_w, n):
    rows, width = grad_proj.shape
    block = whole_w.shape[0] // n
    half = block // 2
    return pl.pallas_call(
        functools.partial(ring_kernel, n),
        out_shape=jax.ShapeDtypeStruct((rows, block), jnp.bfloat16),
        in_specs=[pl.BlockSpec(memory_space=pltpu.VMEM), pl.BlockSpec(memory_space=pl.ANY)],
        out_specs=pl.BlockSpec(memory_space=pltpu.VMEM),
        scratch_shapes=[
            pltpu.VMEM((2, half, width), jnp.bfloat16),
            pltpu.VMEM((2, rows, half), jnp.float32),
            pltpu.VMEM((2, rows, half), jnp.bfloat16),
            pltpu.VMEM((2, n - 1, rows, half), jnp.bfloat16),
            pltpu.SemaphoreType.DMA((2,)),
            pltpu.SemaphoreType.DMA((2,)),
            pltpu.SemaphoreType.DMA((2, n - 1)),
        ],
        compiler_params=pltpu.CompilerParams(
            collective_id=0, has_side_effects=True, vmem_limit_bytes=60 * 1024 * 1024
        ),
        cost_estimate=pl.CostEstimate(
            flops=2 * rows * width * whole_w.shape[0],
            bytes_accessed=2 * (whole_w.size + grad_proj.size + rows * block),
            transcendentals=0,
        ),
    )(grad_proj, whole_w)


def mode_sum(amp, rates, lag):
    total = amp[0] * jnp.exp(-rates[0] * lag)
    for r in range(1, rates.shape[0]):
        total = total + amp[r] * jnp.exp(-rates[r] * lag)
    return total


def local(tokens, proj_weight, residues, decay_rates, skip_gain, grad_out):
    tok_rows = tokens.shape[0]
    chan_count = skip_gain.shape[0]
    seq_count = lax.axis_size(SEQ)
    me = lax.axis_index(SEQ)
    flat_w = proj_weight.reshape(proj_weight.shape[0], 3 * chan_count)
    whole_w = gather_rows(flat_w, 1)
    projected = jnp.dot(tokens, whole_w, preferred_element_type=f32)
    proj_vals = (
        lax.optimization_barrier(projected.astype(bf16))
        .astype(f32)
        .reshape(tok_rows, 3, chan_count)
    )
    query_in = proj_vals[:, 0]
    key_in = proj_vals[:, 1]
    value_in = proj_vals[:, 2]
    mixed_in = key_in * value_in
    grad_gate = grad_out.astype(f32)
    grad_mix = grad_gate * query_in

    rates = decay_rates
    modes = rates.shape[0]
    mode_gain = residues * jnp.sqrt(-jnp.expm1(-2.0 * rates))
    steps = jnp.arange(tok_rows, dtype=f32)

    col = steps[:, None]
    end_fwd = jnp.stack(
        [jnp.sum(jnp.exp(-rates[r] * (tok_rows - 1 - col)) * mixed_in, axis=0) for r in range(modes)]
    )
    end_bwd = jnp.stack(
        [jnp.sum(jnp.exp(-rates[r] * col) * grad_mix, axis=0) for r in range(modes)]
    )
    states = jnp.stack([end_fwd, end_bwd])
    every = gather_rows(states.reshape(2 * modes, chan_count), 2).reshape(seq_count, 2, modes, chan_count)

    others = jnp.arange(seq_count, dtype=jnp.int32)
    gap_f = me - 1 - others
    gap_b = others - me - 1
    span = rates[None] * float(tok_rows)
    w_f = jnp.where(
        (gap_f >= 0)[:, None, None],
        jnp.exp(-span * jnp.maximum(gap_f, 0).astype(f32)[:, None, None]),
        0.0,
    )
    w_b = jnp.where(
        (gap_b >= 0)[:, None, None],
        jnp.exp(-span * jnp.maximum(gap_b, 0).astype(f32)[:, None, None]),
        0.0,
    )
    into_f = jnp.sum(w_f * every[:, 0], axis=0) * mode_gain
    into_b = jnp.sum(w_b * every[:, 1], axis=0) * mode_gain

    taps = mode_sum(mode_gain, rates, col)
    fwd, inv = dft_tables(tok_rows)
    fwd_b = fwd.astype(bf16)
    inv_b = inv.astype(bf16)
    fwd_r, inv_r = dft_tables(tok_rows, flip=True)
    spec = jnp.dot(fwd, taps, precision=lax.Precision.HIGHEST)
    row0 = (jnp.arange(tok_rows) == 0)[:, None]
    h_a = spec[:tok_rows]
    h_a2 = jnp.where(row0, spec[tok_rows:tok_rows + 1], h_a)
    h_b = jnp.where(row0, 0.0, spec[tok_rows:])

    local_f = spectral_conv(mixed_in, fwd_b, inv_b, h_a, h_a2, h_b)
    carry_f = mode_sum(into_f, rates, col + 1.0)
    filtered = local_f + carry_f + skip_gain[None, :] * mixed_in
    gated_output = (query_in * filtered).astype(bf16)
    grad_query = grad_gate * filtered

    local_b = spectral_conv(grad_mix, fwd_r.astype(bf16), inv_r.astype(bf16), h_a, h_a2, h_b)
    carry_b = mode_sum(into_b, rates, tok_rows - col)
    grad_conv = local_b + carry_b + skip_gain[None, :] * grad_mix

    grad_proj = jnp.stack([grad_query, grad_conv * value_in, grad_conv * key_in], axis=1).astype(bf16)
    grad_proj = grad_proj.reshape(tok_rows, 3 * chan_count)
    grad_tokens = ring_reduce(grad_proj, whole_w, lax.axis_size("chan"))
    return (gated_output, grad_tokens)


SEQ = ("x", "y", "core")


def solution(mesh):
    side, cores = 4, 2
    split = jax.sharding.Mesh(
        mesh.devices.reshape(side, mesh.shape["seq"] // (side * cores), cores, mesh.shape["chan"]),
        ("x", "y", "core", "chan"),
    )
    placed = (
        P(SEQ, None),
        P(SEQ, None, "chan"),
        P(None, "chan"),
        P(None, "chan"),
        P("chan"),
        P(SEQ, "chan"),
    )
    return jax.shard_map(
        local,
        mesh=split,
        in_specs=placed,
        out_specs=(P(SEQ, "chan"), P(SEQ, "chan")),
        check_vma=False,
    )
```

```python
import functools
import math

import jax
import jax.numpy as jnp
from jax import lax
from jax.experimental import pallas as pl
from jax.experimental.pallas import tpu as pltpu
from jax.sharding import PartitionSpec as P

MESH = pl.DeviceIdType.MESH

f32 = jnp.float32
bf16 = jnp.bfloat16


def dft_tables(block_len, flip=False):
    n_len = 2 * block_len
    low = 32
    high = block_len // low
    n = jnp.arange(block_len, dtype=jnp.int32)
    if flip:
        n = block_len - 1 - n

    def trig(mult):
        phase = (mult[:, None] * n[None, :]) % n_len
        angle = (2.0 * math.pi / n_len) * phase.astype(f32)
        return jnp.cos(angle), jnp.sin(angle)

    ca, sa = trig(jnp.arange(high, dtype=jnp.int32) * low)
    cb, sb = trig(jnp.arange(low, dtype=jnp.int32))
    nyquist = jnp.where(n % 2 == 0, 1.0, -1.0).astype(f32)
    first = (jnp.arange(block_len) == 0)[:, None]
    weight = jnp.where(jnp.arange(block_len) == 0, 1.0, 2.0).astype(f32) / n_len

    cos_rows = (ca[:, None, :] * cb[None] - sa[:, None, :] * sb[None]).reshape(block_len, block_len)
    sin_rows = (sa[:, None, :] * cb[None] + ca[:, None, :] * sb[None]).reshape(block_len, block_len)
    sin_rows = jnp.where(first, nyquist[None, :], sin_rows)
    fwd = jnp.concatenate([cos_rows, sin_rows], axis=0)

    cos_t = (ca.T[:, :, None] * cb.T[:, None, :] - sa.T[:, :, None] * sb.T[:, None, :]).reshape(
        block_len, block_len
    )
    sin_t = (sa.T[:, :, None] * cb.T[:, None, :] + ca.T[:, :, None] * sb.T[:, None, :]).reshape(
        block_len, block_len
    )
    sin_t = jnp.where(first.T, nyquist[:, None], sin_t)
    inv = jnp.concatenate([cos_t * weight[None, :], sin_t * weight[None, :]], axis=1)
    return fwd, inv


def spectral_conv(signal, fwd, inv, h_a, h_a2, h_b):
    block_len = signal.shape[0]
    spec = jnp.dot(fwd, signal.astype(bf16), preferred_element_type=f32)
    xc = spec[:block_len]
    xs = spec[block_len:]
    pr = xc * h_a - xs * h_b
    pi = xc * h_b + xs * h_a2
    prod = jnp.concatenate([pr, pi], axis=0).astype(bf16)
    return jnp.dot(inv, prod, preferred_element_type=f32)


def gather_kernel(shard_ref, out_hbm, send_sem, recv_sem, local_sem):
    rows = shard_ref.shape[0]
    side = 4
    x = lax.axis_index("x")
    y = lax.axis_index("y")
    core = lax.axis_index("core")
    other = 1 - core
    a0 = x * other + y * core
    b0 = y * other + x * core

    def coords(a, b):
        a = lax.rem(a + 2 * side, side)
        b = lax.rem(b + 2 * side, side)
        return a * other + b * core, b * other + a * core

    def slot(a, b, c):
        xx, yy = coords(a, b)
        return out_hbm.at[pl.ds(pl.multiple_of(((xx * side + yy) * 2 + c) * rows, rows), rows)]

    def device(a, b, c):
        xx, yy = coords(a, b)
        return {"x": xx, "y": yy, "core": c}

    peers = [device(a0 + 1, b0, core), device(a0 - 1, b0, core), device(a0, b0 + 1, core),
             device(a0, b0 - 1, core), device(a0, b0, other)]
    barrier = pltpu.get_barrier_semaphore()
    for peer in peers:
        pl.semaphore_signal(barrier, inc=1, device_id=peer, device_id_type=MESH)
    pl.semaphore_wait(barrier, len(peers))

    sent = []

    def push(src, dst, target, index):
        cp = pltpu.make_async_remote_copy(
            src_ref=src, dst_ref=dst, send_sem=send_sem.at[index], recv_sem=recv_sem.at[index],
            device_id=target, device_id_type=MESH,
        )
        cp.start()
        sent.append(cp)
        return cp

    mine = slot(a0, b0, core)
    own = pltpu.make_async_copy(shard_ref, mine, local_sem.at[0])
    own.start()
    partner = device(a0, b0, other)
    up = push(shard_ref, mine, device(a0 + 1, b0, core), 0)
    down = push(shard_ref, mine, device(a0 - 1, b0, core), 1)
    own.wait()
    push(mine, mine, partner, 15)
    up.wait_recv()
    fwd = push(slot(a0 - 1, b0, core), slot(a0 - 1, b0, core), device(a0 + 1, b0, core), 2)
    push(slot(a0 - 1, b0, core), slot(a0 - 1, b0, core), partner, 16)
    down.wait_recv()
    push(slot(a0 + 1, b0, core), slot(a0 + 1, b0, core), partner, 17)
    fwd.wait_recv()
    push(slot(a0 + 2, b0, core), slot(a0 + 2, b0, core), partner, 18)
    outs = []
    for j in range(side):
        src = slot(a0 + j, b0, core)
        outs.append(push(src, src, device(a0, b0 + 1, core), 3 + j))
    for j in range(side):
        src = slot(a0 + j, b0, core)
        outs.append(push(src, src, device(a0, b0 - 1, core), 7 + j))
    later = []
    for j in range(side):
        outs[j].wait_recv()
        src = slot(a0 + j, b0 - 1, core)
        if j < 2:
            later.append(push(src, src, device(a0, b0 + 1, core), 11 + j))
        push(src, src, partner, 19 + j)
    for j in range(side):
        outs[side + j].wait_recv()
        src = slot(a0 + j, b0 + 1, core)
        if j >= 2:
            later.append(push(src, src, device(a0, b0 - 1, core), 11 + j))
        push(src, src, partner, 23 + j)
    for j in range(side):
        later[j].wait_recv()
        src = slot(a0 + j, b0 + 2, core)
        push(src, src, partner, 27 + j)
    for cp in sent:
        cp.wait_send()
    for index in range(15, 31):
        pltpu.make_async_remote_copy(
            src_ref=mine, dst_ref=mine, send_sem=send_sem.at[index], recv_sem=recv_sem.at[index],
            device_id=partner, device_id_type=MESH,
        ).wait_recv()


def gather_rows(shard, collective):
    rows, width = shard.shape
    total = rows * lax.axis_size(SEQ)
    return pl.pallas_call(
        gather_kernel,
        out_shape=jax.ShapeDtypeStruct((total, width), shard.dtype),
        in_specs=[pl.BlockSpec(memory_space=pltpu.VMEM)],
        out_specs=pl.BlockSpec(memory_space=pl.ANY),
        scratch_shapes=[
            pltpu.SemaphoreType.DMA((31,)),
            pltpu.SemaphoreType.DMA((31,)),
            pltpu.SemaphoreType.DMA((1,)),
        ],
        compiler_params=pltpu.CompilerParams(collective_id=collective, has_side_effects=True),
        cost_estimate=pl.CostEstimate(flops=0, bytes_accessed=2 * total * width * 2, transcendentals=0),
    )(shard)


def state_kernel(st_ref, out_ref, send_sem, recv_sem):
    count = out_ref.shape[0]
    side = 4
    me = (lax.axis_index("x") * side + lax.axis_index("y")) * 2 + lax.axis_index("core")

    def device(j):
        return {"x": j // (2 * side), "y": (j // 2) % side, "core": j % 2}

    barrier = pltpu.get_barrier_semaphore()

    def greet(o, carry):
        pl.semaphore_signal(barrier, inc=1, device_id=device(lax.rem(me + o, count)), device_id_type=MESH)
        return carry

    lax.fori_loop(1, count, greet, 0)
    pl.semaphore_wait(barrier, count - 1)

    def copy(o):
        j = lax.rem(me + o, count)
        return pltpu.make_async_remote_copy(
            src_ref=st_ref.at[(me + o) // count],
            dst_ref=out_ref.at[me],
            send_sem=send_sem.at[o - 1],
            recv_sem=recv_sem.at[o - 1],
            device_id=device(j),
            device_id_type=MESH,
        )

    def start(o, carry):
        copy(o).start()
        return carry

    lax.fori_loop(1, count, start, 0)
    out_ref[me] = jnp.zeros(out_ref.shape[1:], out_ref.dtype)

    def finish(o, carry):
        cp = copy(o)
        cp.wait_send()
        cp.wait_recv()
        return carry

    lax.fori_loop(1, count, finish, 0)


def exchange_states(states):
    count = lax.axis_size(SEQ)
    return pl.pallas_call(
        state_kernel,
        out_shape=jax.ShapeDtypeStruct((count,) + states.shape[1:], states.dtype),
        in_specs=[pl.BlockSpec(memory_space=pltpu.VMEM)],
        out_specs=pl.BlockSpec(memory_space=pltpu.VMEM),
        scratch_shapes=[pltpu.SemaphoreType.DMA((count - 1,)), pltpu.SemaphoreType.DMA((count - 1,))],
        compiler_params=pltpu.CompilerParams(collective_id=2, has_side_effects=True),
        cost_estimate=pl.CostEstimate(flops=0, bytes_accessed=8 * states[0].size * count, transcendentals=0),
    )(states)


def ring_kernel(n, gp_ref, w_hbm, out_ref, wbuf, acc, snd, rcv, wsem, send_sem, recv_sem):
    me = lax.axis_index("chan")
    right = lax.rem(me + 1, n)
    left = lax.rem(me + n - 1, n)
    half = out_ref.shape[1] // 2
    block = 2 * half
    tile = min(256, half)

    barrier = pltpu.get_barrier_semaphore()
    for neighbour in (left, right):
        pl.semaphore_signal(barrier, inc=1, device_id={"chan": neighbour}, device_id_type=MESH)
    pl.semaphore_wait(barrier, 2)

    def load(d, dest):
        first = pl.multiple_of(dest * block + d * half, 8)
        cp = pltpu.make_async_copy(w_hbm.at[pl.ds(first, half)], wbuf.at[d], wsem.at[d])
        cp.start()
        return cp

    def product(d):
        def body(j, carry):
            rows = pl.ds(pl.multiple_of(j * tile, tile), tile)
            acc[d, :, rows] = lax.dot_general(
                gp_ref[...], wbuf[d, rows, :], (((1,), (1,)), ((), ())),
                preferred_element_type=jnp.float32,
            )
            return carry

        lax.fori_loop(0, half // tile, body, 0)

    targets = (right, left)
    copies = [None, None]
    for step in range(n - 1):
        dests = (lax.rem(me + 2 * n - 1 - step, n), lax.rem(me + 1 + step, n))
        loads = [load(d, dests[d]) for d in (0, 1)]
        for d in (0, 1):
            loads[d].wait()
            product(d)
            if copies[d] is not None:
                copies[d].wait_recv()
                copies[d].wait_send()
                snd[d] = (acc[d] + rcv[d, step - 1].astype(jnp.float32)).astype(snd.dtype)
            else:
                snd[d] = acc[d].astype(snd.dtype)
            copies[d] = pltpu.make_async_remote_copy(
                src_ref=snd.at[d],
                dst_ref=rcv.at[d, step],
                send_sem=send_sem.at[d],
                recv_sem=recv_sem.at[d, step],
                device_id={"chan": targets[d]},
                device_id_type=MESH,
            )
            copies[d].start()
    loads = [load(d, me) for d in (0, 1)]
    for d in (0, 1):
        loads[d].wait()
        product(d)
        copies[d].wait_recv()
        copies[d].wait_send()
        out_ref[:, pl.ds(d * half, half)] = (
            acc[d] + rcv[d, n - 2].astype(jnp.float32)
        ).astype(out_ref.dtype)


def ring_reduce(grad_proj, whole_w, n):
    rows, width = grad_proj.shape
    block = whole_w.shape[0] // n
    half = block // 2
    return pl.pallas_call(
        functools.partial(ring_kernel, n),
        out_shape=jax.ShapeDtypeStruct((rows, block), jnp.bfloat16),
        in_specs=[pl.BlockSpec(memory_space=pltpu.VMEM), pl.BlockSpec(memory_space=pl.ANY)],
        out_specs=pl.BlockSpec(memory_space=pltpu.VMEM),
        scratch_shapes=[
            pltpu.VMEM((2, half, width), jnp.bfloat16),
            pltpu.VMEM((2, rows, half), jnp.float32),
            pltpu.VMEM((2, rows, half), jnp.bfloat16),
            pltpu.VMEM((2, n - 1, rows, half), jnp.bfloat16),
            pltpu.SemaphoreType.DMA((2,)),
            pltpu.SemaphoreType.DMA((2,)),
            pltpu.SemaphoreType.DMA((2, n - 1)),
        ],
        compiler_params=pltpu.CompilerParams(
            collective_id=0, has_side_effects=True, vmem_limit_bytes=60 * 1024 * 1024
        ),
        cost_estimate=pl.CostEstimate(
            flops=2 * rows * width * whole_w.shape[0],
            bytes_accessed=2 * (whole_w.size + grad_proj.size + rows * block),
            transcendentals=0,
        ),
    )(grad_proj, whole_w)


def mode_sum(amp, rates, lag):
    total = amp[0] * jnp.exp(-rates[0] * lag)
    for r in range(1, rates.shape[0]):
        total = total + amp[r] * jnp.exp(-rates[r] * lag)
    return total


def local(tokens, proj_weight, residues, decay_rates, skip_gain, grad_out):
    tok_rows = tokens.shape[0]
    chan_count = skip_gain.shape[0]
    seq_count = lax.axis_size(SEQ)
    me = lax.axis_index(SEQ)
    flat_w = proj_weight.reshape(proj_weight.shape[0], 3 * chan_count)
    whole_w = gather_rows(flat_w, 1)
    projected = jnp.dot(tokens, whole_w, preferred_element_type=f32)
    proj_vals = (
        lax.optimization_barrier(projected.astype(bf16))
        .astype(f32)
        .reshape(tok_rows, 3, chan_count)
    )
    query_in = proj_vals[:, 0]
    key_in = proj_vals[:, 1]
    value_in = proj_vals[:, 2]
    mixed_in = key_in * value_in
    grad_gate = grad_out.astype(f32)
    grad_mix = grad_gate * query_in

    rates = decay_rates
    modes = rates.shape[0]
    mode_gain = residues * jnp.sqrt(-jnp.expm1(-2.0 * rates))
    steps = jnp.arange(tok_rows, dtype=f32)

    col = steps[:, None]
    end_fwd = jnp.stack(
        [jnp.sum(jnp.exp(-rates[r] * (tok_rows - 1 - col)) * mixed_in, axis=0) for r in range(modes)]
    )
    end_bwd = jnp.stack(
        [jnp.sum(jnp.exp(-rates[r] * col) * grad_mix, axis=0) for r in range(modes)]
    )
    states = jnp.stack([end_fwd, end_bwd])
    every = exchange_states(states)

    others = jnp.arange(seq_count, dtype=jnp.int32)
    gap_f = me - 1 - others
    gap_b = others - me - 1
    span = rates[None] * float(tok_rows)
    w_f = jnp.where(
        (gap_f >= 0)[:, None, None],
        jnp.exp(-span * jnp.maximum(gap_f, 0).astype(f32)[:, None, None]),
        0.0,
    )
    w_b = jnp.where(
        (gap_b >= 0)[:, None, None],
        jnp.exp(-span * jnp.maximum(gap_b, 0).astype(f32)[:, None, None]),
        0.0,
    )
    into_f = jnp.sum(w_f * every, axis=0) * mode_gain
    into_b = jnp.sum(w_b * every, axis=0) * mode_gain

    taps = mode_sum(mode_gain, rates, col)
    fwd, inv = dft_tables(tok_rows)
    fwd_b = fwd.astype(bf16)
    inv_b = inv.astype(bf16)
    fwd_r, inv_r = dft_tables(tok_rows, flip=True)
    spec = jnp.dot(fwd, taps, precision=lax.Precision.HIGHEST)
    row0 = (jnp.arange(tok_rows) == 0)[:, None]
    h_a = spec[:tok_rows]
    h_a2 = jnp.where(row0, spec[tok_rows:tok_rows + 1], h_a)
    h_b = jnp.where(row0, 0.0, spec[tok_rows:])

    local_f = spectral_conv(mixed_in, fwd_b, inv_b, h_a, h_a2, h_b)
    carry_f = mode_sum(into_f, rates, col + 1.0)
    filtered = local_f + carry_f + skip_gain[None, :] * mixed_in
    gated_output = (query_in * filtered).astype(bf16)
    grad_query = grad_gate * filtered

    local_b = spectral_conv(grad_mix, fwd_r.astype(bf16), inv_r.astype(bf16), h_a, h_a2, h_b)
    carry_b = mode_sum(into_b, rates, tok_rows - col)
    grad_conv = local_b + carry_b + skip_gain[None, :] * grad_mix

    grad_proj = jnp.stack([grad_query, grad_conv * value_in, grad_conv * key_in], axis=1).astype(bf16)
    grad_proj = grad_proj.reshape(tok_rows, 3 * chan_count)
    grad_tokens = ring_reduce(grad_proj, whole_w, lax.axis_size("chan"))
    return (gated_output, grad_tokens)


SEQ = ("x", "y", "core")


def solution(mesh):
    side, cores = 4, 2
    split = jax.sharding.Mesh(
        mesh.devices.reshape(side, mesh.shape["seq"] // (side * cores), cores, mesh.shape["chan"]),
        ("x", "y", "core", "chan"),
    )
    placed = (
        P(SEQ, None),
        P(SEQ, None, "chan"),
        P(None, "chan"),
        P(None, "chan"),
        P("chan"),
        P(SEQ, "chan"),
    )
    return jax.shard_map(
        local,
        mesh=split,
        in_specs=placed,
        out_specs=(P(SEQ, "chan"), P(SEQ, "chan")),
        check_vma=False,
    )
```

```python
import functools
import math

import jax
import jax.numpy as jnp
from jax import lax
from jax.experimental import pallas as pl
from jax.experimental.pallas import tpu as pltpu
from jax.sharding import PartitionSpec as P

MESH = pl.DeviceIdType.MESH

f32 = jnp.float32
bf16 = jnp.bfloat16


def dft_tables(block_len, flip=False):
    n_len = 2 * block_len
    low = 32
    high = block_len // low
    n = jnp.arange(block_len, dtype=jnp.int32)
    if flip:
        n = block_len - 1 - n

    def trig(mult):
        phase = (mult[:, None] * n[None, :]) % n_len
        angle = (2.0 * math.pi / n_len) * phase.astype(f32)
        return jnp.cos(angle), jnp.sin(angle)

    ca, sa = trig(jnp.arange(high, dtype=jnp.int32) * low)
    cb, sb = trig(jnp.arange(low, dtype=jnp.int32))
    nyquist = jnp.where(n % 2 == 0, 1.0, -1.0).astype(f32)
    first = (jnp.arange(block_len) == 0)[:, None]
    weight = jnp.where(jnp.arange(block_len) == 0, 1.0, 2.0).astype(f32) / n_len

    cos_rows = (ca[:, None, :] * cb[None] - sa[:, None, :] * sb[None]).reshape(block_len, block_len)
    sin_rows = (sa[:, None, :] * cb[None] + ca[:, None, :] * sb[None]).reshape(block_len, block_len)
    sin_rows = jnp.where(first, nyquist[None, :], sin_rows)
    fwd = jnp.concatenate([cos_rows, sin_rows], axis=0)

    cos_t = (ca.T[:, :, None] * cb.T[:, None, :] - sa.T[:, :, None] * sb.T[:, None, :]).reshape(
        block_len, block_len
    )
    sin_t = (sa.T[:, :, None] * cb.T[:, None, :] + ca.T[:, :, None] * sb.T[:, None, :]).reshape(
        block_len, block_len
    )
    sin_t = jnp.where(first.T, nyquist[:, None], sin_t)
    inv = jnp.concatenate([cos_t * weight[None, :], sin_t * weight[None, :]], axis=1)
    return fwd, inv


def spectral_conv(signal, fwd, inv, h_a, h_a2, h_b):
    block_len = signal.shape[0]
    spec = jnp.dot(fwd, signal.astype(bf16), preferred_element_type=f32)
    xc = spec[:block_len]
    xs = spec[block_len:]
    pr = xc * h_a - xs * h_b
    pi = xc * h_b + xs * h_a2
    prod = jnp.concatenate([pr, pi], axis=0).astype(bf16)
    return jnp.dot(inv, prod, preferred_element_type=f32)


def gather_kernel(shard_ref, out_hbm, send_sem, recv_sem, local_sem):
    rows = shard_ref.shape[0]
    side = 4
    x = lax.axis_index("x")
    y = lax.axis_index("y")
    core = lax.axis_index("core")
    other = 1 - core
    a0 = x * other + y * core
    b0 = y * other + x * core

    def coords(a, b):
        a = lax.rem(a + 2 * side, side)
        b = lax.rem(b + 2 * side, side)
        return a * other + b * core, b * other + a * core

    def slot(a, b):
        xx, yy = coords(a, b)
        return out_hbm.at[pl.ds(pl.multiple_of(((xx * side + yy) * 2 + core) * rows, rows), rows)]

    def device(a, b, c):
        xx, yy = coords(a, b)
        return {"x": xx, "y": yy, "core": c}

    partner = device(a0, b0, other)
    peers = [device(a0 + 1, b0, core), device(a0 - 1, b0, core), device(a0, b0 + 1, core),
             device(a0, b0 - 1, core), partner]
    barrier = pltpu.get_barrier_semaphore()
    for peer in peers:
        pl.semaphore_signal(barrier, inc=1, device_id=peer, device_id_type=MESH)
    pl.semaphore_wait(barrier, len(peers))

    sent = {}

    def push(src, dst, target, index):
        cp = pltpu.make_async_remote_copy(
            src_ref=src, dst_ref=dst, send_sem=send_sem.at[index], recv_sem=recv_sem.at[index],
            device_id=target, device_id_type=MESH,
        )
        cp.start()
        sent[index] = cp
        return cp

    def along_b(j):
        src = slot(a0 + j, b0)
        push(src, src, device(a0, b0 + 1, core), 3 + j)
        push(src, src, device(a0, b0 - 1, core), 7 + j)

    mine = slot(a0, b0)
    own = pltpu.make_async_copy(shard_ref, mine, local_sem.at[0])
    own.start()
    up = push(shard_ref, mine, device(a0 + 1, b0, core), 0)
    down = push(shard_ref, mine, device(a0 - 1, b0, core), 1)
    own.wait()
    along_b(0)
    push(mine, mine, partner, 15)
    up.wait_recv()
    fwd = push(slot(a0 - 1, b0), slot(a0 - 1, b0), device(a0 + 1, b0, core), 2)
    along_b(3)
    push(slot(a0 - 1, b0), slot(a0 - 1, b0), partner, 16)
    down.wait_recv()
    along_b(1)
    push(slot(a0 + 1, b0), slot(a0 + 1, b0), partner, 17)
    fwd.wait_recv()
    along_b(2)
    push(slot(a0 + 2, b0), slot(a0 + 2, b0), partner, 18)
    later = {}
    for j in (0, 3, 1, 2):
        sent[3 + j].wait_recv()
        src = slot(a0 + j, b0 - 1)
        if j < 2:
            later[j] = push(src, src, device(a0, b0 + 1, core), 11 + j)
        push(src, src, partner, 19 + j)
        sent[7 + j].wait_recv()
        src = slot(a0 + j, b0 + 1)
        if j >= 2:
            later[j] = push(src, src, device(a0, b0 - 1, core), 11 + j)
        push(src, src, partner, 23 + j)
    for j in (0, 3, 1, 2):
        later[j].wait_recv()
        src = slot(a0 + j, b0 + 2)
        push(src, src, partner, 27 + j)
    for index in range(15, 31):
        pltpu.make_async_remote_copy(
            src_ref=mine, dst_ref=mine, send_sem=send_sem.at[index], recv_sem=recv_sem.at[index],
            device_id=partner, device_id_type=MESH,
        ).wait_recv()
    for index in sorted(sent):
        sent[index].wait_send()


def gather_rows(shard, collective):
    rows, width = shard.shape
    total = rows * lax.axis_size(SEQ)
    return pl.pallas_call(
        gather_kernel,
        out_shape=jax.ShapeDtypeStruct((total, width), shard.dtype),
        in_specs=[pl.BlockSpec(memory_space=pltpu.VMEM)],
        out_specs=pl.BlockSpec(memory_space=pl.ANY),
        scratch_shapes=[
            pltpu.SemaphoreType.DMA((31,)),
            pltpu.SemaphoreType.DMA((31,)),
            pltpu.SemaphoreType.DMA((1,)),
        ],
        compiler_params=pltpu.CompilerParams(collective_id=collective, has_side_effects=True),
        cost_estimate=pl.CostEstimate(flops=0, bytes_accessed=4 * total * width, transcendentals=0),
    )(shard)


def state_kernel(st_ref, out_ref, send_sem, recv_sem):
    count = out_ref.shape[0]
    side = 4
    me = (lax.axis_index("x") * side + lax.axis_index("y")) * 2 + lax.axis_index("core")

    def device(j):
        return {"x": j // (2 * side), "y": (j // 2) % side, "core": j % 2}

    barrier = pltpu.get_barrier_semaphore()

    def greet(o, carry):
        pl.semaphore_signal(barrier, inc=1, device_id=device(lax.rem(me + o, count)), device_id_type=MESH)
        return carry

    lax.fori_loop(1, count, greet, 0)
    pl.semaphore_wait(barrier, count - 1)

    def copy(o):
        j = lax.rem(me + o, count)
        return pltpu.make_async_remote_copy(
            src_ref=st_ref.at[(me + o) // count],
            dst_ref=out_ref.at[me],
            send_sem=send_sem.at[o - 1],
            recv_sem=recv_sem.at[o - 1],
            device_id=device(j),
            device_id_type=MESH,
        )

    def start(o, carry):
        copy(o).start()
        return carry

    lax.fori_loop(1, count, start, 0)
    out_ref[me] = jnp.zeros(out_ref.shape[1:], out_ref.dtype)

    def finish(o, carry):
        cp = copy(o)
        cp.wait_send()
        cp.wait_recv()
        return carry

    lax.fori_loop(1, count, finish, 0)


def exchange_states(states):
    count = lax.axis_size(SEQ)
    return pl.pallas_call(
        state_kernel,
        out_shape=jax.ShapeDtypeStruct((count,) + states.shape[1:], states.dtype),
        in_specs=[pl.BlockSpec(memory_space=pltpu.VMEM)],
        out_specs=pl.BlockSpec(memory_space=pltpu.VMEM),
        scratch_shapes=[pltpu.SemaphoreType.DMA((count - 1,)), pltpu.SemaphoreType.DMA((count - 1,))],
        compiler_params=pltpu.CompilerParams(collective_id=2, has_side_effects=True),
        cost_estimate=pl.CostEstimate(flops=0, bytes_accessed=8 * states[0].size * count, transcendentals=0),
    )(states)


def ring_kernel(n, gp_ref, w_hbm, out_ref, wbuf, acc, snd, rcv, wsem, send_sem, recv_sem):
    me = lax.axis_index("chan")
    right = lax.rem(me + 1, n)
    left = lax.rem(me + n - 1, n)
    half = out_ref.shape[1] // 2
    block = 2 * half
    tile = min(256, half)

    barrier = pltpu.get_barrier_semaphore()
    for neighbour in (left, right):
        pl.semaphore_signal(barrier, inc=1, device_id={"chan": neighbour}, device_id_type=MESH)
    pl.semaphore_wait(barrier, 2)

    def load(d, dest):
        first = pl.multiple_of(dest * block + d * half, 8)
        cp = pltpu.make_async_copy(w_hbm.at[pl.ds(first, half)], wbuf.at[d], wsem.at[d])
        cp.start()
        return cp

    def product(d):
        def body(j, carry):
            rows = pl.ds(pl.multiple_of(j * tile, tile), tile)
            acc[d, :, rows] = lax.dot_general(
                gp_ref[...], wbuf[d, rows, :], (((1,), (1,)), ((), ())),
                preferred_element_type=jnp.float32,
            )
            return carry

        lax.fori_loop(0, half // tile, body, 0)

    targets = (right, left)
    copies = [None, None]
    for step in range(n - 1):
        dests = (lax.rem(me + 2 * n - 1 - step, n), lax.rem(me + 1 + step, n))
        loads = [load(d, dests[d]) for d in (0, 1)]
        for d in (0, 1):
            loads[d].wait()
            product(d)
            if copies[d] is not None:
                copies[d].wait_recv()
                copies[d].wait_send()
                snd[d] = (acc[d] + rcv[d, step - 1].astype(jnp.float32)).astype(snd.dtype)
            else:
                snd[d] = acc[d].astype(snd.dtype)
            copies[d] = pltpu.make_async_remote_copy(
                src_ref=snd.at[d],
                dst_ref=rcv.at[d, step],
                send_sem=send_sem.at[d],
                recv_sem=recv_sem.at[d, step],
                device_id={"chan": targets[d]},
                device_id_type=MESH,
            )
            copies[d].start()
    loads = [load(d, me) for d in (0, 1)]
    for d in (0, 1):
        loads[d].wait()
        product(d)
        copies[d].wait_recv()
        copies[d].wait_send()
        out_ref[:, pl.ds(d * half, half)] = (
            acc[d] + rcv[d, n - 2].astype(jnp.float32)
        ).astype(out_ref.dtype)


def ring_reduce(grad_proj, whole_w, n):
    rows, width = grad_proj.shape
    block = whole_w.shape[0] // n
    half = block // 2
    return pl.pallas_call(
        functools.partial(ring_kernel, n),
        out_shape=jax.ShapeDtypeStruct((rows, block), jnp.bfloat16),
        in_specs=[pl.BlockSpec(memory_space=pltpu.VMEM), pl.BlockSpec(memory_space=pl.ANY)],
        out_specs=pl.BlockSpec(memory_space=pltpu.VMEM),
        scratch_shapes=[
            pltpu.VMEM((2, half, width), jnp.bfloat16),
            pltpu.VMEM((2, rows, half), jnp.float32),
            pltpu.VMEM((2, rows, half), jnp.bfloat16),
            pltpu.VMEM((2, n - 1, rows, half), jnp.bfloat16),
            pltpu.SemaphoreType.DMA((2,)),
            pltpu.SemaphoreType.DMA((2,)),
            pltpu.SemaphoreType.DMA((2, n - 1)),
        ],
        compiler_params=pltpu.CompilerParams(
            collective_id=0, has_side_effects=True, vmem_limit_bytes=60 * 1024 * 1024
        ),
        cost_estimate=pl.CostEstimate(
            flops=2 * rows * width * whole_w.shape[0],
            bytes_accessed=2 * (whole_w.size + grad_proj.size + rows * block),
            transcendentals=0,
        ),
    )(grad_proj, whole_w)


def mode_sum(amp, rates, lag):
    total = amp[0] * jnp.exp(-rates[0] * lag)
    for r in range(1, rates.shape[0]):
        total = total + amp[r] * jnp.exp(-rates[r] * lag)
    return total


def local(tokens, proj_weight, residues, decay_rates, skip_gain, grad_out):
    tok_rows = tokens.shape[0]
    chan_count = skip_gain.shape[0]
    seq_count = lax.axis_size(SEQ)
    me = lax.axis_index(SEQ)
    flat_w = proj_weight.reshape(proj_weight.shape[0], 3 * chan_count)
    whole_w = gather_rows(flat_w, 1)
    projected = jnp.dot(tokens, whole_w, preferred_element_type=f32)
    proj_vals = (
        lax.optimization_barrier(projected.astype(bf16))
        .astype(f32)
        .reshape(tok_rows, 3, chan_count)
    )
    query_in = proj_vals[:, 0]
    key_in = proj_vals[:, 1]
    value_in = proj_vals[:, 2]
    mixed_in = key_in * value_in
    grad_gate = grad_out.astype(f32)
    grad_mix = grad_gate * query_in

    rates = decay_rates
    modes = rates.shape[0]
    mode_gain = residues * jnp.sqrt(-jnp.expm1(-2.0 * rates))
    steps = jnp.arange(tok_rows, dtype=f32)

    col = steps[:, None]
    end_fwd = jnp.stack(
        [jnp.sum(jnp.exp(-rates[r] * (tok_rows - 1 - col)) * mixed_in, axis=0) for r in range(modes)]
    )
    end_bwd = jnp.stack(
        [jnp.sum(jnp.exp(-rates[r] * col) * grad_mix, axis=0) for r in range(modes)]
    )
    states = jnp.stack([end_fwd, end_bwd])
    every = exchange_states(states)

    others = jnp.arange(seq_count, dtype=jnp.int32)
    gap_f = me - 1 - others
    gap_b = others - me - 1
    span = rates[None] * float(tok_rows)
    w_f = jnp.where(
        (gap_f >= 0)[:, None, None],
        jnp.exp(-span * jnp.maximum(gap_f, 0).astype(f32)[:, None, None]),
        0.0,
    )
    w_b = jnp.where(
        (gap_b >= 0)[:, None, None],
        jnp.exp(-span * jnp.maximum(gap_b, 0).astype(f32)[:, None, None]),
        0.0,
    )
    into_f = jnp.sum(w_f * every, axis=0) * mode_gain
    into_b = jnp.sum(w_b * every, axis=0) * mode_gain

    taps = mode_sum(mode_gain, rates, col)
    fwd, inv = dft_tables(tok_rows)
    fwd_b = fwd.astype(bf16)
    inv_b = inv.astype(bf16)
    fwd_r, inv_r = dft_tables(tok_rows, flip=True)
    spec = jnp.dot(fwd, taps, precision=lax.Precision.HIGHEST)
    row0 = (jnp.arange(tok_rows) == 0)[:, None]
    h_a = spec[:tok_rows]
    h_a2 = jnp.where(row0, spec[tok_rows:tok_rows + 1], h_a)
    h_b = jnp.where(row0, 0.0, spec[tok_rows:])

    local_f = spectral_conv(mixed_in, fwd_b, inv_b, h_a, h_a2, h_b)
    carry_f = mode_sum(into_f, rates, col + 1.0)
    filtered = local_f + carry_f + skip_gain[None, :] * mixed_in
    gated_output = (query_in * filtered).astype(bf16)
    grad_query = grad_gate * filtered

    local_b = spectral_conv(grad_mix, fwd_r.astype(bf16), inv_r.astype(bf16), h_a, h_a2, h_b)
    carry_b = mode_sum(into_b, rates, tok_rows - col)
    grad_conv = local_b + carry_b + skip_gain[None, :] * grad_mix

    grad_proj = jnp.stack([grad_query, grad_conv * value_in, grad_conv * key_in], axis=1).astype(bf16)
    grad_proj = grad_proj.reshape(tok_rows, 3 * chan_count)
    grad_tokens = ring_reduce(grad_proj, whole_w, lax.axis_size("chan"))
    return (gated_output, grad_tokens)


SEQ = ("x", "y", "core")


def solution(mesh):
    side, cores = 4, 2
    split = jax.sharding.Mesh(
        mesh.devices.reshape(side, mesh.shape["seq"] // (side * cores), cores, mesh.shape["chan"]),
        ("x", "y", "core", "chan"),
    )
    placed = (
        P(SEQ, None),
        P(SEQ, None, "chan"),
        P(None, "chan"),
        P(None, "chan"),
        P("chan"),
        P(SEQ, "chan"),
    )
    return jax.shard_map(
        local,
        mesh=split,
        in_specs=placed,
        out_specs=(P(SEQ, "chan"), P(SEQ, "chan")),
        check_vma=False,
    )
```

```python
import functools
import math

import jax
import jax.numpy as jnp
from jax import lax
from jax.experimental import pallas as pl
from jax.experimental.pallas import tpu as pltpu
from jax.sharding import PartitionSpec as P

MESH = pl.DeviceIdType.MESH

f32 = jnp.float32
bf16 = jnp.bfloat16


def dft_tables(block_len, flip=False):
    n_len = 2 * block_len
    low = 32
    high = block_len // low
    n = jnp.arange(block_len, dtype=jnp.int32)
    if flip:
        n = block_len - 1 - n

    def trig(mult):
        phase = (mult[:, None] * n[None, :]) % n_len
        angle = (2.0 * math.pi / n_len) * phase.astype(f32)
        return jnp.cos(angle), jnp.sin(angle)

    ca, sa = trig(jnp.arange(high, dtype=jnp.int32) * low)
    cb, sb = trig(jnp.arange(low, dtype=jnp.int32))
    nyquist = jnp.where(n % 2 == 0, 1.0, -1.0).astype(f32)
    first = (jnp.arange(block_len) == 0)[:, None]
    weight = jnp.where(jnp.arange(block_len) == 0, 1.0, 2.0).astype(f32) / n_len

    cos_rows = (ca[:, None, :] * cb[None] - sa[:, None, :] * sb[None]).reshape(block_len, block_len)
    sin_rows = (sa[:, None, :] * cb[None] + ca[:, None, :] * sb[None]).reshape(block_len, block_len)
    sin_rows = jnp.where(first, nyquist[None, :], sin_rows)
    fwd = jnp.concatenate([cos_rows, sin_rows], axis=0)

    cos_t = (ca.T[:, :, None] * cb.T[:, None, :] - sa.T[:, :, None] * sb.T[:, None, :]).reshape(
        block_len, block_len
    )
    sin_t = (sa.T[:, :, None] * cb.T[:, None, :] + ca.T[:, :, None] * sb.T[:, None, :]).reshape(
        block_len, block_len
    )
    sin_t = jnp.where(first.T, nyquist[:, None], sin_t)
    inv = jnp.concatenate([cos_t * weight[None, :], sin_t * weight[None, :]], axis=1)
    return fwd, inv


def spectral_conv(signal, fwd, inv, h_a, h_a2, h_b):
    block_len = signal.shape[0]
    spec = jnp.dot(fwd, signal.astype(bf16), preferred_element_type=f32)
    xc = spec[:block_len]
    xs = spec[block_len:]
    pr = xc * h_a - xs * h_b
    pi = xc * h_b + xs * h_a2
    prod = jnp.concatenate([pr, pi], axis=0).astype(bf16)
    return jnp.dot(inv, prod, preferred_element_type=f32)


def gather_kernel(shard_ref, out_hbm, send_sem, recv_sem, local_sem):
    rows = shard_ref.shape[0]
    side = 4
    x = lax.axis_index("x")
    y = lax.axis_index("y")
    core = lax.axis_index("core")
    other = 1 - core
    a0 = x * other + y * core
    b0 = y * other + x * core

    def coords(a, b):
        a = lax.rem(a + 2 * side, side)
        b = lax.rem(b + 2 * side, side)
        return a * other + b * core, b * other + a * core

    def slot(a, b):
        xx, yy = coords(a, b)
        return out_hbm.at[pl.ds(pl.multiple_of(((xx * side + yy) * 2 + core) * rows, rows), rows)]

    def device(a, b, c):
        xx, yy = coords(a, b)
        return {"x": xx, "y": yy, "core": c}

    partner = device(a0, b0, other)
    peers = [device(a0 + 1, b0, core), device(a0 - 1, b0, core), device(a0, b0 + 1, core),
             device(a0, b0 - 1, core), partner]
    barrier = pltpu.get_barrier_semaphore()
    for peer in peers:
        pl.semaphore_signal(barrier, inc=1, device_id=peer, device_id_type=MESH)
    pl.semaphore_wait(barrier, len(peers))

    sent = {}

    def push(src, dst, target, index):
        cp = pltpu.make_async_remote_copy(
            src_ref=src, dst_ref=dst, send_sem=send_sem.at[index], recv_sem=recv_sem.at[index],
            device_id=target, device_id_type=MESH,
        )
        cp.start()
        sent[index] = cp
        return cp

    def along_b(j):
        src = slot(a0 + j, b0)
        push(src, src, device(a0, b0 + 1, core), 3 + j)
        push(src, src, device(a0, b0 - 1, core), 7 + j)

    mine = slot(a0, b0)
    own = pltpu.make_async_copy(shard_ref, mine, local_sem.at[0])
    own.start()
    up = push(shard_ref, mine, device(a0 + 1, b0, core), 0)
    down = push(shard_ref, mine, device(a0 - 1, b0, core), 1)
    own.wait()
    along_b(0)
    push(mine, mine, partner, 15)
    up.wait_recv()
    fwd = push(slot(a0 - 1, b0), slot(a0 - 1, b0), device(a0 + 1, b0, core), 2)
    along_b(3)
    push(slot(a0 - 1, b0), slot(a0 - 1, b0), partner, 16)
    down.wait_recv()
    along_b(1)
    push(slot(a0 + 1, b0), slot(a0 + 1, b0), partner, 17)
    fwd.wait_recv()
    along_b(2)
    push(slot(a0 + 2, b0), slot(a0 + 2, b0), partner, 18)
    later = {}
    for j in (0, 3, 1, 2):
        sent[3 + j].wait_recv()
        src = slot(a0 + j, b0 - 1)
        if j < 2:
            later[j] = push(src, src, device(a0, b0 + 1, core), 11 + j)
        push(src, src, partner, 19 + j)
        sent[7 + j].wait_recv()
        src = slot(a0 + j, b0 + 1)
        if j >= 2:
            later[j] = push(src, src, device(a0, b0 - 1, core), 11 + j)
        push(src, src, partner, 23 + j)
    for j in (0, 3, 1, 2):
        later[j].wait_recv()
        src = slot(a0 + j, b0 + 2)
        push(src, src, partner, 27 + j)
    for index in range(15, 31):
        pltpu.make_async_remote_copy(
            src_ref=mine, dst_ref=mine, send_sem=send_sem.at[index], recv_sem=recv_sem.at[index],
            device_id=partner, device_id_type=MESH,
        ).wait_recv()
    for index in sorted(sent):
        sent[index].wait_send()


def gather_rows(shard, collective):
    rows, width = shard.shape
    total = rows * lax.axis_size(SEQ)
    return pl.pallas_call(
        gather_kernel,
        out_shape=jax.ShapeDtypeStruct((total, width), shard.dtype),
        in_specs=[pl.BlockSpec(memory_space=pltpu.VMEM)],
        out_specs=pl.BlockSpec(memory_space=pl.ANY),
        scratch_shapes=[
            pltpu.SemaphoreType.DMA((31,)),
            pltpu.SemaphoreType.DMA((31,)),
            pltpu.SemaphoreType.DMA((1,)),
        ],
        compiler_params=pltpu.CompilerParams(collective_id=collective, has_side_effects=True),
        cost_estimate=pl.CostEstimate(flops=0, bytes_accessed=4 * total * width, transcendentals=0),
    )(shard)


def state_kernel(st_ref, out_ref, send_sem, recv_sem):
    count = out_ref.shape[0]
    side = 4
    me = (lax.axis_index("x") * side + lax.axis_index("y")) * 2 + lax.axis_index("core")

    def device(j):
        return {"x": j // (2 * side), "y": (j // 2) % side, "core": j % 2}

    barrier = pltpu.get_barrier_semaphore()

    def greet(o, carry):
        pl.semaphore_signal(barrier, inc=1, device_id=device(lax.rem(me + o, count)), device_id_type=MESH)
        return carry

    lax.fori_loop(1, count, greet, 0)
    pl.semaphore_wait(barrier, count - 1)

    def copy(o):
        j = lax.rem(me + o, count)
        return pltpu.make_async_remote_copy(
            src_ref=st_ref.at[(me + o) // count],
            dst_ref=out_ref.at[me],
            send_sem=send_sem.at[o - 1],
            recv_sem=recv_sem.at[o - 1],
            device_id=device(j),
            device_id_type=MESH,
        )

    def start(o, carry):
        copy(o).start()
        return carry

    lax.fori_loop(1, count, start, 0)
    out_ref[me] = jnp.zeros(out_ref.shape[1:], out_ref.dtype)

    def finish(o, carry):
        cp = copy(o)
        cp.wait_send()
        cp.wait_recv()
        return carry

    lax.fori_loop(1, count, finish, 0)


def exchange_states(states):
    count = lax.axis_size(SEQ)
    return pl.pallas_call(
        state_kernel,
        out_shape=jax.ShapeDtypeStruct((count,) + states.shape[1:], states.dtype),
        in_specs=[pl.BlockSpec(memory_space=pltpu.VMEM)],
        out_specs=pl.BlockSpec(memory_space=pltpu.VMEM),
        scratch_shapes=[pltpu.SemaphoreType.DMA((count - 1,)), pltpu.SemaphoreType.DMA((count - 1,))],
        compiler_params=pltpu.CompilerParams(collective_id=2, has_side_effects=True),
        cost_estimate=pl.CostEstimate(flops=0, bytes_accessed=8 * states[0].size * count, transcendentals=0),
    )(states)


def ring_kernel(n, gp_ref, w_hbm, out_ref, wbuf, acc, snd, rcv, wsem, send_sem, recv_sem):
    me = lax.axis_index("chan")
    right = lax.rem(me + 1, n)
    left = lax.rem(me + n - 1, n)
    half = out_ref.shape[1] // 2
    block = 2 * half
    tile = min(256, half)

    barrier = pltpu.get_barrier_semaphore()
    for neighbour in (left, right):
        pl.semaphore_signal(barrier, inc=1, device_id={"chan": neighbour}, device_id_type=MESH)
    pl.semaphore_wait(barrier, 2)

    def load(d, dest):
        first = pl.multiple_of(dest * block + d * half, 8)
        cp = pltpu.make_async_copy(w_hbm.at[pl.ds(first, half)], wbuf.at[d], wsem.at[d])
        cp.start()
        return cp

    def product(d):
        def body(j, carry):
            rows = pl.ds(pl.multiple_of(j * tile, tile), tile)
            acc[d, :, rows] = lax.dot_general(
                gp_ref[...], wbuf[d, rows, :], (((1,), (1,)), ((), ())),
                preferred_element_type=jnp.float32,
            )
            return carry

        lax.fori_loop(0, half // tile, body, 0)

    targets = (right, left)
    copies = [None, None]
    for step in range(n - 1):
        dests = (lax.rem(me + 2 * n - 1 - step, n), lax.rem(me + 1 + step, n))
        loads = [load(d, dests[d]) for d in (0, 1)]
        for d in (0, 1):
            loads[d].wait()
            product(d)
            if copies[d] is not None:
                copies[d].wait_recv()
                copies[d].wait_send()
                snd[d] = (acc[d] + rcv[d, step - 1].astype(jnp.float32)).astype(snd.dtype)
            else:
                snd[d] = acc[d].astype(snd.dtype)
            copies[d] = pltpu.make_async_remote_copy(
                src_ref=snd.at[d],
                dst_ref=rcv.at[d, step],
                send_sem=send_sem.at[d],
                recv_sem=recv_sem.at[d, step],
                device_id={"chan": targets[d]},
                device_id_type=MESH,
            )
            copies[d].start()
    loads = [load(d, me) for d in (0, 1)]
    for d in (0, 1):
        loads[d].wait()
        product(d)
        copies[d].wait_recv()
        copies[d].wait_send()
        out_ref[:, pl.ds(d * half, half)] = (
            acc[d] + rcv[d, n - 2].astype(jnp.float32)
        ).astype(out_ref.dtype)


def ring_reduce(grad_proj, whole_w, n):
    rows, width = grad_proj.shape
    block = whole_w.shape[0] // n
    half = block // 2
    return pl.pallas_call(
        functools.partial(ring_kernel, n),
        out_shape=jax.ShapeDtypeStruct((rows, block), jnp.bfloat16),
        in_specs=[pl.BlockSpec(memory_space=pltpu.VMEM), pl.BlockSpec(memory_space=pl.ANY)],
        out_specs=pl.BlockSpec(memory_space=pltpu.VMEM),
        scratch_shapes=[
            pltpu.VMEM((2, half, width), jnp.bfloat16),
            pltpu.VMEM((2, rows, half), jnp.float32),
            pltpu.VMEM((2, rows, half), jnp.bfloat16),
            pltpu.VMEM((2, n - 1, rows, half), jnp.bfloat16),
            pltpu.SemaphoreType.DMA((2,)),
            pltpu.SemaphoreType.DMA((2,)),
            pltpu.SemaphoreType.DMA((2, n - 1)),
        ],
        compiler_params=pltpu.CompilerParams(
            collective_id=0, has_side_effects=True, vmem_limit_bytes=60 * 1024 * 1024
        ),
        cost_estimate=pl.CostEstimate(
            flops=2 * rows * width * whole_w.shape[0],
            bytes_accessed=2 * (whole_w.size + grad_proj.size + rows * block),
            transcendentals=0,
        ),
    )(grad_proj, whole_w)


def split_powers(rates, first, step, count_hi, low):
    hi = jnp.arange(count_hi, dtype=f32)[:, None, None]
    lo = jnp.arange(low, dtype=f32)[:, None, None]
    shift = 0.0 if step > 0 else -step * low * (count_hi - 1)
    return (
        jnp.exp(-rates[None] * (step * low * hi + shift)),
        jnp.exp(-rates[None] * (first - shift + step * lo)),
    )


def mode_sum(amp, rates, first, step, length):
    low = 32
    e_hi, e_lo = split_powers(rates, first, step, length // low, low)
    scaled = amp[None] * e_hi
    total = jnp.sum(scaled[:, None] * e_lo[None], axis=2)
    return total.reshape(length, amp.shape[1])


def mode_states(signal, rates, first, step):
    low = 32
    length = signal.shape[0]
    e_hi, e_lo = split_powers(rates, first, step, length // low, low)
    pieces = signal.reshape(length // low, low, 1, signal.shape[1])
    inner = jnp.sum(pieces * e_lo[None], axis=1)
    return jnp.sum(inner * e_hi, axis=0)


def local(tokens, proj_weight, residues, decay_rates, skip_gain, grad_out):
    tok_rows = tokens.shape[0]
    chan_count = skip_gain.shape[0]
    seq_count = lax.axis_size(SEQ)
    me = lax.axis_index(SEQ)
    flat_w = proj_weight.reshape(proj_weight.shape[0], 3 * chan_count)
    whole_w = gather_rows(flat_w, 1)
    projected = jnp.dot(tokens, whole_w, preferred_element_type=f32)
    proj_vals = (
        lax.optimization_barrier(projected.astype(bf16))
        .astype(f32)
        .reshape(tok_rows, 3, chan_count)
    )
    query_in = proj_vals[:, 0]
    key_in = proj_vals[:, 1]
    value_in = proj_vals[:, 2]
    mixed_in = key_in * value_in
    grad_gate = grad_out.astype(f32)
    grad_mix = grad_gate * query_in

    rates = decay_rates
    modes = rates.shape[0]
    mode_gain = residues * jnp.sqrt(-jnp.expm1(-2.0 * rates))
    steps = jnp.arange(tok_rows, dtype=f32)

    end_fwd = mode_states(mixed_in, rates, float(tok_rows - 1), -1.0)
    end_bwd = mode_states(grad_mix, rates, 0.0, 1.0)
    states = jnp.stack([end_fwd, end_bwd])
    every = exchange_states(states)

    others = jnp.arange(seq_count, dtype=jnp.int32)
    gap_f = me - 1 - others
    gap_b = others - me - 1
    span = rates[None] * float(tok_rows)
    w_f = jnp.where(
        (gap_f >= 0)[:, None, None],
        jnp.exp(-span * jnp.maximum(gap_f, 0).astype(f32)[:, None, None]),
        0.0,
    )
    w_b = jnp.where(
        (gap_b >= 0)[:, None, None],
        jnp.exp(-span * jnp.maximum(gap_b, 0).astype(f32)[:, None, None]),
        0.0,
    )
    into_f = jnp.sum(w_f * every, axis=0) * mode_gain
    into_b = jnp.sum(w_b * every, axis=0) * mode_gain

    taps = mode_sum(mode_gain, rates, 0.0, 1.0, tok_rows)
    fwd, inv = dft_tables(tok_rows)
    fwd_b = fwd.astype(bf16)
    inv_b = inv.astype(bf16)
    fwd_r, inv_r = dft_tables(tok_rows, flip=True)
    spec = jnp.dot(fwd, taps, precision=lax.Precision.HIGHEST)
    row0 = (jnp.arange(tok_rows) == 0)[:, None]
    h_a = spec[:tok_rows]
    h_a2 = jnp.where(row0, spec[tok_rows:tok_rows + 1], h_a)
    h_b = jnp.where(row0, 0.0, spec[tok_rows:])

    local_f = spectral_conv(mixed_in, fwd_b, inv_b, h_a, h_a2, h_b)
    carry_f = mode_sum(into_f, rates, 1.0, 1.0, tok_rows)
    filtered = local_f + carry_f + skip_gain[None, :] * mixed_in
    gated_output = (query_in * filtered).astype(bf16)
    grad_query = grad_gate * filtered

    local_b = spectral_conv(grad_mix, fwd_r.astype(bf16), inv_r.astype(bf16), h_a, h_a2, h_b)
    carry_b = mode_sum(into_b, rates, float(tok_rows), -1.0, tok_rows)
    grad_conv = local_b + carry_b + skip_gain[None, :] * grad_mix

    grad_proj = jnp.stack([grad_query, grad_conv * value_in, grad_conv * key_in], axis=1).astype(bf16)
    grad_proj = grad_proj.reshape(tok_rows, 3 * chan_count)
    grad_tokens = ring_reduce(grad_proj, whole_w, lax.axis_size("chan"))
    return (gated_output, grad_tokens)


SEQ = ("x", "y", "core")


def solution(mesh):
    side, cores = 4, 2
    split = jax.sharding.Mesh(
        mesh.devices.reshape(side, mesh.shape["seq"] // (side * cores), cores, mesh.shape["chan"]),
        ("x", "y", "core", "chan"),
    )
    placed = (
        P(SEQ, None),
        P(SEQ, None, "chan"),
        P(None, "chan"),
        P(None, "chan"),
        P("chan"),
        P(SEQ, "chan"),
    )
    return jax.shard_map(
        local,
        mesh=split,
        in_specs=placed,
        out_specs=(P(SEQ, "chan"), P(SEQ, "chan")),
        check_vma=False,
    )
```

```python
import functools
import math

import jax
import jax.numpy as jnp
from jax import lax
from jax.experimental import pallas as pl
from jax.experimental.pallas import tpu as pltpu
from jax.sharding import PartitionSpec as P

MESH = pl.DeviceIdType.MESH

f32 = jnp.float32
bf16 = jnp.bfloat16


def dft_tables(block_len, flip=False):
    n_len = 2 * block_len
    low = 32
    high = block_len // low
    n = jnp.arange(block_len, dtype=jnp.int32)
    if flip:
        n = block_len - 1 - n

    def trig(mult):
        phase = (mult[:, None] * n[None, :]) % n_len
        angle = (2.0 * math.pi / n_len) * phase.astype(f32)
        return jnp.cos(angle), jnp.sin(angle)

    ca, sa = trig(jnp.arange(high, dtype=jnp.int32) * low)
    cb, sb = trig(jnp.arange(low, dtype=jnp.int32))
    nyquist = jnp.where(n % 2 == 0, 1.0, -1.0).astype(f32)
    first = (jnp.arange(block_len) == 0)[:, None]
    weight = jnp.where(jnp.arange(block_len) == 0, 1.0, 2.0).astype(f32) / n_len

    cos_rows = (ca[:, None, :] * cb[None] - sa[:, None, :] * sb[None]).reshape(block_len, block_len)
    sin_rows = (sa[:, None, :] * cb[None] + ca[:, None, :] * sb[None]).reshape(block_len, block_len)
    sin_rows = jnp.where(first, nyquist[None, :], sin_rows)
    fwd = jnp.concatenate([cos_rows, sin_rows], axis=0)

    cos_t = (ca.T[:, :, None] * cb.T[:, None, :] - sa.T[:, :, None] * sb.T[:, None, :]).reshape(
        block_len, block_len
    )
    sin_t = (sa.T[:, :, None] * cb.T[:, None, :] + ca.T[:, :, None] * sb.T[:, None, :]).reshape(
        block_len, block_len
    )
    sin_t = jnp.where(first.T, nyquist[:, None], sin_t)
    inv = jnp.concatenate([cos_t * weight[None, :], sin_t * weight[None, :]], axis=1)
    return fwd, inv


def gather_kernel(shard_ref, out_hbm, send_sem, recv_sem, local_sem):
    rows = shard_ref.shape[0]
    side = 4
    x = lax.axis_index("x")
    y = lax.axis_index("y")
    core = lax.axis_index("core")
    other = 1 - core
    a0 = x * other + y * core
    b0 = y * other + x * core

    def coords(a, b):
        a = lax.rem(a + 2 * side, side)
        b = lax.rem(b + 2 * side, side)
        return a * other + b * core, b * other + a * core

    def slot(a, b):
        xx, yy = coords(a, b)
        return out_hbm.at[pl.ds(pl.multiple_of(((xx * side + yy) * 2 + core) * rows, rows), rows)]

    def device(a, b, c):
        xx, yy = coords(a, b)
        return {"x": xx, "y": yy, "core": c}

    partner = device(a0, b0, other)
    peers = [device(a0 + 1, b0, core), device(a0 - 1, b0, core), device(a0, b0 + 1, core),
             device(a0, b0 - 1, core), partner]
    barrier = pltpu.get_barrier_semaphore()
    for peer in peers:
        pl.semaphore_signal(barrier, inc=1, device_id=peer, device_id_type=MESH)
    pl.semaphore_wait(barrier, len(peers))

    sent = {}

    def push(src, dst, target, index):
        cp = pltpu.make_async_remote_copy(
            src_ref=src, dst_ref=dst, send_sem=send_sem.at[index], recv_sem=recv_sem.at[index],
            device_id=target, device_id_type=MESH,
        )
        cp.start()
        sent[index] = cp
        return cp

    def along_b(j):
        src = slot(a0 + j, b0)
        push(src, src, device(a0, b0 + 1, core), 3 + j)
        push(src, src, device(a0, b0 - 1, core), 7 + j)

    mine = slot(a0, b0)
    own = pltpu.make_async_copy(shard_ref, mine, local_sem.at[0])
    own.start()
    up = push(shard_ref, mine, device(a0 + 1, b0, core), 0)
    down = push(shard_ref, mine, device(a0 - 1, b0, core), 1)
    own.wait()
    along_b(0)
    push(mine, mine, partner, 15)
    up.wait_recv()
    fwd = push(slot(a0 - 1, b0), slot(a0 - 1, b0), device(a0 + 1, b0, core), 2)
    along_b(3)
    push(slot(a0 - 1, b0), slot(a0 - 1, b0), partner, 16)
    down.wait_recv()
    along_b(1)
    push(slot(a0 + 1, b0), slot(a0 + 1, b0), partner, 17)
    fwd.wait_recv()
    along_b(2)
    push(slot(a0 + 2, b0), slot(a0 + 2, b0), partner, 18)
    later = {}
    for j in (0, 3, 1, 2):
        sent[3 + j].wait_recv()
        src = slot(a0 + j, b0 - 1)
        if j < 2:
            later[j] = push(src, src, device(a0, b0 + 1, core), 11 + j)
        push(src, src, partner, 19 + j)
        sent[7 + j].wait_recv()
        src = slot(a0 + j, b0 + 1)
        if j >= 2:
            later[j] = push(src, src, device(a0, b0 - 1, core), 11 + j)
        push(src, src, partner, 23 + j)
    for j in (0, 3, 1, 2):
        later[j].wait_recv()
        src = slot(a0 + j, b0 + 2)
        push(src, src, partner, 27 + j)
    for index in range(15, 31):
        pltpu.make_async_remote_copy(
            src_ref=mine, dst_ref=mine, send_sem=send_sem.at[index], recv_sem=recv_sem.at[index],
            device_id=partner, device_id_type=MESH,
        ).wait_recv()
    for index in sorted(sent):
        sent[index].wait_send()


def gather_rows(shard, collective):
    rows, width = shard.shape
    total = rows * lax.axis_size(SEQ)
    return pl.pallas_call(
        gather_kernel,
        out_shape=jax.ShapeDtypeStruct((total, width), shard.dtype),
        in_specs=[pl.BlockSpec(memory_space=pltpu.VMEM)],
        out_specs=pl.BlockSpec(memory_space=pl.ANY),
        scratch_shapes=[
            pltpu.SemaphoreType.DMA((31,)),
            pltpu.SemaphoreType.DMA((31,)),
            pltpu.SemaphoreType.DMA((1,)),
        ],
        compiler_params=pltpu.CompilerParams(collective_id=collective, has_side_effects=True),
        cost_estimate=pl.CostEstimate(flops=0, bytes_accessed=4 * total * width, transcendentals=0),
    )(shard)


def local_conv(sig_ref, fwd_ref, inv_ref, ha_ref, ha2_ref, hb_ref, out_ref):
    block_len = sig_ref.shape[0]
    lanes = 128

    def body(j, carry):
        cols = pl.ds(pl.multiple_of(j * lanes, lanes), lanes)
        sig = sig_ref[:, cols].astype(jnp.bfloat16)
        xc = jnp.dot(fwd_ref[:block_len, :], sig, preferred_element_type=jnp.float32)
        xs = jnp.dot(fwd_ref[block_len:, :], sig, preferred_element_type=jnp.float32)
        ha = ha_ref[:, cols]
        hb = hb_ref[:, cols]
        pr = (xc * ha - xs * hb).astype(jnp.bfloat16)
        pi = (xc * hb + xs * ha2_ref[:, cols]).astype(jnp.bfloat16)
        out_ref[:, cols] = jnp.dot(
            inv_ref[:, :block_len], pr, preferred_element_type=jnp.float32
        ) + jnp.dot(inv_ref[:, block_len:], pi, preferred_element_type=jnp.float32)
        return carry

    lax.fori_loop(0, sig_ref.shape[1] // lanes, body, 0)


def state_kernel(st_ref, mix_ref, gm_ref, fwd_ref, inv_ref, fwdr_ref, invr_ref, ha_ref, ha2_ref,
                 hb_ref, out_ref, loc_f_ref, loc_b_ref, send_sem, recv_sem):
    count = out_ref.shape[0]
    side = 4
    me = (lax.axis_index("x") * side + lax.axis_index("y")) * 2 + lax.axis_index("core")

    def device(j):
        return {"x": j // (2 * side), "y": (j // 2) % side, "core": j % 2}

    barrier = pltpu.get_barrier_semaphore()

    def greet(o, carry):
        pl.semaphore_signal(barrier, inc=1, device_id=device(lax.rem(me + o, count)), device_id_type=MESH)
        return carry

    lax.fori_loop(1, count, greet, 0)
    local_conv(mix_ref, fwd_ref, inv_ref, ha_ref, ha2_ref, hb_ref, loc_f_ref)
    pl.semaphore_wait(barrier, count - 1)

    def copy(o):
        j = lax.rem(me + o, count)
        return pltpu.make_async_remote_copy(
            src_ref=st_ref.at[(me + o) // count],
            dst_ref=out_ref.at[me],
            send_sem=send_sem.at[o - 1],
            recv_sem=recv_sem.at[o - 1],
            device_id=device(j),
            device_id_type=MESH,
        )

    def start(o, carry):
        copy(o).start()
        return carry

    lax.fori_loop(1, count, start, 0)
    out_ref[me] = jnp.zeros(out_ref.shape[1:], out_ref.dtype)
    local_conv(gm_ref, fwdr_ref, invr_ref, ha_ref, ha2_ref, hb_ref, loc_b_ref)

    def finish(o, carry):
        cp = copy(o)
        cp.wait_send()
        cp.wait_recv()
        return carry

    lax.fori_loop(1, count, finish, 0)


def exchange_states(states, mixed_in, grad_mix, tables, spectra):
    count = lax.axis_size(SEQ)
    vmem = pl.BlockSpec(memory_space=pltpu.VMEM)
    block = jax.ShapeDtypeStruct(mixed_in.shape, jnp.float32)
    rows, chans = mixed_in.shape
    return pl.pallas_call(
        state_kernel,
        out_shape=(jax.ShapeDtypeStruct((count,) + states.shape[1:], states.dtype), block, block),
        in_specs=[vmem] * 10,
        out_specs=(vmem, vmem, vmem),
        scratch_shapes=[pltpu.SemaphoreType.DMA((count - 1,)), pltpu.SemaphoreType.DMA((count - 1,))],
        compiler_params=pltpu.CompilerParams(
            collective_id=2, has_side_effects=True, vmem_limit_bytes=60 * 1024 * 1024
        ),
        cost_estimate=pl.CostEstimate(
            flops=2 * 4 * 2 * rows * rows * chans,
            bytes_accessed=8 * states[0].size * count + 4 * 8 * rows * chans,
            transcendentals=0,
        ),
    )(states, mixed_in, grad_mix, *tables, *spectra)


def ring_kernel(n, gp_ref, w_hbm, out_ref, wbuf, acc, snd, rcv, wsem, send_sem, recv_sem):
    me = lax.axis_index("chan")
    right = lax.rem(me + 1, n)
    left = lax.rem(me + n - 1, n)
    half = out_ref.shape[1] // 2
    block = 2 * half
    tile = min(256, half)

    barrier = pltpu.get_barrier_semaphore()
    for neighbour in (left, right):
        pl.semaphore_signal(barrier, inc=1, device_id={"chan": neighbour}, device_id_type=MESH)
    pl.semaphore_wait(barrier, 2)

    def load(d, dest):
        first = pl.multiple_of(dest * block + d * half, 8)
        cp = pltpu.make_async_copy(w_hbm.at[pl.ds(first, half)], wbuf.at[d], wsem.at[d])
        cp.start()
        return cp

    def product(d):
        def body(j, carry):
            rows = pl.ds(pl.multiple_of(j * tile, tile), tile)
            acc[d, :, rows] = lax.dot_general(
                gp_ref[...], wbuf[d, rows, :], (((1,), (1,)), ((), ())),
                preferred_element_type=jnp.float32,
            )
            return carry

        lax.fori_loop(0, half // tile, body, 0)

    targets = (right, left)
    copies = [None, None]
    for step in range(n - 1):
        dests = (lax.rem(me + 2 * n - 1 - step, n), lax.rem(me + 1 + step, n))
        loads = [load(d, dests[d]) for d in (0, 1)]
        for d in (0, 1):
            loads[d].wait()
            product(d)
            if copies[d] is not None:
                copies[d].wait_recv()
                copies[d].wait_send()
                snd[d] = (acc[d] + rcv[d, step - 1].astype(jnp.float32)).astype(snd.dtype)
            else:
                snd[d] = acc[d].astype(snd.dtype)
            copies[d] = pltpu.make_async_remote_copy(
                src_ref=snd.at[d],
                dst_ref=rcv.at[d, step],
                send_sem=send_sem.at[d],
                recv_sem=recv_sem.at[d, step],
                device_id={"chan": targets[d]},
                device_id_type=MESH,
            )
            copies[d].start()
    loads = [load(d, me) for d in (0, 1)]
    for d in (0, 1):
        loads[d].wait()
        product(d)
        copies[d].wait_recv()
        copies[d].wait_send()
        out_ref[:, pl.ds(d * half, half)] = (
            acc[d] + rcv[d, n - 2].astype(jnp.float32)
        ).astype(out_ref.dtype)


def ring_reduce(grad_proj, whole_w, n):
    rows, width = grad_proj.shape
    block = whole_w.shape[0] // n
    half = block // 2
    return pl.pallas_call(
        functools.partial(ring_kernel, n),
        out_shape=jax.ShapeDtypeStruct((rows, block), jnp.bfloat16),
        in_specs=[pl.BlockSpec(memory_space=pltpu.VMEM), pl.BlockSpec(memory_space=pl.ANY)],
        out_specs=pl.BlockSpec(memory_space=pltpu.VMEM),
        scratch_shapes=[
            pltpu.VMEM((2, half, width), jnp.bfloat16),
            pltpu.VMEM((2, rows, half), jnp.float32),
            pltpu.VMEM((2, rows, half), jnp.bfloat16),
            pltpu.VMEM((2, n - 1, rows, half), jnp.bfloat16),
            pltpu.SemaphoreType.DMA((2,)),
            pltpu.SemaphoreType.DMA((2,)),
            pltpu.SemaphoreType.DMA((2, n - 1)),
        ],
        compiler_params=pltpu.CompilerParams(
            collective_id=0, has_side_effects=True, vmem_limit_bytes=60 * 1024 * 1024
        ),
        cost_estimate=pl.CostEstimate(
            flops=2 * rows * width * whole_w.shape[0],
            bytes_accessed=2 * (whole_w.size + grad_proj.size + rows * block),
            transcendentals=0,
        ),
    )(grad_proj, whole_w)


def mode_sum(amp, rates, lag):
    total = amp[0] * jnp.exp(-rates[0] * lag)
    for r in range(1, rates.shape[0]):
        total = total + amp[r] * jnp.exp(-rates[r] * lag)
    return total


def local(tokens, proj_weight, residues, decay_rates, skip_gain, grad_out):
    tok_rows = tokens.shape[0]
    chan_count = skip_gain.shape[0]
    seq_count = lax.axis_size(SEQ)
    me = lax.axis_index(SEQ)
    flat_w = proj_weight.reshape(proj_weight.shape[0], 3 * chan_count)
    whole_w = gather_rows(flat_w, 1)
    projected = jnp.dot(tokens, whole_w, preferred_element_type=f32)
    proj_vals = (
        lax.optimization_barrier(projected.astype(bf16))
        .astype(f32)
        .reshape(tok_rows, 3, chan_count)
    )
    query_in = proj_vals[:, 0]
    key_in = proj_vals[:, 1]
    value_in = proj_vals[:, 2]
    mixed_in = key_in * value_in
    grad_gate = grad_out.astype(f32)
    grad_mix = grad_gate * query_in

    rates = decay_rates
    modes = rates.shape[0]
    mode_gain = residues * jnp.sqrt(-jnp.expm1(-2.0 * rates))
    steps = jnp.arange(tok_rows, dtype=f32)

    col = steps[:, None]
    end_fwd = jnp.stack(
        [jnp.sum(jnp.exp(-rates[r] * (tok_rows - 1 - col)) * mixed_in, axis=0) for r in range(modes)]
    )
    end_bwd = jnp.stack(
        [jnp.sum(jnp.exp(-rates[r] * col) * grad_mix, axis=0) for r in range(modes)]
    )
    states = jnp.stack([end_fwd, end_bwd])
    fwd, inv = dft_tables(tok_rows)
    fwd_r, inv_r = dft_tables(tok_rows, flip=True)
    taps = mode_sum(mode_gain, rates, col)
    spec = jnp.dot(fwd, taps, precision=lax.Precision.HIGHEST)
    row0 = (jnp.arange(tok_rows) == 0)[:, None]
    h_a = spec[:tok_rows]
    h_a2 = jnp.where(row0, spec[tok_rows:tok_rows + 1], h_a)
    h_b = jnp.where(row0, 0.0, spec[tok_rows:])
    tables = [t.astype(bf16) for t in (fwd, inv, fwd_r, inv_r)]
    every, local_f, local_b = exchange_states(states, mixed_in, grad_mix, tables, (h_a, h_a2, h_b))

    others = jnp.arange(seq_count, dtype=jnp.int32)
    gap_f = me - 1 - others
    gap_b = others - me - 1
    span = rates[None] * float(tok_rows)
    w_f = jnp.where(
        (gap_f >= 0)[:, None, None],
        jnp.exp(-span * jnp.maximum(gap_f, 0).astype(f32)[:, None, None]),
        0.0,
    )
    w_b = jnp.where(
        (gap_b >= 0)[:, None, None],
        jnp.exp(-span * jnp.maximum(gap_b, 0).astype(f32)[:, None, None]),
        0.0,
    )
    into_f = jnp.sum(w_f * every, axis=0) * mode_gain
    into_b = jnp.sum(w_b * every, axis=0) * mode_gain

    carry_f = mode_sum(into_f, rates, col + 1.0)
    filtered = local_f + carry_f + skip_gain[None, :] * mixed_in
    gated_output = (query_in * filtered).astype(bf16)
    grad_query = grad_gate * filtered

    carry_b = mode_sum(into_b, rates, tok_rows - col)
    grad_conv = local_b + carry_b + skip_gain[None, :] * grad_mix

    grad_proj = jnp.stack([grad_query, grad_conv * value_in, grad_conv * key_in], axis=1).astype(bf16)
    grad_proj = grad_proj.reshape(tok_rows, 3 * chan_count)
    grad_tokens = ring_reduce(grad_proj, whole_w, lax.axis_size("chan"))
    return (gated_output, grad_tokens)


SEQ = ("x", "y", "core")


def solution(mesh):
    side, cores = 4, 2
    split = jax.sharding.Mesh(
        mesh.devices.reshape(side, mesh.shape["seq"] // (side * cores), cores, mesh.shape["chan"]),
        ("x", "y", "core", "chan"),
    )
    placed = (
        P(SEQ, None),
        P(SEQ, None, "chan"),
        P(None, "chan"),
        P(None, "chan"),
        P("chan"),
        P(SEQ, "chan"),
    )
    return jax.shard_map(
        local,
        mesh=split,
        in_specs=placed,
        out_specs=(P(SEQ, "chan"), P(SEQ, "chan")),
        check_vma=False,
    )
```

```python
import functools
import math

import jax
import jax.numpy as jnp
from jax import lax
from jax.experimental import pallas as pl
from jax.experimental.pallas import tpu as pltpu
from jax.sharding import PartitionSpec as P

MESH = pl.DeviceIdType.MESH

f32 = jnp.float32
bf16 = jnp.bfloat16


def dft_tables(block_len, flip=False):
    n_len = 2 * block_len
    low = 32
    high = block_len // low
    n = jnp.arange(block_len, dtype=jnp.int32)
    if flip:
        n = block_len - 1 - n

    def trig(mult):
        phase = (mult[:, None] * n[None, :]) % n_len
        angle = (2.0 * math.pi / n_len) * phase.astype(f32)
        return jnp.cos(angle), jnp.sin(angle)

    ca, sa = trig(jnp.arange(high, dtype=jnp.int32) * low)
    cb, sb = trig(jnp.arange(low, dtype=jnp.int32))
    nyquist = jnp.where(n % 2 == 0, 1.0, -1.0).astype(f32)
    first = (jnp.arange(block_len) == 0)[:, None]
    weight = jnp.where(jnp.arange(block_len) == 0, 1.0, 2.0).astype(f32) / n_len

    cos_rows = (ca[:, None, :] * cb[None] - sa[:, None, :] * sb[None]).reshape(block_len, block_len)
    sin_rows = (sa[:, None, :] * cb[None] + ca[:, None, :] * sb[None]).reshape(block_len, block_len)
    sin_rows = jnp.where(first, nyquist[None, :], sin_rows)
    fwd = jnp.concatenate([cos_rows, sin_rows], axis=0)

    cos_t = (ca.T[:, :, None] * cb.T[:, None, :] - sa.T[:, :, None] * sb.T[:, None, :]).reshape(
        block_len, block_len
    )
    sin_t = (sa.T[:, :, None] * cb.T[:, None, :] + ca.T[:, :, None] * sb.T[:, None, :]).reshape(
        block_len, block_len
    )
    sin_t = jnp.where(first.T, nyquist[:, None], sin_t)
    inv = jnp.concatenate([cos_t * weight[None, :], sin_t * weight[None, :]], axis=1)
    return fwd, inv


def spectral_conv(signal, fwd, inv, h_a, h_a2, h_b):
    block_len = signal.shape[0]
    spec = jnp.dot(fwd, signal.astype(bf16), preferred_element_type=f32)
    xc = spec[:block_len]
    xs = spec[block_len:]
    pr = xc * h_a - xs * h_b
    pi = xc * h_b + xs * h_a2
    prod = jnp.concatenate([pr, pi], axis=0).astype(bf16)
    return jnp.dot(inv, prod, preferred_element_type=f32)


def gather_kernel(shard_ref, out_hbm, send_sem, recv_sem, local_sem):
    rows = shard_ref.shape[0]
    side = 4
    x = lax.axis_index("x")
    y = lax.axis_index("y")
    core = lax.axis_index("core")
    other = 1 - core
    a0 = x * other + y * core
    b0 = y * other + x * core

    def coords(a, b):
        a = lax.rem(a + 2 * side, side)
        b = lax.rem(b + 2 * side, side)
        return a * other + b * core, b * other + a * core

    def slot(a, b):
        xx, yy = coords(a, b)
        return out_hbm.at[pl.ds(pl.multiple_of(((xx * side + yy) * 2 + core) * rows, rows), rows)]

    def device(a, b, c):
        xx, yy = coords(a, b)
        return {"x": xx, "y": yy, "core": c}

    partner = device(a0, b0, other)
    peers = [device(a0 + 1, b0, core), device(a0 - 1, b0, core), device(a0, b0 + 1, core),
             device(a0, b0 - 1, core), partner]
    barrier = pltpu.get_barrier_semaphore()
    for peer in peers:
        pl.semaphore_signal(barrier, inc=1, device_id=peer, device_id_type=MESH)
    pl.semaphore_wait(barrier, len(peers))

    sent = {}

    def push(src, dst, target, index):
        cp = pltpu.make_async_remote_copy(
            src_ref=src, dst_ref=dst, send_sem=send_sem.at[index], recv_sem=recv_sem.at[index],
            device_id=target, device_id_type=MESH,
        )
        cp.start()
        sent[index] = cp
        return cp

    def along_b(j):
        src = slot(a0 + j, b0)
        push(src, src, device(a0, b0 + 1, core), 3 + j)
        push(src, src, device(a0, b0 - 1, core), 7 + j)

    mine = slot(a0, b0)
    own = pltpu.make_async_copy(shard_ref, mine, local_sem.at[0])
    own.start()
    up = push(shard_ref, mine, device(a0 + 1, b0, core), 0)
    down = push(shard_ref, mine, device(a0 - 1, b0, core), 1)
    own.wait()
    along_b(0)
    push(mine, mine, partner, 15)
    up.wait_recv()
    fwd = push(slot(a0 - 1, b0), slot(a0 - 1, b0), device(a0 + 1, b0, core), 2)
    along_b(3)
    push(slot(a0 - 1, b0), slot(a0 - 1, b0), partner, 16)
    down.wait_recv()
    along_b(1)
    push(slot(a0 + 1, b0), slot(a0 + 1, b0), partner, 17)
    fwd.wait_recv()
    along_b(2)
    push(slot(a0 + 2, b0), slot(a0 + 2, b0), partner, 18)
    later = {}
    for j in (0, 3, 1, 2):
        sent[3 + j].wait_recv()
        src = slot(a0 + j, b0 - 1)
        if j < 2:
            later[j] = push(src, src, device(a0, b0 + 1, core), 11 + j)
        push(src, src, partner, 19 + j)
        sent[7 + j].wait_recv()
        src = slot(a0 + j, b0 + 1)
        if j >= 2:
            later[j] = push(src, src, device(a0, b0 - 1, core), 11 + j)
        push(src, src, partner, 23 + j)
    for j in (0, 3, 1, 2):
        later[j].wait_recv()
        src = slot(a0 + j, b0 + 2)
        push(src, src, partner, 27 + j)
    for index in range(15, 31):
        pltpu.make_async_remote_copy(
            src_ref=mine, dst_ref=mine, send_sem=send_sem.at[index], recv_sem=recv_sem.at[index],
            device_id=partner, device_id_type=MESH,
        ).wait_recv()
    for index in sorted(sent):
        sent[index].wait_send()


def gather_rows(shard, collective):
    rows, width = shard.shape
    total = rows * lax.axis_size(SEQ)
    return pl.pallas_call(
        gather_kernel,
        out_shape=jax.ShapeDtypeStruct((total, width), shard.dtype),
        in_specs=[pl.BlockSpec(memory_space=pltpu.VMEM)],
        out_specs=pl.BlockSpec(memory_space=pl.ANY),
        scratch_shapes=[
            pltpu.SemaphoreType.DMA((31,)),
            pltpu.SemaphoreType.DMA((31,)),
            pltpu.SemaphoreType.DMA((1,)),
        ],
        compiler_params=pltpu.CompilerParams(collective_id=collective, has_side_effects=True),
        cost_estimate=pl.CostEstimate(flops=0, bytes_accessed=4 * total * width, transcendentals=0),
    )(shard)


def state_kernel(st_ref, out_ref, send_sem, recv_sem):
    count = out_ref.shape[0]
    side = 4
    me = (lax.axis_index("x") * side + lax.axis_index("y")) * 2 + lax.axis_index("core")

    def device(j):
        return {"x": j // (2 * side), "y": (j // 2) % side, "core": j % 2}

    barrier = pltpu.get_barrier_semaphore()

    def greet(o, carry):
        pl.semaphore_signal(barrier, inc=1, device_id=device(lax.rem(me + o, count)), device_id_type=MESH)
        return carry

    lax.fori_loop(1, count, greet, 0)
    pl.semaphore_wait(barrier, count - 1)

    def copy(o):
        j = lax.rem(me + o, count)
        return pltpu.make_async_remote_copy(
            src_ref=st_ref.at[(me + o) // count],
            dst_ref=out_ref.at[me],
            send_sem=send_sem.at[o - 1],
            recv_sem=recv_sem.at[o - 1],
            device_id=device(j),
            device_id_type=MESH,
        )

    def start(o, carry):
        copy(o).start()
        return carry

    lax.fori_loop(1, count, start, 0)
    out_ref[me] = jnp.zeros(out_ref.shape[1:], out_ref.dtype)

    def finish(o, carry):
        cp = copy(o)
        cp.wait_send()
        cp.wait_recv()
        return carry

    lax.fori_loop(1, count, finish, 0)


def exchange_states(states):
    count = lax.axis_size(SEQ)
    return pl.pallas_call(
        state_kernel,
        out_shape=jax.ShapeDtypeStruct((count,) + states.shape[1:], states.dtype),
        in_specs=[pl.BlockSpec(memory_space=pltpu.VMEM)],
        out_specs=pl.BlockSpec(memory_space=pltpu.VMEM),
        scratch_shapes=[pltpu.SemaphoreType.DMA((count - 1,)), pltpu.SemaphoreType.DMA((count - 1,))],
        compiler_params=pltpu.CompilerParams(collective_id=2, has_side_effects=True),
        cost_estimate=pl.CostEstimate(flops=0, bytes_accessed=8 * states[0].size * count, transcendentals=0),
    )(states)


def ring_kernel(n, gp_ref, w_hbm, out_ref, wbuf, acc, snd, rcv, wsem, send_sem, recv_sem):
    me = lax.axis_index("chan")
    right = lax.rem(me + 1, n)
    left = lax.rem(me + n - 1, n)
    half = out_ref.shape[1] // 2
    block = 2 * half
    tile = min(256, half)

    barrier = pltpu.get_barrier_semaphore()
    for neighbour in (left, right):
        pl.semaphore_signal(barrier, inc=1, device_id={"chan": neighbour}, device_id_type=MESH)
    pl.semaphore_wait(barrier, 2)

    def load(d, dest):
        first = pl.multiple_of(dest * block + d * half, 8)
        cp = pltpu.make_async_copy(w_hbm.at[pl.ds(first, half)], wbuf.at[d], wsem.at[d])
        cp.start()
        return cp

    def product(d):
        def body(j, carry):
            rows = pl.ds(pl.multiple_of(j * tile, tile), tile)
            acc[d, :, rows] = lax.dot_general(
                gp_ref[...], wbuf[d, rows, :], (((1,), (1,)), ((), ())),
                preferred_element_type=jnp.float32,
            )
            return carry

        lax.fori_loop(0, half // tile, body, 0)

    targets = (right, left)
    copies = [None, None]
    for step in range(n - 1):
        dests = (lax.rem(me + 2 * n - 1 - step, n), lax.rem(me + 1 + step, n))
        loads = [load(d, dests[d]) for d in (0, 1)]
        for d in (0, 1):
            loads[d].wait()
            product(d)
            if copies[d] is not None:
                copies[d].wait_recv()
                copies[d].wait_send()
                snd[d] = (acc[d] + rcv[d, step - 1].astype(jnp.float32)).astype(snd.dtype)
            else:
                snd[d] = acc[d].astype(snd.dtype)
            copies[d] = pltpu.make_async_remote_copy(
                src_ref=snd.at[d],
                dst_ref=rcv.at[d, step],
                send_sem=send_sem.at[d],
                recv_sem=recv_sem.at[d, step],
                device_id={"chan": targets[d]},
                device_id_type=MESH,
            )
            copies[d].start()
    loads = [load(d, me) for d in (0, 1)]
    for d in (0, 1):
        loads[d].wait()
        product(d)
        copies[d].wait_recv()
        copies[d].wait_send()
        out_ref[:, pl.ds(d * half, half)] = acc[d] + rcv[d, n - 2].astype(jnp.float32)


def ring_reduce(grad_proj, whole_w, n):
    rows, width = grad_proj.shape
    block = whole_w.shape[0] // n
    half = block // 2
    return pl.pallas_call(
        functools.partial(ring_kernel, n),
        out_shape=jax.ShapeDtypeStruct((rows, block), jnp.float32),
        in_specs=[pl.BlockSpec(memory_space=pltpu.VMEM), pl.BlockSpec(memory_space=pl.ANY)],
        out_specs=pl.BlockSpec(memory_space=pltpu.VMEM),
        scratch_shapes=[
            pltpu.VMEM((2, half, width), jnp.bfloat16),
            pltpu.VMEM((2, rows, half), jnp.float32),
            pltpu.VMEM((2, rows, half), jnp.bfloat16),
            pltpu.VMEM((2, n - 1, rows, half), jnp.bfloat16),
            pltpu.SemaphoreType.DMA((2,)),
            pltpu.SemaphoreType.DMA((2,)),
            pltpu.SemaphoreType.DMA((2, n - 1)),
        ],
        compiler_params=pltpu.CompilerParams(
            collective_id=0, has_side_effects=True, vmem_limit_bytes=60 * 1024 * 1024
        ),
        cost_estimate=pl.CostEstimate(
            flops=2 * rows * width * whole_w.shape[0],
            bytes_accessed=2 * (whole_w.size + grad_proj.size + rows * block),
            transcendentals=0,
        ),
    )(grad_proj, whole_w)


def mode_sum(amp, rates, lag):
    total = amp[0] * jnp.exp(-rates[0] * lag)
    for r in range(1, rates.shape[0]):
        total = total + amp[r] * jnp.exp(-rates[r] * lag)
    return total


def local(tokens, proj_weight, residues, decay_rates, skip_gain, grad_out):
    tok_rows = tokens.shape[0]
    chan_count = skip_gain.shape[0]
    seq_count = lax.axis_size(SEQ)
    me = lax.axis_index(SEQ)
    flat_w = proj_weight.reshape(proj_weight.shape[0], 3 * chan_count)
    whole_w = gather_rows(flat_w, 1)
    projected = jnp.dot(tokens, whole_w, preferred_element_type=f32)
    proj_vals = (
        lax.optimization_barrier(projected.astype(bf16))
        .astype(f32)
        .reshape(tok_rows, 3, chan_count)
    )
    query_in = proj_vals[:, 0]
    key_in = proj_vals[:, 1]
    value_in = proj_vals[:, 2]
    mixed_in = key_in * value_in
    grad_gate = grad_out.astype(f32)
    grad_mix = grad_gate * query_in

    rates = decay_rates
    modes = rates.shape[0]
    mode_gain = residues * jnp.sqrt(-jnp.expm1(-2.0 * rates))
    steps = jnp.arange(tok_rows, dtype=f32)

    col = steps[:, None]
    end_fwd = jnp.stack(
        [jnp.sum(jnp.exp(-rates[r] * (tok_rows - 1 - col)) * mixed_in, axis=0) for r in range(modes)]
    )
    end_bwd = jnp.stack(
        [jnp.sum(jnp.exp(-rates[r] * col) * grad_mix, axis=0) for r in range(modes)]
    )
    states = jnp.stack([end_fwd, end_bwd])
    every = exchange_states(states)

    others = jnp.arange(seq_count, dtype=jnp.int32)
    gap_f = me - 1 - others
    gap_b = others - me - 1
    span = rates[None] * float(tok_rows)
    w_f = jnp.where(
        (gap_f >= 0)[:, None, None],
        jnp.exp(-span * jnp.maximum(gap_f, 0).astype(f32)[:, None, None]),
        0.0,
    )
    w_b = jnp.where(
        (gap_b >= 0)[:, None, None],
        jnp.exp(-span * jnp.maximum(gap_b, 0).astype(f32)[:, None, None]),
        0.0,
    )
    into_f = jnp.sum(w_f * every, axis=0) * mode_gain
    into_b = jnp.sum(w_b * every, axis=0) * mode_gain

    taps = mode_sum(mode_gain, rates, col)
    fwd, inv = dft_tables(tok_rows)
    fwd_b = fwd.astype(bf16)
    inv_b = inv.astype(bf16)
    fwd_r, inv_r = dft_tables(tok_rows, flip=True)
    spec = jnp.dot(fwd, taps, precision=lax.Precision.HIGHEST)
    row0 = (jnp.arange(tok_rows) == 0)[:, None]
    h_a = spec[:tok_rows]
    h_a2 = jnp.where(row0, spec[tok_rows:tok_rows + 1], h_a)
    h_b = jnp.where(row0, 0.0, spec[tok_rows:])

    local_f = spectral_conv(mixed_in, fwd_b, inv_b, h_a, h_a2, h_b)
    carry_f = mode_sum(into_f, rates, col + 1.0)
    filtered = local_f + carry_f + skip_gain[None, :] * mixed_in
    gated_output = (query_in * filtered).astype(bf16)
    grad_query = grad_gate * filtered

    local_b = spectral_conv(grad_mix, fwd_r.astype(bf16), inv_r.astype(bf16), h_a, h_a2, h_b)
    carry_b = mode_sum(into_b, rates, tok_rows - col)
    grad_conv = local_b + carry_b + skip_gain[None, :] * grad_mix

    grad_proj = jnp.stack([grad_query, grad_conv * value_in, grad_conv * key_in], axis=1).astype(bf16)
    grad_proj = grad_proj.reshape(tok_rows, 3 * chan_count)
    grad_tokens = ring_reduce(grad_proj, whole_w, lax.axis_size("chan")).astype(bf16)
    return (gated_output, grad_tokens)


SEQ = ("x", "y", "core")


def solution(mesh):
    side, cores = 4, 2
    split = jax.sharding.Mesh(
        mesh.devices.reshape(side, mesh.shape["seq"] // (side * cores), cores, mesh.shape["chan"]),
        ("x", "y", "core", "chan"),
    )
    placed = (
        P(SEQ, None),
        P(SEQ, None, "chan"),
        P(None, "chan"),
        P(None, "chan"),
        P("chan"),
        P(SEQ, "chan"),
    )
    return jax.shard_map(
        local,
        mesh=split,
        in_specs=placed,
        out_specs=(P(SEQ, "chan"), P(SEQ, "chan")),
        check_vma=False,
    )
```

```python
import functools
import math

import jax
import jax.numpy as jnp
from jax import lax
from jax.experimental import pallas as pl
from jax.experimental.pallas import tpu as pltpu
from jax.sharding import PartitionSpec as P

MESH = pl.DeviceIdType.MESH

f32 = jnp.float32
bf16 = jnp.bfloat16


def dft_tables(block_len, flip=False):
    n_len = 2 * block_len
    low = 32
    high = block_len // low
    n = jnp.arange(block_len, dtype=jnp.int32)
    if flip:
        n = block_len - 1 - n

    def trig(mult):
        phase = (mult[:, None] * n[None, :]) % n_len
        angle = (2.0 * math.pi / n_len) * phase.astype(f32)
        return jnp.cos(angle), jnp.sin(angle)

    ca, sa = trig(jnp.arange(high, dtype=jnp.int32) * low)
    cb, sb = trig(jnp.arange(low, dtype=jnp.int32))
    nyquist = jnp.where(n % 2 == 0, 1.0, -1.0).astype(f32)
    first = (jnp.arange(block_len) == 0)[:, None]
    weight = jnp.where(jnp.arange(block_len) == 0, 1.0, 2.0).astype(f32) / n_len

    cos_rows = (ca[:, None, :] * cb[None] - sa[:, None, :] * sb[None]).reshape(block_len, block_len)
    sin_rows = (sa[:, None, :] * cb[None] + ca[:, None, :] * sb[None]).reshape(block_len, block_len)
    sin_rows = jnp.where(first, nyquist[None, :], sin_rows)
    fwd = jnp.concatenate([cos_rows, sin_rows], axis=0)

    cos_t = (ca.T[:, :, None] * cb.T[:, None, :] - sa.T[:, :, None] * sb.T[:, None, :]).reshape(
        block_len, block_len
    )
    sin_t = (sa.T[:, :, None] * cb.T[:, None, :] + ca.T[:, :, None] * sb.T[:, None, :]).reshape(
        block_len, block_len
    )
    sin_t = jnp.where(first.T, nyquist[:, None], sin_t)
    inv = jnp.concatenate([cos_t * weight[None, :], sin_t * weight[None, :]], axis=1)
    return fwd, inv


def spectral_conv(signal, fwd, inv, h_a, h_a2, h_b):
    block_len = signal.shape[0]
    spec = jnp.dot(fwd, signal.astype(bf16), preferred_element_type=f32)
    xc = spec[:block_len]
    xs = spec[block_len:]
    pr = xc * h_a - xs * h_b
    pi = xc * h_b + xs * h_a2
    prod = jnp.concatenate([pr, pi], axis=0).astype(bf16)
    return jnp.dot(inv, prod, preferred_element_type=f32)


def gather_kernel(shard_ref, out_hbm, send_sem, recv_sem, local_sem):
    rows = shard_ref.shape[0]
    side = 4
    x = lax.axis_index("x")
    y = lax.axis_index("y")
    core = lax.axis_index("core")
    other = 1 - core
    a0 = x * other + y * core
    b0 = y * other + x * core

    def coords(a, b):
        a = lax.rem(a + 2 * side, side)
        b = lax.rem(b + 2 * side, side)
        return a * other + b * core, b * other + a * core

    def slot(a, b):
        xx, yy = coords(a, b)
        return out_hbm.at[pl.ds(pl.multiple_of(((xx * side + yy) * 2 + core) * rows, rows), rows)]

    def device(a, b, c):
        xx, yy = coords(a, b)
        return {"x": xx, "y": yy, "core": c}

    partner = device(a0, b0, other)
    peers = [device(a0 + 1, b0, core), device(a0 - 1, b0, core), device(a0, b0 + 1, core),
             device(a0, b0 - 1, core), partner]
    barrier = pltpu.get_barrier_semaphore()
    for peer in peers:
        pl.semaphore_signal(barrier, inc=1, device_id=peer, device_id_type=MESH)
    pl.semaphore_wait(barrier, len(peers))

    sent = {}

    def push(src, dst, target, index):
        cp = pltpu.make_async_remote_copy(
            src_ref=src, dst_ref=dst, send_sem=send_sem.at[index], recv_sem=recv_sem.at[index],
            device_id=target, device_id_type=MESH,
        )
        cp.start()
        sent[index] = cp
        return cp

    def along_b(j):
        src = slot(a0 + j, b0)
        push(src, src, device(a0, b0 + 1, core), 3 + j)
        push(src, src, device(a0, b0 - 1, core), 7 + j)

    mine = slot(a0, b0)
    own = pltpu.make_async_copy(shard_ref, mine, local_sem.at[0])
    own.start()
    up = push(shard_ref, mine, device(a0 + 1, b0, core), 0)
    down = push(shard_ref, mine, device(a0 - 1, b0, core), 1)
    own.wait()
    along_b(0)
    push(mine, mine, partner, 15)
    up.wait_recv()
    fwd = push(slot(a0 - 1, b0), slot(a0 - 1, b0), device(a0 + 1, b0, core), 2)
    along_b(3)
    push(slot(a0 - 1, b0), slot(a0 - 1, b0), partner, 16)
    down.wait_recv()
    along_b(1)
    push(slot(a0 + 1, b0), slot(a0 + 1, b0), partner, 17)
    fwd.wait_recv()
    along_b(2)
    push(slot(a0 + 2, b0), slot(a0 + 2, b0), partner, 18)
    later = {}
    for j in (0, 3, 1, 2):
        sent[3 + j].wait_recv()
        src = slot(a0 + j, b0 - 1)
        if j < 2:
            later[j] = push(src, src, device(a0, b0 + 1, core), 11 + j)
        push(src, src, partner, 19 + j)
        sent[7 + j].wait_recv()
        src = slot(a0 + j, b0 + 1)
        if j >= 2:
            later[j] = push(src, src, device(a0, b0 - 1, core), 11 + j)
        push(src, src, partner, 23 + j)
    for j in (0, 3, 1, 2):
        later[j].wait_recv()
        src = slot(a0 + j, b0 + 2)
        push(src, src, partner, 27 + j)
    for index in range(15, 31):
        pltpu.make_async_remote_copy(
            src_ref=mine, dst_ref=mine, send_sem=send_sem.at[index], recv_sem=recv_sem.at[index],
            device_id=partner, device_id_type=MESH,
        ).wait_recv()
    for index in sorted(sent):
        sent[index].wait_send()


def gather_rows(shard, collective):
    rows, width = shard.shape
    total = rows * lax.axis_size(SEQ)
    return pl.pallas_call(
        gather_kernel,
        out_shape=jax.ShapeDtypeStruct((total, width), shard.dtype),
        in_specs=[pl.BlockSpec(memory_space=pltpu.VMEM)],
        out_specs=pl.BlockSpec(memory_space=pl.ANY),
        scratch_shapes=[
            pltpu.SemaphoreType.DMA((31,)),
            pltpu.SemaphoreType.DMA((31,)),
            pltpu.SemaphoreType.DMA((1,)),
        ],
        compiler_params=pltpu.CompilerParams(collective_id=collective, has_side_effects=True),
        cost_estimate=pl.CostEstimate(flops=0, bytes_accessed=4 * total * width, transcendentals=0),
    )(shard)


def state_kernel(st_ref, out_ref, send_sem, recv_sem):
    count = out_ref.shape[0]
    side = 4
    me = (lax.axis_index("x") * side + lax.axis_index("y")) * 2 + lax.axis_index("core")

    def device(j):
        return {"x": j // (2 * side), "y": (j // 2) % side, "core": j % 2}

    barrier = pltpu.get_barrier_semaphore()

    def greet(o, carry):
        pl.semaphore_signal(barrier, inc=1, device_id=device(lax.rem(me + o, count)), device_id_type=MESH)
        return carry

    lax.fori_loop(1, count, greet, 0)
    pl.semaphore_wait(barrier, count - 1)

    def copy(o):
        j = lax.rem(me + o, count)
        return pltpu.make_async_remote_copy(
            src_ref=st_ref.at[(me + o) // count],
            dst_ref=out_ref.at[me],
            send_sem=send_sem.at[o - 1],
            recv_sem=recv_sem.at[o - 1],
            device_id=device(j),
            device_id_type=MESH,
        )

    def start(o, carry):
        copy(o).start()
        return carry

    lax.fori_loop(1, count, start, 0)
    out_ref[me] = jnp.zeros(out_ref.shape[1:], out_ref.dtype)

    def finish(o, carry):
        cp = copy(o)
        cp.wait_send()
        cp.wait_recv()
        return carry

    lax.fori_loop(1, count, finish, 0)


def exchange_states(states):
    count = lax.axis_size(SEQ)
    return pl.pallas_call(
        state_kernel,
        out_shape=jax.ShapeDtypeStruct((count,) + states.shape[1:], states.dtype),
        in_specs=[pl.BlockSpec(memory_space=pltpu.VMEM)],
        out_specs=pl.BlockSpec(memory_space=pltpu.VMEM),
        scratch_shapes=[pltpu.SemaphoreType.DMA((count - 1,)), pltpu.SemaphoreType.DMA((count - 1,))],
        compiler_params=pltpu.CompilerParams(collective_id=2, has_side_effects=True),
        cost_estimate=pl.CostEstimate(flops=0, bytes_accessed=8 * states[0].size * count, transcendentals=0),
    )(states)


def ring_kernel(n, gp_ref, w_hbm, out_ref, wbuf, acc, snd, rcv, wsem, send_sem, recv_sem):
    me = lax.axis_index("chan")
    right = lax.rem(me + 1, n)
    left = lax.rem(me + n - 1, n)
    half = out_ref.shape[1] // 2
    block = 2 * half
    tile = min(256, half)

    barrier = pltpu.get_barrier_semaphore()
    for neighbour in (left, right):
        pl.semaphore_signal(barrier, inc=1, device_id={"chan": neighbour}, device_id_type=MESH)

    def load(d, dest):
        first = pl.multiple_of(dest * block + d * half, 8)
        cp = pltpu.make_async_copy(w_hbm.at[pl.ds(first, half)], wbuf.at[d], wsem.at[d])
        cp.start()
        return cp

    def product(d):
        def body(j, carry):
            rows = pl.ds(pl.multiple_of(j * tile, tile), tile)
            acc[d, :, rows] = lax.dot_general(
                gp_ref[...], wbuf[d, rows, :], (((1,), (1,)), ((), ())),
                preferred_element_type=jnp.float32,
            )
            return carry

        lax.fori_loop(0, half // tile, body, 0)

    targets = (right, left)
    copies = [None, None]
    for step in range(n - 1):
        dests = (lax.rem(me + 2 * n - 1 - step, n), lax.rem(me + 1 + step, n))
        loads = [load(d, dests[d]) for d in (0, 1)]
        if step == 0:
            for d in (0, 1):
                loads[d].wait()
                product(d)
            pl.semaphore_wait(barrier, 2)
        for d in (0, 1):
            if step > 0:
                loads[d].wait()
                product(d)
            if copies[d] is not None:
                copies[d].wait_recv()
                copies[d].wait_send()
                snd[d] = (acc[d] + rcv[d, step - 1].astype(jnp.float32)).astype(snd.dtype)
            else:
                snd[d] = acc[d].astype(snd.dtype)
            copies[d] = pltpu.make_async_remote_copy(
                src_ref=snd.at[d],
                dst_ref=rcv.at[d, step],
                send_sem=send_sem.at[d],
                recv_sem=recv_sem.at[d, step],
                device_id={"chan": targets[d]},
                device_id_type=MESH,
            )
            copies[d].start()
    loads = [load(d, me) for d in (0, 1)]
    for d in (0, 1):
        loads[d].wait()
        product(d)
        copies[d].wait_recv()
        copies[d].wait_send()
        out_ref[:, pl.ds(d * half, half)] = (
            acc[d] + rcv[d, n - 2].astype(jnp.float32)
        ).astype(out_ref.dtype)


def ring_reduce(grad_proj, whole_w, n):
    rows, width = grad_proj.shape
    block = whole_w.shape[0] // n
    half = block // 2
    return pl.pallas_call(
        functools.partial(ring_kernel, n),
        out_shape=jax.ShapeDtypeStruct((rows, block), jnp.bfloat16),
        in_specs=[pl.BlockSpec(memory_space=pltpu.VMEM), pl.BlockSpec(memory_space=pl.ANY)],
        out_specs=pl.BlockSpec(memory_space=pltpu.VMEM),
        scratch_shapes=[
            pltpu.VMEM((2, half, width), jnp.bfloat16),
            pltpu.VMEM((2, rows, half), jnp.float32),
            pltpu.VMEM((2, rows, half), jnp.bfloat16),
            pltpu.VMEM((2, n - 1, rows, half), jnp.bfloat16),
            pltpu.SemaphoreType.DMA((2,)),
            pltpu.SemaphoreType.DMA((2,)),
            pltpu.SemaphoreType.DMA((2, n - 1)),
        ],
        compiler_params=pltpu.CompilerParams(
            collective_id=0, has_side_effects=True, vmem_limit_bytes=60 * 1024 * 1024
        ),
        cost_estimate=pl.CostEstimate(
            flops=2 * rows * width * whole_w.shape[0],
            bytes_accessed=2 * (whole_w.size + grad_proj.size + rows * block),
            transcendentals=0,
        ),
    )(grad_proj, whole_w)


def mode_sum(amp, rates, lag):
    total = amp[0] * jnp.exp(-rates[0] * lag)
    for r in range(1, rates.shape[0]):
        total = total + amp[r] * jnp.exp(-rates[r] * lag)
    return total


def local(tokens, proj_weight, residues, decay_rates, skip_gain, grad_out):
    tok_rows = tokens.shape[0]
    chan_count = skip_gain.shape[0]
    seq_count = lax.axis_size(SEQ)
    me = lax.axis_index(SEQ)
    flat_w = proj_weight.reshape(proj_weight.shape[0], 3 * chan_count)
    whole_w = gather_rows(flat_w, 1)
    projected = jnp.dot(tokens, whole_w, preferred_element_type=f32)
    proj_vals = (
        lax.optimization_barrier(projected.astype(bf16))
        .astype(f32)
        .reshape(tok_rows, 3, chan_count)
    )
    query_in = proj_vals[:, 0]
    key_in = proj_vals[:, 1]
    value_in = proj_vals[:, 2]
    mixed_in = key_in * value_in
    grad_gate = grad_out.astype(f32)
    grad_mix = grad_gate * query_in

    rates = decay_rates
    modes = rates.shape[0]
    mode_gain = residues * jnp.sqrt(-jnp.expm1(-2.0 * rates))
    steps = jnp.arange(tok_rows, dtype=f32)

    col = steps[:, None]
    end_fwd = jnp.stack(
        [jnp.sum(jnp.exp(-rates[r] * (tok_rows - 1 - col)) * mixed_in, axis=0) for r in range(modes)]
    )
    end_bwd = jnp.stack(
        [jnp.sum(jnp.exp(-rates[r] * col) * grad_mix, axis=0) for r in range(modes)]
    )
    states = jnp.stack([end_fwd, end_bwd])
    every = exchange_states(states)

    others = jnp.arange(seq_count, dtype=jnp.int32)
    gap_f = me - 1 - others
    gap_b = others - me - 1
    span = rates[None] * float(tok_rows)
    w_f = jnp.where(
        (gap_f >= 0)[:, None, None],
        jnp.exp(-span * jnp.maximum(gap_f, 0).astype(f32)[:, None, None]),
        0.0,
    )
    w_b = jnp.where(
        (gap_b >= 0)[:, None, None],
        jnp.exp(-span * jnp.maximum(gap_b, 0).astype(f32)[:, None, None]),
        0.0,
    )
    into_f = jnp.sum(w_f * every, axis=0) * mode_gain
    into_b = jnp.sum(w_b * every, axis=0) * mode_gain

    taps = mode_sum(mode_gain, rates, col)
    fwd, inv = dft_tables(tok_rows)
    fwd_b = fwd.astype(bf16)
    inv_b = inv.astype(bf16)
    fwd_r, inv_r = dft_tables(tok_rows, flip=True)
    spec = jnp.dot(fwd, taps, precision=lax.Precision.HIGHEST)
    row0 = (jnp.arange(tok_rows) == 0)[:, None]
    h_a = spec[:tok_rows]
    h_a2 = jnp.where(row0, spec[tok_rows:tok_rows + 1], h_a)
    h_b = jnp.where(row0, 0.0, spec[tok_rows:])

    local_f = spectral_conv(mixed_in, fwd_b, inv_b, h_a, h_a2, h_b)
    carry_f = mode_sum(into_f, rates, col + 1.0)
    filtered = local_f + carry_f + skip_gain[None, :] * mixed_in
    gated_output = (query_in * filtered).astype(bf16)
    grad_query = grad_gate * filtered

    local_b = spectral_conv(grad_mix, fwd_r.astype(bf16), inv_r.astype(bf16), h_a, h_a2, h_b)
    carry_b = mode_sum(into_b, rates, tok_rows - col)
    grad_conv = local_b + carry_b + skip_gain[None, :] * grad_mix

    grad_proj = jnp.stack([grad_query, grad_conv * value_in, grad_conv * key_in], axis=1).astype(bf16)
    grad_proj = grad_proj.reshape(tok_rows, 3 * chan_count)
    grad_tokens = ring_reduce(grad_proj, whole_w, lax.axis_size("chan"))
    return (gated_output, grad_tokens)


SEQ = ("x", "y", "core")


def solution(mesh):
    side, cores = 4, 2
    split = jax.sharding.Mesh(
        mesh.devices.reshape(side, mesh.shape["seq"] // (side * cores), cores, mesh.shape["chan"]),
        ("x", "y", "core", "chan"),
    )
    placed = (
        P(SEQ, None),
        P(SEQ, None, "chan"),
        P(None, "chan"),
        P(None, "chan"),
        P("chan"),
        P(SEQ, "chan"),
    )
    return jax.shard_map(
        local,
        mesh=split,
        in_specs=placed,
        out_specs=(P(SEQ, "chan"), P(SEQ, "chan")),
        check_vma=False,
    )
```

```python
import functools
import math

import jax
import jax.numpy as jnp
from jax import lax
from jax.experimental import pallas as pl
from jax.experimental.pallas import tpu as pltpu
from jax.sharding import PartitionSpec as P

MESH = pl.DeviceIdType.MESH

f32 = jnp.float32
bf16 = jnp.bfloat16


def dft_tables(block_len, flip=False):
    n_len = 2 * block_len
    low = 32
    high = block_len // low
    n = jnp.arange(block_len, dtype=jnp.int32)
    if flip:
        n = block_len - 1 - n

    def trig(mult):
        phase = (mult[:, None] * n[None, :]) % n_len
        angle = (2.0 * math.pi / n_len) * phase.astype(f32)
        return jnp.cos(angle), jnp.sin(angle)

    ca, sa = trig(jnp.arange(high, dtype=jnp.int32) * low)
    cb, sb = trig(jnp.arange(low, dtype=jnp.int32))
    nyquist = jnp.where(n % 2 == 0, 1.0, -1.0).astype(f32)
    first = (jnp.arange(block_len) == 0)[:, None]
    weight = jnp.where(jnp.arange(block_len) == 0, 1.0, 2.0).astype(f32) / n_len

    cos_rows = (ca[:, None, :] * cb[None] - sa[:, None, :] * sb[None]).reshape(block_len, block_len)
    sin_rows = (sa[:, None, :] * cb[None] + ca[:, None, :] * sb[None]).reshape(block_len, block_len)
    sin_rows = jnp.where(first, nyquist[None, :], sin_rows)
    fwd = jnp.concatenate([cos_rows, sin_rows], axis=0)

    cos_t = (ca.T[:, :, None] * cb.T[:, None, :] - sa.T[:, :, None] * sb.T[:, None, :]).reshape(
        block_len, block_len
    )
    sin_t = (sa.T[:, :, None] * cb.T[:, None, :] + ca.T[:, :, None] * sb.T[:, None, :]).reshape(
        block_len, block_len
    )
    sin_t = jnp.where(first.T, nyquist[:, None], sin_t)
    inv = jnp.concatenate([cos_t * weight[None, :], sin_t * weight[None, :]], axis=1)
    return fwd, inv


def spectral_conv(signal, fwd, inv, h_a, h_a2, h_b):
    block_len = signal.shape[0]
    spec = jnp.dot(fwd, signal.astype(bf16), preferred_element_type=f32)
    xc = spec[:block_len]
    xs = spec[block_len:]
    pr = xc * h_a - xs * h_b
    pi = xc * h_b + xs * h_a2
    prod = jnp.concatenate([pr, pi], axis=0).astype(bf16)
    return jnp.dot(inv, prod, preferred_element_type=f32)


def gather_kernel(shard_ref, out_hbm, send_sem, recv_sem, local_sem):
    rows = shard_ref.shape[0]
    side = 4
    x = lax.axis_index("x")
    y = lax.axis_index("y")
    core = lax.axis_index("core")
    other = 1 - core
    a0 = x * other + y * core
    b0 = y * other + x * core

    def coords(a, b):
        a = lax.rem(a + 2 * side, side)
        b = lax.rem(b + 2 * side, side)
        return a * other + b * core, b * other + a * core

    def slot(a, b):
        xx, yy = coords(a, b)
        return out_hbm.at[pl.ds(pl.multiple_of(((xx * side + yy) * 2 + core) * rows, rows), rows)]

    def device(a, b, c):
        xx, yy = coords(a, b)
        return {"x": xx, "y": yy, "core": c}

    partner = device(a0, b0, other)
    peers = [device(a0 + 1, b0, core), device(a0 - 1, b0, core), device(a0, b0 + 1, core),
             device(a0, b0 - 1, core), partner]
    barrier = pltpu.get_barrier_semaphore()
    for peer in peers:
        pl.semaphore_signal(barrier, inc=1, device_id=peer, device_id_type=MESH)
    pl.semaphore_wait(barrier, len(peers))

    sent = {}

    def push(src, dst, target, index):
        cp = pltpu.make_async_remote_copy(
            src_ref=src, dst_ref=dst, send_sem=send_sem.at[index], recv_sem=recv_sem.at[index],
            device_id=target, device_id_type=MESH,
        )
        cp.start()
        sent[index] = cp
        return cp

    def along_b(j):
        src = slot(a0 + j, b0)
        push(src, src, device(a0, b0 + 1, core), 3 + j)
        push(src, src, device(a0, b0 - 1, core), 7 + j)

    mine = slot(a0, b0)
    own = pltpu.make_async_copy(shard_ref, mine, local_sem.at[0])
    own.start()
    up = push(shard_ref, mine, device(a0 + 1, b0, core), 0)
    down = push(shard_ref, mine, device(a0 - 1, b0, core), 1)
    own.wait()
    along_b(0)
    push(mine, mine, partner, 15)
    up.wait_recv()
    fwd = push(slot(a0 - 1, b0), slot(a0 - 1, b0), device(a0 + 1, b0, core), 2)
    along_b(3)
    push(slot(a0 - 1, b0), slot(a0 - 1, b0), partner, 16)
    down.wait_recv()
    along_b(1)
    push(slot(a0 + 1, b0), slot(a0 + 1, b0), partner, 17)
    fwd.wait_recv()
    along_b(2)
    push(slot(a0 + 2, b0), slot(a0 + 2, b0), partner, 18)
    later = {}
    for j in (0, 3, 1, 2):
        sent[3 + j].wait_recv()
        src = slot(a0 + j, b0 - 1)
        if j < 2:
            later[j] = push(src, src, device(a0, b0 + 1, core), 11 + j)
        push(src, src, partner, 19 + j)
        sent[7 + j].wait_recv()
        src = slot(a0 + j, b0 + 1)
        if j >= 2:
            later[j] = push(src, src, device(a0, b0 - 1, core), 11 + j)
        push(src, src, partner, 23 + j)
    for j in (0, 3, 1, 2):
        later[j].wait_recv()
        src = slot(a0 + j, b0 + 2)
        push(src, src, partner, 27 + j)
    for index in range(15, 31):
        pltpu.make_async_remote_copy(
            src_ref=mine, dst_ref=mine, send_sem=send_sem.at[index], recv_sem=recv_sem.at[index],
            device_id=partner, device_id_type=MESH,
        ).wait_recv()
    for index in sorted(sent):
        sent[index].wait_send()


def gather_rows(shard, collective):
    rows, width = shard.shape
    total = rows * lax.axis_size(SEQ)
    return pl.pallas_call(
        gather_kernel,
        out_shape=jax.ShapeDtypeStruct((total, width), shard.dtype),
        in_specs=[pl.BlockSpec(memory_space=pltpu.VMEM)],
        out_specs=pl.BlockSpec(memory_space=pl.ANY),
        scratch_shapes=[
            pltpu.SemaphoreType.DMA((31,)),
            pltpu.SemaphoreType.DMA((31,)),
            pltpu.SemaphoreType.DMA((1,)),
        ],
        compiler_params=pltpu.CompilerParams(collective_id=collective, has_side_effects=True),
        cost_estimate=pl.CostEstimate(flops=0, bytes_accessed=4 * total * width, transcendentals=0),
    )(shard)


def state_kernel(st_ref, out_ref, send_sem, recv_sem):
    count = out_ref.shape[0]
    side = 4
    me = (lax.axis_index("x") * side + lax.axis_index("y")) * 2 + lax.axis_index("core")

    def device(j):
        return {"x": j // (2 * side), "y": (j // 2) % side, "core": j % 2}

    barrier = pltpu.get_barrier_semaphore()

    def greet(o, carry):
        pl.semaphore_signal(barrier, inc=1, device_id=device(lax.rem(me + o, count)), device_id_type=MESH)
        return carry

    lax.fori_loop(1, count, greet, 0)
    pl.semaphore_wait(barrier, count - 1)

    def copy(o):
        j = lax.rem(me + o, count)
        return pltpu.make_async_remote_copy(
            src_ref=st_ref.at[(me + o) // count],
            dst_ref=out_ref.at[me],
            send_sem=send_sem.at[o - 1],
            recv_sem=recv_sem.at[o - 1],
            device_id=device(j),
            device_id_type=MESH,
        )

    def start(o, carry):
        copy(o).start()
        return carry

    lax.fori_loop(1, count, start, 0)
    out_ref[me] = jnp.zeros(out_ref.shape[1:], out_ref.dtype)

    def finish(o, carry):
        cp = copy(o)
        cp.wait_send()
        cp.wait_recv()
        return carry

    lax.fori_loop(1, count, finish, 0)


def exchange_states(states):
    count = lax.axis_size(SEQ)
    return pl.pallas_call(
        state_kernel,
        out_shape=jax.ShapeDtypeStruct((count,) + states.shape[1:], states.dtype),
        in_specs=[pl.BlockSpec(memory_space=pltpu.VMEM)],
        out_specs=pl.BlockSpec(memory_space=pltpu.VMEM),
        scratch_shapes=[pltpu.SemaphoreType.DMA((count - 1,)), pltpu.SemaphoreType.DMA((count - 1,))],
        compiler_params=pltpu.CompilerParams(collective_id=2, has_side_effects=True),
        cost_estimate=pl.CostEstimate(flops=0, bytes_accessed=8 * states[0].size * count, transcendentals=0),
    )(states)


def ring_kernel(n, gp_ref, w_hbm, out_ref, wbuf, acc, snd, rcv, wsem, send_sem, recv_sem):
    me = lax.axis_index("chan")
    right = lax.rem(me + 1, n)
    left = lax.rem(me + n - 1, n)
    half = out_ref.shape[1] // 2
    block = 2 * half
    tile = min(256, half)

    barrier = pltpu.get_barrier_semaphore()
    for neighbour in (left, right):
        pl.semaphore_signal(barrier, inc=1, device_id={"chan": neighbour}, device_id_type=MESH)
    pl.semaphore_wait(barrier, 2)

    def load(d, dest):
        first = pl.multiple_of(dest * block + d * half, 8)
        cp = pltpu.make_async_copy(w_hbm.at[pl.ds(first, half)], wbuf.at[d], wsem.at[d])
        cp.start()
        return cp

    def product(d):
        def body(j, carry):
            rows = pl.ds(pl.multiple_of(j * tile, tile), tile)
            acc[d, :, rows] = lax.dot_general(
                gp_ref[...], wbuf[d, rows, :], (((1,), (1,)), ((), ())),
                preferred_element_type=jnp.float32,
            )
            return carry

        lax.fori_loop(0, half // tile, body, 0)

    targets = (right, left)
    copies = [None, None]
    for step in range(n - 1):
        dests = (lax.rem(me + 2 * n - 1 - step, n), lax.rem(me + 1 + step, n))
        loads = [load(d, dests[d]) for d in (0, 1)]
        for d in (0, 1):
            loads[d].wait()
            product(d)
            if copies[d] is not None:
                copies[d].wait_recv()
                copies[d].wait_send()
                snd[d] = (acc[d] + rcv[d, step - 1].astype(jnp.float32)).astype(snd.dtype)
            else:
                snd[d] = acc[d].astype(snd.dtype)
            copies[d] = pltpu.make_async_remote_copy(
                src_ref=snd.at[d],
                dst_ref=rcv.at[d, step],
                send_sem=send_sem.at[d],
                recv_sem=recv_sem.at[d, step],
                device_id={"chan": targets[d]},
                device_id_type=MESH,
            )
            copies[d].start()
    loads = [load(d, me) for d in (0, 1)]
    for d in (0, 1):
        loads[d].wait()
        product(d)
        copies[d].wait_recv()
        copies[d].wait_send()
        out_ref[:, pl.ds(d * half, half)] = (
            acc[d] + rcv[d, n - 2].astype(jnp.float32)
        ).astype(out_ref.dtype)


def ring_reduce(grad_proj, whole_w, n):
    rows, width = grad_proj.shape
    block = whole_w.shape[0] // n
    half = block // 2
    return pl.pallas_call(
        functools.partial(ring_kernel, n),
        out_shape=jax.ShapeDtypeStruct((rows, block), jnp.bfloat16),
        in_specs=[pl.BlockSpec(memory_space=pltpu.VMEM), pl.BlockSpec(memory_space=pl.ANY)],
        out_specs=pl.BlockSpec(memory_space=pltpu.VMEM),
        scratch_shapes=[
            pltpu.VMEM((2, half, width), jnp.bfloat16),
            pltpu.VMEM((2, rows, half), jnp.float32),
            pltpu.VMEM((2, rows, half), jnp.bfloat16),
            pltpu.VMEM((2, n - 1, rows, half), jnp.bfloat16),
            pltpu.SemaphoreType.DMA((2,)),
            pltpu.SemaphoreType.DMA((2,)),
            pltpu.SemaphoreType.DMA((2, n - 1)),
        ],
        compiler_params=pltpu.CompilerParams(
            collective_id=0, has_side_effects=True, vmem_limit_bytes=60 * 1024 * 1024
        ),
        cost_estimate=pl.CostEstimate(
            flops=2 * rows * width * whole_w.shape[0],
            bytes_accessed=2 * (whole_w.size + grad_proj.size + rows * block),
            transcendentals=0,
        ),
    )(grad_proj, whole_w)


def mode_sum(amp, rates, lag):
    total = amp[0] * jnp.exp(-rates[0] * lag)
    for r in range(1, rates.shape[0]):
        total = total + amp[r] * jnp.exp(-rates[r] * lag)
    return total


def local(tokens, proj_weight, residues, decay_rates, skip_gain, grad_out):
    tok_rows = tokens.shape[0]
    chan_count = skip_gain.shape[0]
    seq_count = lax.axis_size(SEQ)
    me = lax.axis_index(SEQ)
    flat_w = proj_weight.reshape(proj_weight.shape[0], 3 * chan_count)
    whole_w = gather_rows(flat_w, 1)
    projected = jnp.dot(tokens, whole_w, preferred_element_type=f32)
    proj_vals = (
        lax.optimization_barrier(projected.astype(bf16))
        .astype(f32)
        .reshape(tok_rows, 3, chan_count)
    )
    query_in = proj_vals[:, 0]
    key_in = proj_vals[:, 1]
    value_in = proj_vals[:, 2]
    mixed_in = key_in * value_in
    grad_gate = grad_out.astype(f32)
    grad_mix = grad_gate * query_in

    rates = decay_rates
    modes = rates.shape[0]
    mode_gain = residues * jnp.sqrt(-jnp.expm1(-2.0 * rates))
    steps = jnp.arange(tok_rows, dtype=f32)

    col = steps[:, None]
    end_fwd = jnp.stack(
        [jnp.sum(jnp.exp(-rates[r] * (tok_rows - 1 - col)) * mixed_in, axis=0) for r in range(modes)]
    )
    end_bwd = jnp.stack(
        [jnp.sum(jnp.exp(-rates[r] * col) * grad_mix, axis=0) for r in range(modes)]
    )
    states = jnp.stack([end_fwd, end_bwd])
    every = exchange_states(states.astype(bf16)).astype(f32)

    others = jnp.arange(seq_count, dtype=jnp.int32)
    gap_f = me - 1 - others
    gap_b = others - me - 1
    span = rates[None] * float(tok_rows)
    w_f = jnp.where(
        (gap_f >= 0)[:, None, None],
        jnp.exp(-span * jnp.maximum(gap_f, 0).astype(f32)[:, None, None]),
        0.0,
    )
    w_b = jnp.where(
        (gap_b >= 0)[:, None, None],
        jnp.exp(-span * jnp.maximum(gap_b, 0).astype(f32)[:, None, None]),
        0.0,
    )
    into_f = jnp.sum(w_f * every, axis=0) * mode_gain
    into_b = jnp.sum(w_b * every, axis=0) * mode_gain

    taps = mode_sum(mode_gain, rates, col)
    fwd, inv = dft_tables(tok_rows)
    fwd_b = fwd.astype(bf16)
    inv_b = inv.astype(bf16)
    fwd_r, inv_r = dft_tables(tok_rows, flip=True)
    spec = jnp.dot(fwd, taps, precision=lax.Precision.HIGHEST)
    row0 = (jnp.arange(tok_rows) == 0)[:, None]
    h_a = spec[:tok_rows]
    h_a2 = jnp.where(row0, spec[tok_rows:tok_rows + 1], h_a)
    h_b = jnp.where(row0, 0.0, spec[tok_rows:])

    local_f = spectral_conv(mixed_in, fwd_b, inv_b, h_a, h_a2, h_b)
    carry_f = mode_sum(into_f, rates, col + 1.0)
    filtered = local_f + carry_f + skip_gain[None, :] * mixed_in
    gated_output = (query_in * filtered).astype(bf16)
    grad_query = grad_gate * filtered

    local_b = spectral_conv(grad_mix, fwd_r.astype(bf16), inv_r.astype(bf16), h_a, h_a2, h_b)
    carry_b = mode_sum(into_b, rates, tok_rows - col)
    grad_conv = local_b + carry_b + skip_gain[None, :] * grad_mix

    grad_proj = jnp.stack([grad_query, grad_conv * value_in, grad_conv * key_in], axis=1).astype(bf16)
    grad_proj = grad_proj.reshape(tok_rows, 3 * chan_count)
    grad_tokens = ring_reduce(grad_proj, whole_w, lax.axis_size("chan"))
    return (gated_output, grad_tokens)


SEQ = ("x", "y", "core")


def solution(mesh):
    side, cores = 4, 2
    split = jax.sharding.Mesh(
        mesh.devices.reshape(side, mesh.shape["seq"] // (side * cores), cores, mesh.shape["chan"]),
        ("x", "y", "core", "chan"),
    )
    placed = (
        P(SEQ, None),
        P(SEQ, None, "chan"),
        P(None, "chan"),
        P(None, "chan"),
        P("chan"),
        P(SEQ, "chan"),
    )
    return jax.shard_map(
        local,
        mesh=split,
        in_specs=placed,
        out_specs=(P(SEQ, "chan"), P(SEQ, "chan")),
        check_vma=False,
    )
```

```python
import functools
import math

import jax
import jax.numpy as jnp
from jax import lax
from jax.experimental import pallas as pl
from jax.experimental.pallas import tpu as pltpu
from jax.sharding import PartitionSpec as P

MESH = pl.DeviceIdType.MESH

f32 = jnp.float32
bf16 = jnp.bfloat16


def dft_tables(block_len, flip=False):
    n_len = 2 * block_len
    low = 32
    high = block_len // low
    n = jnp.arange(block_len, dtype=jnp.int32)
    if flip:
        n = block_len - 1 - n

    def trig(mult):
        phase = (mult[:, None] * n[None, :]) % n_len
        angle = (2.0 * math.pi / n_len) * phase.astype(f32)
        return jnp.cos(angle), jnp.sin(angle)

    ca, sa = trig(jnp.arange(high, dtype=jnp.int32) * low)
    cb, sb = trig(jnp.arange(low, dtype=jnp.int32))
    nyquist = jnp.where(n % 2 == 0, 1.0, -1.0).astype(f32)
    first = (jnp.arange(block_len) == 0)[:, None]
    weight = jnp.where(jnp.arange(block_len) == 0, 1.0, 2.0).astype(f32) / n_len

    cos_rows = (ca[:, None, :] * cb[None] - sa[:, None, :] * sb[None]).reshape(block_len, block_len)
    sin_rows = (sa[:, None, :] * cb[None] + ca[:, None, :] * sb[None]).reshape(block_len, block_len)
    sin_rows = jnp.where(first, nyquist[None, :], sin_rows)
    fwd = jnp.concatenate([cos_rows, sin_rows], axis=0)

    cos_t = (ca.T[:, :, None] * cb.T[:, None, :] - sa.T[:, :, None] * sb.T[:, None, :]).reshape(
        block_len, block_len
    )
    sin_t = (sa.T[:, :, None] * cb.T[:, None, :] + ca.T[:, :, None] * sb.T[:, None, :]).reshape(
        block_len, block_len
    )
    sin_t = jnp.where(first.T, nyquist[:, None], sin_t)
    inv = jnp.concatenate([cos_t * weight[None, :], sin_t * weight[None, :]], axis=1)
    return fwd, inv


def spectral_conv(signal, fwd, inv, h_a, h_a2, h_b):
    block_len = signal.shape[0]
    spec = jnp.dot(fwd, signal.astype(bf16), preferred_element_type=f32)
    xc = spec[:block_len]
    xs = spec[block_len:]
    pr = xc * h_a - xs * h_b
    pi = xc * h_b + xs * h_a2
    prod = jnp.concatenate([pr, pi], axis=0).astype(bf16)
    return jnp.dot(inv, prod, preferred_element_type=f32)


def gather_kernel(shard_ref, out_hbm, send_sem, recv_sem, local_sem):
    rows = shard_ref.shape[0]
    side = 4
    x = lax.axis_index("x")
    y = lax.axis_index("y")
    core = lax.axis_index("core")
    other = 1 - core
    a0 = x * other + y * core
    b0 = y * other + x * core

    def coords(a, b):
        a = lax.rem(a + 2 * side, side)
        b = lax.rem(b + 2 * side, side)
        return a * other + b * core, b * other + a * core

    def slot(a, b):
        xx, yy = coords(a, b)
        return out_hbm.at[pl.ds(pl.multiple_of(((xx * side + yy) * 2 + core) * rows, rows), rows)]

    def device(a, b, c):
        xx, yy = coords(a, b)
        return {"x": xx, "y": yy, "core": c}

    partner = device(a0, b0, other)
    peers = [device(a0 + 1, b0, core), device(a0 - 1, b0, core), device(a0, b0 + 1, core),
             device(a0, b0 - 1, core), partner]
    barrier = pltpu.get_barrier_semaphore()
    for peer in peers:
        pl.semaphore_signal(barrier, inc=1, device_id=peer, device_id_type=MESH)
    pl.semaphore_wait(barrier, len(peers))

    sent = {}

    def push(src, dst, target, index):
        cp = pltpu.make_async_remote_copy(
            src_ref=src, dst_ref=dst, send_sem=send_sem.at[index], recv_sem=recv_sem.at[index],
            device_id=target, device_id_type=MESH,
        )
        cp.start()
        sent[index] = cp
        return cp

    def along_b(j):
        src = slot(a0 + j, b0)
        push(src, src, device(a0, b0 + 1, core), 3 + j)
        push(src, src, device(a0, b0 - 1, core), 7 + j)

    mine = slot(a0, b0)
    own = pltpu.make_async_copy(shard_ref, mine, local_sem.at[0])
    own.start()
    up = push(shard_ref, mine, device(a0 + 1, b0, core), 0)
    down = push(shard_ref, mine, device(a0 - 1, b0, core), 1)
    own.wait()
    along_b(0)
    push(mine, mine, partner, 15)
    up.wait_recv()
    fwd = push(slot(a0 - 1, b0), slot(a0 - 1, b0), device(a0 + 1, b0, core), 2)
    along_b(3)
    push(slot(a0 - 1, b0), slot(a0 - 1, b0), partner, 16)
    down.wait_recv()
    along_b(1)
    push(slot(a0 + 1, b0), slot(a0 + 1, b0), partner, 17)
    fwd.wait_recv()
    along_b(2)
    push(slot(a0 + 2, b0), slot(a0 + 2, b0), partner, 18)
    later = {}
    for j in (0, 3, 1, 2):
        sent[3 + j].wait_recv()
        src = slot(a0 + j, b0 - 1)
        if j < 2:
            later[j] = push(src, src, device(a0, b0 + 1, core), 11 + j)
        push(src, src, partner, 19 + j)
        sent[7 + j].wait_recv()
        src = slot(a0 + j, b0 + 1)
        if j >= 2:
            later[j] = push(src, src, device(a0, b0 - 1, core), 11 + j)
        push(src, src, partner, 23 + j)
    for j in (0, 3, 1, 2):
        later[j].wait_recv()
        src = slot(a0 + j, b0 + 2)
        push(src, src, partner, 27 + j)
    for index in range(15, 31):
        pltpu.make_async_remote_copy(
            src_ref=mine, dst_ref=mine, send_sem=send_sem.at[index], recv_sem=recv_sem.at[index],
            device_id=partner, device_id_type=MESH,
        ).wait_recv()
    for index in sorted(sent):
        sent[index].wait_send()


def gather_rows(shard, collective):
    rows, width = shard.shape
    total = rows * lax.axis_size(SEQ)
    return pl.pallas_call(
        gather_kernel,
        out_shape=jax.ShapeDtypeStruct((total, width), shard.dtype),
        in_specs=[pl.BlockSpec(memory_space=pltpu.VMEM)],
        out_specs=pl.BlockSpec(memory_space=pl.ANY),
        scratch_shapes=[
            pltpu.SemaphoreType.DMA((31,)),
            pltpu.SemaphoreType.DMA((31,)),
            pltpu.SemaphoreType.DMA((1,)),
        ],
        compiler_params=pltpu.CompilerParams(collective_id=collective, has_side_effects=True),
        cost_estimate=pl.CostEstimate(flops=0, bytes_accessed=4 * total * width, transcendentals=0),
    )(shard)


def state_kernel(st_ref, out_ref, pair, send_sem, recv_sem, pair_sem):
    chips = out_ref.shape[0]
    side = 4
    chip = lax.axis_index("x") * side + lax.axis_index("y")
    core = lax.axis_index("core")
    other = 1 - core

    def device(k, c):
        return {"x": k // side, "y": k % side, "core": c}

    barrier = pltpu.get_barrier_semaphore()
    pl.semaphore_signal(barrier, inc=1, device_id=device(chip, other), device_id_type=MESH)

    def greet(o, carry):
        pl.semaphore_signal(barrier, inc=1, device_id=device(lax.rem(chip + o, chips), core),
                            device_id_type=MESH)
        return carry

    lax.fori_loop(1, chips, greet, 0)
    pl.semaphore_wait(barrier, chips)

    swap = pltpu.make_async_remote_copy(
        src_ref=st_ref, dst_ref=pair.at[core], send_sem=pair_sem.at[0], recv_sem=pair_sem.at[1],
        device_id=device(chip, other), device_id_type=MESH,
    )
    swap.start()
    pair[core] = st_ref[...]
    swap.wait()

    def copy(o):
        return pltpu.make_async_remote_copy(
            src_ref=pair.at[:, (chip + o) // chips],
            dst_ref=out_ref.at[chip],
            send_sem=send_sem.at[o - 1],
            recv_sem=recv_sem.at[o - 1],
            device_id=device(lax.rem(chip + o, chips), core),
            device_id_type=MESH,
        )

    def start(o, carry):
        copy(o).start()
        return carry

    lax.fori_loop(1, chips, start, 0)
    out_ref[chip, core] = jnp.zeros(out_ref.shape[2:], out_ref.dtype)
    out_ref[chip, other] = pair[other, other]

    def finish(o, carry):
        cp = copy(o)
        cp.wait_send()
        cp.wait_recv()
        return carry

    lax.fori_loop(1, chips, finish, 0)


def exchange_states(states):
    chips = lax.axis_size(SEQ) // 2
    return pl.pallas_call(
        state_kernel,
        out_shape=jax.ShapeDtypeStruct((chips, 2) + states.shape[1:], states.dtype),
        in_specs=[pl.BlockSpec(memory_space=pltpu.VMEM)],
        out_specs=pl.BlockSpec(memory_space=pltpu.VMEM),
        scratch_shapes=[
            pltpu.VMEM((2,) + states.shape, states.dtype),
            pltpu.SemaphoreType.DMA((chips - 1,)),
            pltpu.SemaphoreType.DMA((chips - 1,)),
            pltpu.SemaphoreType.DMA((2,)),
        ],
        compiler_params=pltpu.CompilerParams(collective_id=2, has_side_effects=True),
        cost_estimate=pl.CostEstimate(flops=0, bytes_accessed=8 * states[0].size * chips, transcendentals=0),
    )(states).reshape((2 * chips,) + states.shape[1:])


def ring_kernel(n, gp_ref, w_hbm, out_ref, wbuf, acc, snd, rcv, wsem, send_sem, recv_sem):
    me = lax.axis_index("chan")
    right = lax.rem(me + 1, n)
    left = lax.rem(me + n - 1, n)
    half = out_ref.shape[1] // 2
    block = 2 * half
    tile = min(256, half)

    barrier = pltpu.get_barrier_semaphore()
    for neighbour in (left, right):
        pl.semaphore_signal(barrier, inc=1, device_id={"chan": neighbour}, device_id_type=MESH)
    pl.semaphore_wait(barrier, 2)

    def load(d, dest):
        first = pl.multiple_of(dest * block + d * half, 8)
        cp = pltpu.make_async_copy(w_hbm.at[pl.ds(first, half)], wbuf.at[d], wsem.at[d])
        cp.start()
        return cp

    def product(d):
        def body(j, carry):
            rows = pl.ds(pl.multiple_of(j * tile, tile), tile)
            acc[d, :, rows] = lax.dot_general(
                gp_ref[...], wbuf[d, rows, :], (((1,), (1,)), ((), ())),
                preferred_element_type=jnp.float32,
            )
            return carry

        lax.fori_loop(0, half // tile, body, 0)

    targets = (right, left)
    copies = [None, None]
    for step in range(n - 1):
        dests = (lax.rem(me + 2 * n - 1 - step, n), lax.rem(me + 1 + step, n))
        loads = [load(d, dests[d]) for d in (0, 1)]
        for d in (0, 1):
            loads[d].wait()
            product(d)
            if copies[d] is not None:
                copies[d].wait_recv()
                copies[d].wait_send()
                snd[d] = (acc[d] + rcv[d, step - 1].astype(jnp.float32)).astype(snd.dtype)
            else:
                snd[d] = acc[d].astype(snd.dtype)
            copies[d] = pltpu.make_async_remote_copy(
                src_ref=snd.at[d],
                dst_ref=rcv.at[d, step],
                send_sem=send_sem.at[d],
                recv_sem=recv_sem.at[d, step],
                device_id={"chan": targets[d]},
                device_id_type=MESH,
            )
            copies[d].start()
    loads = [load(d, me) for d in (0, 1)]
    for d in (0, 1):
        loads[d].wait()
        product(d)
        copies[d].wait_recv()
        copies[d].wait_send()
        out_ref[:, pl.ds(d * half, half)] = (
            acc[d] + rcv[d, n - 2].astype(jnp.float32)
        ).astype(out_ref.dtype)


def ring_reduce(grad_proj, whole_w, n):
    rows, width = grad_proj.shape
    block = whole_w.shape[0] // n
    half = block // 2
    return pl.pallas_call(
        functools.partial(ring_kernel, n),
        out_shape=jax.ShapeDtypeStruct((rows, block), jnp.bfloat16),
        in_specs=[pl.BlockSpec(memory_space=pltpu.VMEM), pl.BlockSpec(memory_space=pl.ANY)],
        out_specs=pl.BlockSpec(memory_space=pltpu.VMEM),
        scratch_shapes=[
            pltpu.VMEM((2, half, width), jnp.bfloat16),
            pltpu.VMEM((2, rows, half), jnp.float32),
            pltpu.VMEM((2, rows, half), jnp.bfloat16),
            pltpu.VMEM((2, n - 1, rows, half), jnp.bfloat16),
            pltpu.SemaphoreType.DMA((2,)),
            pltpu.SemaphoreType.DMA((2,)),
            pltpu.SemaphoreType.DMA((2, n - 1)),
        ],
        compiler_params=pltpu.CompilerParams(
            collective_id=0, has_side_effects=True, vmem_limit_bytes=60 * 1024 * 1024
        ),
        cost_estimate=pl.CostEstimate(
            flops=2 * rows * width * whole_w.shape[0],
            bytes_accessed=2 * (whole_w.size + grad_proj.size + rows * block),
            transcendentals=0,
        ),
    )(grad_proj, whole_w)


def mode_sum(amp, rates, lag):
    total = amp[0] * jnp.exp(-rates[0] * lag)
    for r in range(1, rates.shape[0]):
        total = total + amp[r] * jnp.exp(-rates[r] * lag)
    return total


def local(tokens, proj_weight, residues, decay_rates, skip_gain, grad_out):
    tok_rows = tokens.shape[0]
    chan_count = skip_gain.shape[0]
    seq_count = lax.axis_size(SEQ)
    me = lax.axis_index(SEQ)
    flat_w = proj_weight.reshape(proj_weight.shape[0], 3 * chan_count)
    whole_w = gather_rows(flat_w, 1)
    projected = jnp.dot(tokens, whole_w, preferred_element_type=f32)
    proj_vals = (
        lax.optimization_barrier(projected.astype(bf16))
        .astype(f32)
        .reshape(tok_rows, 3, chan_count)
    )
    query_in = proj_vals[:, 0]
    key_in = proj_vals[:, 1]
    value_in = proj_vals[:, 2]
    mixed_in = key_in * value_in
    grad_gate = grad_out.astype(f32)
    grad_mix = grad_gate * query_in

    rates = decay_rates
    modes = rates.shape[0]
    mode_gain = residues * jnp.sqrt(-jnp.expm1(-2.0 * rates))
    steps = jnp.arange(tok_rows, dtype=f32)

    col = steps[:, None]
    end_fwd = jnp.stack(
        [jnp.sum(jnp.exp(-rates[r] * (tok_rows - 1 - col)) * mixed_in, axis=0) for r in range(modes)]
    )
    end_bwd = jnp.stack(
        [jnp.sum(jnp.exp(-rates[r] * col) * grad_mix, axis=0) for r in range(modes)]
    )
    states = jnp.stack([end_fwd, end_bwd])
    every = exchange_states(states.astype(bf16)).astype(f32)

    others = jnp.arange(seq_count, dtype=jnp.int32)
    gap_f = me - 1 - others
    gap_b = others - me - 1
    span = rates[None] * float(tok_rows)
    w_f = jnp.where(
        (gap_f >= 0)[:, None, None],
        jnp.exp(-span * jnp.maximum(gap_f, 0).astype(f32)[:, None, None]),
        0.0,
    )
    w_b = jnp.where(
        (gap_b >= 0)[:, None, None],
        jnp.exp(-span * jnp.maximum(gap_b, 0).astype(f32)[:, None, None]),
        0.0,
    )
    into_f = jnp.sum(w_f * every, axis=0) * mode_gain
    into_b = jnp.sum(w_b * every, axis=0) * mode_gain

    taps = mode_sum(mode_gain, rates, col)
    fwd, inv = dft_tables(tok_rows)
    fwd_b = fwd.astype(bf16)
    inv_b = inv.astype(bf16)
    fwd_r, inv_r = dft_tables(tok_rows, flip=True)
    spec = jnp.dot(fwd, taps, precision=lax.Precision.HIGHEST)
    row0 = (jnp.arange(tok_rows) == 0)[:, None]
    h_a = spec[:tok_rows]
    h_a2 = jnp.where(row0, spec[tok_rows:tok_rows + 1], h_a)
    h_b = jnp.where(row0, 0.0, spec[tok_rows:])

    local_f = spectral_conv(mixed_in, fwd_b, inv_b, h_a, h_a2, h_b)
    carry_f = mode_sum(into_f, rates, col + 1.0)
    filtered = local_f + carry_f + skip_gain[None, :] * mixed_in
    gated_output = (query_in * filtered).astype(bf16)
    grad_query = grad_gate * filtered

    local_b = spectral_conv(grad_mix, fwd_r.astype(bf16), inv_r.astype(bf16), h_a, h_a2, h_b)
    carry_b = mode_sum(into_b, rates, tok_rows - col)
    grad_conv = local_b + carry_b + skip_gain[None, :] * grad_mix

    grad_proj = jnp.stack([grad_query, grad_conv * value_in, grad_conv * key_in], axis=1).astype(bf16)
    grad_proj = grad_proj.reshape(tok_rows, 3 * chan_count)
    grad_tokens = ring_reduce(grad_proj, whole_w, lax.axis_size("chan"))
    return (gated_output, grad_tokens)


SEQ = ("x", "y", "core")


def solution(mesh):
    side, cores = 4, 2
    split = jax.sharding.Mesh(
        mesh.devices.reshape(side, mesh.shape["seq"] // (side * cores), cores, mesh.shape["chan"]),
        ("x", "y", "core", "chan"),
    )
    placed = (
        P(SEQ, None),
        P(SEQ, None, "chan"),
        P(None, "chan"),
        P(None, "chan"),
        P("chan"),
        P(SEQ, "chan"),
    )
    return jax.shard_map(
        local,
        mesh=split,
        in_specs=placed,
        out_specs=(P(SEQ, "chan"), P(SEQ, "chan")),
        check_vma=False,
    )
```

```python
import functools
import math

import jax
import jax.numpy as jnp
from jax import lax
from jax.experimental import pallas as pl
from jax.experimental.pallas import tpu as pltpu
from jax.sharding import PartitionSpec as P

MESH = pl.DeviceIdType.MESH

f32 = jnp.float32
bf16 = jnp.bfloat16


def dft_tables(block_len, flip=False):
    n_len = 2 * block_len
    low = 32
    high = block_len // low
    n = jnp.arange(block_len, dtype=jnp.int32)
    if flip:
        n = block_len - 1 - n

    def trig(mult):
        phase = (mult[:, None] * n[None, :]) % n_len
        angle = (2.0 * math.pi / n_len) * phase.astype(f32)
        return jnp.cos(angle), jnp.sin(angle)

    ca, sa = trig(jnp.arange(high, dtype=jnp.int32) * low)
    cb, sb = trig(jnp.arange(low, dtype=jnp.int32))
    nyquist = jnp.where(n % 2 == 0, 1.0, -1.0).astype(f32)
    first = (jnp.arange(block_len) == 0)[:, None]
    weight = jnp.where(jnp.arange(block_len) == 0, 1.0, 2.0).astype(f32) / n_len

    cos_rows = (ca[:, None, :] * cb[None] - sa[:, None, :] * sb[None]).reshape(block_len, block_len)
    sin_rows = (sa[:, None, :] * cb[None] + ca[:, None, :] * sb[None]).reshape(block_len, block_len)
    sin_rows = jnp.where(first, nyquist[None, :], sin_rows)
    fwd = jnp.concatenate([cos_rows, sin_rows], axis=0)

    cos_t = (ca.T[:, :, None] * cb.T[:, None, :] - sa.T[:, :, None] * sb.T[:, None, :]).reshape(
        block_len, block_len
    )
    sin_t = (sa.T[:, :, None] * cb.T[:, None, :] + ca.T[:, :, None] * sb.T[:, None, :]).reshape(
        block_len, block_len
    )
    sin_t = jnp.where(first.T, nyquist[:, None], sin_t)
    inv = jnp.concatenate([cos_t * weight[None, :], sin_t * weight[None, :]], axis=1)
    return fwd, inv


def spectral_conv(signal, fwd, inv, h_a, h_a2, h_b):
    block_len = signal.shape[0]
    spec = jnp.dot(fwd, signal.astype(bf16), preferred_element_type=f32)
    xc = spec[:block_len]
    xs = spec[block_len:]
    pr = xc * h_a - xs * h_b
    pi = xc * h_b + xs * h_a2
    prod = jnp.concatenate([pr, pi], axis=0).astype(bf16)
    return jnp.dot(inv, prod, preferred_element_type=f32)


def gather_kernel(shard_ref, out_hbm, send_sem, recv_sem, local_sem):
    rows = shard_ref.shape[0]
    side = 4
    x = lax.axis_index("x")
    y = lax.axis_index("y")
    core = lax.axis_index("core")
    other = 1 - core
    a0 = x * other + y * core
    b0 = y * other + x * core

    def coords(a, b):
        a = lax.rem(a + 2 * side, side)
        b = lax.rem(b + 2 * side, side)
        return a * other + b * core, b * other + a * core

    def slot(a, b):
        xx, yy = coords(a, b)
        return out_hbm.at[pl.ds(pl.multiple_of(((xx * side + yy) * 2 + core) * rows, rows), rows)]

    def device(a, b, c):
        xx, yy = coords(a, b)
        return {"x": xx, "y": yy, "core": c}

    partner = device(a0, b0, other)
    peers = [device(a0 + 1, b0, core), device(a0 - 1, b0, core), device(a0, b0 + 1, core),
             device(a0, b0 - 1, core), partner]
    barrier = pltpu.get_barrier_semaphore()
    for peer in peers:
        pl.semaphore_signal(barrier, inc=1, device_id=peer, device_id_type=MESH)
    pl.semaphore_wait(barrier, len(peers))

    sent = {}

    def push(src, dst, target, index):
        cp = pltpu.make_async_remote_copy(
            src_ref=src, dst_ref=dst, send_sem=send_sem.at[index], recv_sem=recv_sem.at[index],
            device_id=target, device_id_type=MESH,
        )
        cp.start()
        sent[index] = cp
        return cp

    def along_b(j):
        src = slot(a0 + j, b0)
        push(src, src, device(a0, b0 + 1, core), 3 + j)
        push(src, src, device(a0, b0 - 1, core), 7 + j)

    mine = slot(a0, b0)
    own = pltpu.make_async_copy(shard_ref, mine, local_sem.at[0])
    own.start()
    up = push(shard_ref, mine, device(a0 + 1, b0, core), 0)
    down = push(shard_ref, mine, device(a0 - 1, b0, core), 1)
    own.wait()
    along_b(0)
    push(mine, mine, partner, 15)
    up.wait_recv()
    fwd = push(slot(a0 - 1, b0), slot(a0 - 1, b0), device(a0 + 1, b0, core), 2)
    along_b(3)
    push(slot(a0 - 1, b0), slot(a0 - 1, b0), partner, 16)
    down.wait_recv()
    along_b(1)
    push(slot(a0 + 1, b0), slot(a0 + 1, b0), partner, 17)
    fwd.wait_recv()
    along_b(2)
    push(slot(a0 + 2, b0), slot(a0 + 2, b0), partner, 18)
    later = {}
    for j in (0, 3, 1, 2):
        sent[3 + j].wait_recv()
        src = slot(a0 + j, b0 - 1)
        if j < 2:
            later[j] = push(src, src, device(a0, b0 + 1, core), 11 + j)
        push(src, src, partner, 19 + j)
        sent[7 + j].wait_recv()
        src = slot(a0 + j, b0 + 1)
        if j >= 2:
            later[j] = push(src, src, device(a0, b0 - 1, core), 11 + j)
        push(src, src, partner, 23 + j)
    for j in (0, 3, 1, 2):
        later[j].wait_recv()
        src = slot(a0 + j, b0 + 2)
        push(src, src, partner, 27 + j)
    for index in range(15, 31):
        pltpu.make_async_remote_copy(
            src_ref=mine, dst_ref=mine, send_sem=send_sem.at[index], recv_sem=recv_sem.at[index],
            device_id=partner, device_id_type=MESH,
        ).wait_recv()
    for index in sorted(sent):
        sent[index].wait_send()


def gather_rows(shard, collective):
    rows, width = shard.shape
    total = rows * lax.axis_size(SEQ)
    return pl.pallas_call(
        gather_kernel,
        out_shape=jax.ShapeDtypeStruct((total, width), shard.dtype),
        in_specs=[pl.BlockSpec(memory_space=pltpu.VMEM)],
        out_specs=pl.BlockSpec(memory_space=pl.ANY),
        scratch_shapes=[
            pltpu.SemaphoreType.DMA((31,)),
            pltpu.SemaphoreType.DMA((31,)),
            pltpu.SemaphoreType.DMA((1,)),
        ],
        compiler_params=pltpu.CompilerParams(collective_id=collective, has_side_effects=True),
        cost_estimate=pl.CostEstimate(flops=0, bytes_accessed=4 * total * width, transcendentals=0),
    )(shard)


def state_kernel(st_ref, out_ref, send_sem, recv_sem):
    count = out_ref.shape[0]
    side = 4
    me = (lax.axis_index("x") * side + lax.axis_index("y")) * 2 + lax.axis_index("core")

    def device(j):
        return {"x": j // (2 * side), "y": (j // 2) % side, "core": j % 2}

    barrier = pltpu.get_barrier_semaphore()

    def greet(o, carry):
        pl.semaphore_signal(barrier, inc=1, device_id=device(lax.rem(me + o, count)), device_id_type=MESH)
        return carry

    lax.fori_loop(1, count, greet, 0)
    pl.semaphore_wait(barrier, count - 1)

    def copy(o):
        j = lax.rem(me + o, count)
        return pltpu.make_async_remote_copy(
            src_ref=st_ref.at[(me + o) // count],
            dst_ref=out_ref.at[me],
            send_sem=send_sem.at[o - 1],
            recv_sem=recv_sem.at[o - 1],
            device_id=device(j),
            device_id_type=MESH,
        )

    def start(o, carry):
        copy(o).start()
        return carry

    lax.fori_loop(1, count, start, 0)
    out_ref[me] = jnp.zeros(out_ref.shape[1:], out_ref.dtype)

    def finish(o, carry):
        cp = copy(o)
        cp.wait_send()
        cp.wait_recv()
        return carry

    lax.fori_loop(1, count, finish, 0)


def exchange_states(states):
    count = lax.axis_size(SEQ)
    return pl.pallas_call(
        state_kernel,
        out_shape=jax.ShapeDtypeStruct((count,) + states.shape[1:], states.dtype),
        in_specs=[pl.BlockSpec(memory_space=pltpu.VMEM)],
        out_specs=pl.BlockSpec(memory_space=pltpu.VMEM),
        scratch_shapes=[pltpu.SemaphoreType.DMA((count - 1,)), pltpu.SemaphoreType.DMA((count - 1,))],
        compiler_params=pltpu.CompilerParams(collective_id=2, has_side_effects=True),
        cost_estimate=pl.CostEstimate(flops=0, bytes_accessed=8 * states[0].size * count, transcendentals=0),
    )(states)


def ring_kernel(n, gp_ref, w_hbm, out_ref, wbuf, acc, snd, rcv, wsem, send_sem, recv_sem):
    me = lax.axis_index("chan")
    right = lax.rem(me + 1, n)
    left = lax.rem(me + n - 1, n)
    half = out_ref.shape[1] // 2
    block = 2 * half
    tile = min(256, half)

    barrier = pltpu.get_barrier_semaphore()
    for neighbour in (left, right):
        pl.semaphore_signal(barrier, inc=1, device_id={"chan": neighbour}, device_id_type=MESH)
    pl.semaphore_wait(barrier, 2)

    def load(d, dest):
        first = pl.multiple_of(dest * block + d * half, 8)
        cp = pltpu.make_async_copy(w_hbm.at[pl.ds(first, half)], wbuf.at[d], wsem.at[d])
        cp.start()
        return cp

    def product(d):
        def body(j, carry):
            rows = pl.ds(pl.multiple_of(j * tile, tile), tile)
            acc[d, :, rows] = lax.dot_general(
                gp_ref[...], wbuf[d, rows, :], (((1,), (1,)), ((), ())),
                preferred_element_type=jnp.float32,
            )
            return carry

        lax.fori_loop(0, half // tile, body, 0)

    targets = (right, left)
    copies = [None, None]
    for step in range(n - 1):
        dests = (lax.rem(me + 2 * n - 1 - step, n), lax.rem(me + 1 + step, n))
        loads = [load(d, dests[d]) for d in (0, 1)]
        for d in (0, 1):
            loads[d].wait()
            product(d)
        for d in (0, 1):
            if copies[d] is not None:
                copies[d].wait_recv()
                copies[d].wait_send()
                snd[d] = (acc[d] + rcv[d, step - 1].astype(jnp.float32)).astype(snd.dtype)
            else:
                snd[d] = acc[d].astype(snd.dtype)
            copies[d] = pltpu.make_async_remote_copy(
                src_ref=snd.at[d],
                dst_ref=rcv.at[d, step],
                send_sem=send_sem.at[d],
                recv_sem=recv_sem.at[d, step],
                device_id={"chan": targets[d]},
                device_id_type=MESH,
            )
            copies[d].start()
    loads = [load(d, me) for d in (0, 1)]
    for d in (0, 1):
        loads[d].wait()
        product(d)
    for d in (0, 1):
        copies[d].wait_recv()
        copies[d].wait_send()
        out_ref[:, pl.ds(d * half, half)] = (
            acc[d] + rcv[d, n - 2].astype(jnp.float32)
        ).astype(out_ref.dtype)


def ring_reduce(grad_proj, whole_w, n):
    rows, width = grad_proj.shape
    block = whole_w.shape[0] // n
    half = block // 2
    return pl.pallas_call(
        functools.partial(ring_kernel, n),
        out_shape=jax.ShapeDtypeStruct((rows, block), jnp.bfloat16),
        in_specs=[pl.BlockSpec(memory_space=pltpu.VMEM), pl.BlockSpec(memory_space=pl.ANY)],
        out_specs=pl.BlockSpec(memory_space=pltpu.VMEM),
        scratch_shapes=[
            pltpu.VMEM((2, half, width), jnp.bfloat16),
            pltpu.VMEM((2, rows, half), jnp.float32),
            pltpu.VMEM((2, rows, half), jnp.bfloat16),
            pltpu.VMEM((2, n - 1, rows, half), jnp.bfloat16),
            pltpu.SemaphoreType.DMA((2,)),
            pltpu.SemaphoreType.DMA((2,)),
            pltpu.SemaphoreType.DMA((2, n - 1)),
        ],
        compiler_params=pltpu.CompilerParams(
            collective_id=0, has_side_effects=True, vmem_limit_bytes=60 * 1024 * 1024
        ),
        cost_estimate=pl.CostEstimate(
            flops=2 * rows * width * whole_w.shape[0],
            bytes_accessed=2 * (whole_w.size + grad_proj.size + rows * block),
            transcendentals=0,
        ),
    )(grad_proj, whole_w)


def mode_sum(amp, rates, lag):
    total = amp[0] * jnp.exp(-rates[0] * lag)
    for r in range(1, rates.shape[0]):
        total = total + amp[r] * jnp.exp(-rates[r] * lag)
    return total


def local(tokens, proj_weight, residues, decay_rates, skip_gain, grad_out):
    tok_rows = tokens.shape[0]
    chan_count = skip_gain.shape[0]
    seq_count = lax.axis_size(SEQ)
    me = lax.axis_index(SEQ)
    flat_w = proj_weight.reshape(proj_weight.shape[0], 3 * chan_count)
    whole_w = gather_rows(flat_w, 1)
    projected = jnp.dot(tokens, whole_w, preferred_element_type=f32)
    proj_vals = (
        lax.optimization_barrier(projected.astype(bf16))
        .astype(f32)
        .reshape(tok_rows, 3, chan_count)
    )
    query_in = proj_vals[:, 0]
    key_in = proj_vals[:, 1]
    value_in = proj_vals[:, 2]
    mixed_in = key_in * value_in
    grad_gate = grad_out.astype(f32)
    grad_mix = grad_gate * query_in

    rates = decay_rates
    modes = rates.shape[0]
    mode_gain = residues * jnp.sqrt(-jnp.expm1(-2.0 * rates))
    steps = jnp.arange(tok_rows, dtype=f32)

    col = steps[:, None]
    end_fwd = jnp.stack(
        [jnp.sum(jnp.exp(-rates[r] * (tok_rows - 1 - col)) * mixed_in, axis=0) for r in range(modes)]
    )
    end_bwd = jnp.stack(
        [jnp.sum(jnp.exp(-rates[r] * col) * grad_mix, axis=0) for r in range(modes)]
    )
    states = jnp.stack([end_fwd, end_bwd])
    every = exchange_states(states.astype(bf16)).astype(f32)

    others = jnp.arange(seq_count, dtype=jnp.int32)
    gap_f = me - 1 - others
    gap_b = others - me - 1
    span = rates[None] * float(tok_rows)
    w_f = jnp.where(
        (gap_f >= 0)[:, None, None],
        jnp.exp(-span * jnp.maximum(gap_f, 0).astype(f32)[:, None, None]),
        0.0,
    )
    w_b = jnp.where(
        (gap_b >= 0)[:, None, None],
        jnp.exp(-span * jnp.maximum(gap_b, 0).astype(f32)[:, None, None]),
        0.0,
    )
    into_f = jnp.sum(w_f * every, axis=0) * mode_gain
    into_b = jnp.sum(w_b * every, axis=0) * mode_gain

    taps = mode_sum(mode_gain, rates, col)
    fwd, inv = dft_tables(tok_rows)
    fwd_b = fwd.astype(bf16)
    inv_b = inv.astype(bf16)
    fwd_r, inv_r = dft_tables(tok_rows, flip=True)
    spec = jnp.dot(fwd, taps, precision=lax.Precision.HIGHEST)
    row0 = (jnp.arange(tok_rows) == 0)[:, None]
    h_a = spec[:tok_rows]
    h_a2 = jnp.where(row0, spec[tok_rows:tok_rows + 1], h_a)
    h_b = jnp.where(row0, 0.0, spec[tok_rows:])

    local_f = spectral_conv(mixed_in, fwd_b, inv_b, h_a, h_a2, h_b)
    carry_f = mode_sum(into_f, rates, col + 1.0)
    filtered = local_f + carry_f + skip_gain[None, :] * mixed_in
    gated_output = (query_in * filtered).astype(bf16)
    grad_query = grad_gate * filtered

    local_b = spectral_conv(grad_mix, fwd_r.astype(bf16), inv_r.astype(bf16), h_a, h_a2, h_b)
    carry_b = mode_sum(into_b, rates, tok_rows - col)
    grad_conv = local_b + carry_b + skip_gain[None, :] * grad_mix

    grad_proj = jnp.stack([grad_query, grad_conv * value_in, grad_conv * key_in], axis=1).astype(bf16)
    grad_proj = grad_proj.reshape(tok_rows, 3 * chan_count)
    grad_tokens = ring_reduce(grad_proj, whole_w, lax.axis_size("chan"))
    return (gated_output, grad_tokens)


SEQ = ("x", "y", "core")


def solution(mesh):
    side, cores = 4, 2
    split = jax.sharding.Mesh(
        mesh.devices.reshape(side, mesh.shape["seq"] // (side * cores), cores, mesh.shape["chan"]),
        ("x", "y", "core", "chan"),
    )
    placed = (
        P(SEQ, None),
        P(SEQ, None, "chan"),
        P(None, "chan"),
        P(None, "chan"),
        P("chan"),
        P(SEQ, "chan"),
    )
    return jax.shard_map(
        local,
        mesh=split,
        in_specs=placed,
        out_specs=(P(SEQ, "chan"), P(SEQ, "chan")),
        check_vma=False,
    )
```

```python
import functools
import math

import jax
import jax.numpy as jnp
from jax import lax
from jax.experimental import pallas as pl
from jax.experimental.pallas import tpu as pltpu
from jax.sharding import PartitionSpec as P

MESH = pl.DeviceIdType.MESH

f32 = jnp.float32
bf16 = jnp.bfloat16


def dft_tables(block_len, flip=False):
    n_len = 2 * block_len
    low = 32
    high = block_len // low
    n = jnp.arange(block_len, dtype=jnp.int32)
    if flip:
        n = block_len - 1 - n

    def trig(mult):
        phase = (mult[:, None] * n[None, :]) % n_len
        angle = (2.0 * math.pi / n_len) * phase.astype(f32)
        return jnp.cos(angle), jnp.sin(angle)

    ca, sa = trig(jnp.arange(high, dtype=jnp.int32) * low)
    cb, sb = trig(jnp.arange(low, dtype=jnp.int32))
    nyquist = jnp.where(n % 2 == 0, 1.0, -1.0).astype(f32)
    first = (jnp.arange(block_len) == 0)[:, None]
    weight = jnp.where(jnp.arange(block_len) == 0, 1.0, 2.0).astype(f32) / n_len

    cos_rows = (ca[:, None, :] * cb[None] - sa[:, None, :] * sb[None]).reshape(block_len, block_len)
    sin_rows = (sa[:, None, :] * cb[None] + ca[:, None, :] * sb[None]).reshape(block_len, block_len)
    sin_rows = jnp.where(first, nyquist[None, :], sin_rows)
    fwd = jnp.concatenate([cos_rows, sin_rows], axis=0)

    cos_t = (ca.T[:, :, None] * cb.T[:, None, :] - sa.T[:, :, None] * sb.T[:, None, :]).reshape(
        block_len, block_len
    )
    sin_t = (sa.T[:, :, None] * cb.T[:, None, :] + ca.T[:, :, None] * sb.T[:, None, :]).reshape(
        block_len, block_len
    )
    sin_t = jnp.where(first.T, nyquist[:, None], sin_t)
    inv = jnp.concatenate([cos_t * weight[None, :], sin_t * weight[None, :]], axis=1)
    return fwd, inv


def spectral_conv(signal, fwd, inv, h_a, h_a2, h_b):
    block_len = signal.shape[0]
    spec = jnp.dot(fwd, signal.astype(bf16), preferred_element_type=f32)
    xc = spec[:block_len]
    xs = spec[block_len:]
    pr = xc * h_a - xs * h_b
    pi = xc * h_b + xs * h_a2
    prod = jnp.concatenate([pr, pi], axis=0).astype(bf16)
    return jnp.dot(inv, prod, preferred_element_type=f32)


def gather_kernel(shard_ref, out_hbm, send_sem, recv_sem, local_sem):
    rows = shard_ref.shape[0]
    side = 4
    x = lax.axis_index("x")
    y = lax.axis_index("y")
    core = lax.axis_index("core")
    other = 1 - core
    a0 = x * other + y * core
    b0 = y * other + x * core

    def coords(a, b):
        a = lax.rem(a + 2 * side, side)
        b = lax.rem(b + 2 * side, side)
        return a * other + b * core, b * other + a * core

    def slot(a, b):
        xx, yy = coords(a, b)
        return out_hbm.at[pl.ds(pl.multiple_of(((xx * side + yy) * 2 + core) * rows, rows), rows)]

    def device(a, b, c):
        xx, yy = coords(a, b)
        return {"x": xx, "y": yy, "core": c}

    partner = device(a0, b0, other)
    peers = [device(a0 + 1, b0, core), device(a0 - 1, b0, core), device(a0, b0 + 1, core),
             device(a0, b0 - 1, core), partner]
    barrier = pltpu.get_barrier_semaphore()
    for peer in peers:
        pl.semaphore_signal(barrier, inc=1, device_id=peer, device_id_type=MESH)
    pl.semaphore_wait(barrier, len(peers))

    sent = {}

    def push(src, dst, target, index):
        cp = pltpu.make_async_remote_copy(
            src_ref=src, dst_ref=dst, send_sem=send_sem.at[index], recv_sem=recv_sem.at[index],
            device_id=target, device_id_type=MESH,
        )
        cp.start()
        sent[index] = cp
        return cp

    def along_b(j):
        src = slot(a0 + j, b0)
        push(src, src, device(a0, b0 + 1, core), 3 + j)
        push(src, src, device(a0, b0 - 1, core), 7 + j)

    mine = slot(a0, b0)
    own = pltpu.make_async_copy(shard_ref, mine, local_sem.at[0])
    own.start()
    up = push(shard_ref, mine, device(a0 + 1, b0, core), 0)
    down = push(shard_ref, mine, device(a0 - 1, b0, core), 1)
    push(shard_ref, mine, device(a0, b0 + 1, core), 3)
    push(shard_ref, mine, device(a0, b0 - 1, core), 7)
    push(shard_ref, mine, partner, 15)
    own.wait()
    up.wait_recv()
    fwd = push(slot(a0 - 1, b0), slot(a0 - 1, b0), device(a0 + 1, b0, core), 2)
    along_b(3)
    push(slot(a0 - 1, b0), slot(a0 - 1, b0), partner, 16)
    down.wait_recv()
    along_b(1)
    push(slot(a0 + 1, b0), slot(a0 + 1, b0), partner, 17)
    fwd.wait_recv()
    along_b(2)
    push(slot(a0 + 2, b0), slot(a0 + 2, b0), partner, 18)
    later = {}
    for j in (0, 3, 1, 2):
        sent[3 + j].wait_recv()
        src = slot(a0 + j, b0 - 1)
        if j < 2:
            later[j] = push(src, src, device(a0, b0 + 1, core), 11 + j)
        push(src, src, partner, 19 + j)
        sent[7 + j].wait_recv()
        src = slot(a0 + j, b0 + 1)
        if j >= 2:
            later[j] = push(src, src, device(a0, b0 - 1, core), 11 + j)
        push(src, src, partner, 23 + j)
    for j in (0, 3, 1, 2):
        later[j].wait_recv()
        src = slot(a0 + j, b0 + 2)
        push(src, src, partner, 27 + j)
    for index in range(15, 31):
        pltpu.make_async_remote_copy(
            src_ref=mine, dst_ref=mine, send_sem=send_sem.at[index], recv_sem=recv_sem.at[index],
            device_id=partner, device_id_type=MESH,
        ).wait_recv()
    for index in sorted(sent):
        sent[index].wait_send()


def gather_rows(shard, collective):
    rows, width = shard.shape
    total = rows * lax.axis_size(SEQ)
    return pl.pallas_call(
        gather_kernel,
        out_shape=jax.ShapeDtypeStruct((total, width), shard.dtype),
        in_specs=[pl.BlockSpec(memory_space=pltpu.VMEM)],
        out_specs=pl.BlockSpec(memory_space=pl.ANY),
        scratch_shapes=[
            pltpu.SemaphoreType.DMA((31,)),
            pltpu.SemaphoreType.DMA((31,)),
            pltpu.SemaphoreType.DMA((1,)),
        ],
        compiler_params=pltpu.CompilerParams(collective_id=collective, has_side_effects=True),
        cost_estimate=pl.CostEstimate(flops=0, bytes_accessed=4 * total * width, transcendentals=0),
    )(shard)


def state_kernel(st_ref, out_ref, send_sem, recv_sem):
    count = out_ref.shape[0]
    side = 4
    me = (lax.axis_index("x") * side + lax.axis_index("y")) * 2 + lax.axis_index("core")

    def device(j):
        return {"x": j // (2 * side), "y": (j // 2) % side, "core": j % 2}

    barrier = pltpu.get_barrier_semaphore()

    def greet(o, carry):
        pl.semaphore_signal(barrier, inc=1, device_id=device(lax.rem(me + o, count)), device_id_type=MESH)
        return carry

    lax.fori_loop(1, count, greet, 0)
    pl.semaphore_wait(barrier, count - 1)

    def copy(o):
        j = lax.rem(me + o, count)
        return pltpu.make_async_remote_copy(
            src_ref=st_ref.at[(me + o) // count],
            dst_ref=out_ref.at[me],
            send_sem=send_sem.at[o - 1],
            recv_sem=recv_sem.at[o - 1],
            device_id=device(j),
            device_id_type=MESH,
        )

    def start(o, carry):
        copy(o).start()
        return carry

    lax.fori_loop(1, count, start, 0)
    out_ref[me] = jnp.zeros(out_ref.shape[1:], out_ref.dtype)

    def finish(o, carry):
        cp = copy(o)
        cp.wait_send()
        cp.wait_recv()
        return carry

    lax.fori_loop(1, count, finish, 0)


def exchange_states(states):
    count = lax.axis_size(SEQ)
    return pl.pallas_call(
        state_kernel,
        out_shape=jax.ShapeDtypeStruct((count,) + states.shape[1:], states.dtype),
        in_specs=[pl.BlockSpec(memory_space=pltpu.VMEM)],
        out_specs=pl.BlockSpec(memory_space=pltpu.VMEM),
        scratch_shapes=[pltpu.SemaphoreType.DMA((count - 1,)), pltpu.SemaphoreType.DMA((count - 1,))],
        compiler_params=pltpu.CompilerParams(collective_id=2, has_side_effects=True),
        cost_estimate=pl.CostEstimate(flops=0, bytes_accessed=8 * states[0].size * count, transcendentals=0),
    )(states)


def ring_kernel(n, gp_ref, w_hbm, out_ref, wbuf, acc, snd, rcv, wsem, send_sem, recv_sem):
    me = lax.axis_index("chan")
    right = lax.rem(me + 1, n)
    left = lax.rem(me + n - 1, n)
    half = out_ref.shape[1] // 2
    block = 2 * half
    tile = min(256, half)

    barrier = pltpu.get_barrier_semaphore()
    for neighbour in (left, right):
        pl.semaphore_signal(barrier, inc=1, device_id={"chan": neighbour}, device_id_type=MESH)
    pl.semaphore_wait(barrier, 2)

    def load(d, dest):
        first = pl.multiple_of(dest * block + d * half, 8)
        cp = pltpu.make_async_copy(w_hbm.at[pl.ds(first, half)], wbuf.at[d], wsem.at[d])
        cp.start()
        return cp

    def product(d):
        def body(j, carry):
            rows = pl.ds(pl.multiple_of(j * tile, tile), tile)
            acc[d, :, rows] = lax.dot_general(
                gp_ref[...], wbuf[d, rows, :], (((1,), (1,)), ((), ())),
                preferred_element_type=jnp.float32,
            )
            return carry

        lax.fori_loop(0, half // tile, body, 0)

    targets = (right, left)
    copies = [None, None]
    for step in range(n - 1):
        dests = (lax.rem(me + 2 * n - 1 - step, n), lax.rem(me + 1 + step, n))
        loads = [load(d, dests[d]) for d in (0, 1)]
        for d in (0, 1):
            loads[d].wait()
            product(d)
            if copies[d] is not None:
                copies[d].wait_recv()
                copies[d].wait_send()
                snd[d] = (acc[d] + rcv[d, step - 1].astype(jnp.float32)).astype(snd.dtype)
            else:
                snd[d] = acc[d].astype(snd.dtype)
            copies[d] = pltpu.make_async_remote_copy(
                src_ref=snd.at[d],
                dst_ref=rcv.at[d, step],
                send_sem=send_sem.at[d],
                recv_sem=recv_sem.at[d, step],
                device_id={"chan": targets[d]},
                device_id_type=MESH,
            )
            copies[d].start()
    loads = [load(d, me) for d in (0, 1)]
    for d in (0, 1):
        loads[d].wait()
        product(d)
        copies[d].wait_recv()
        copies[d].wait_send()
        out_ref[:, pl.ds(d * half, half)] = (
            acc[d] + rcv[d, n - 2].astype(jnp.float32)
        ).astype(out_ref.dtype)


def ring_reduce(grad_proj, whole_w, n):
    rows, width = grad_proj.shape
    block = whole_w.shape[0] // n
    half = block // 2
    return pl.pallas_call(
        functools.partial(ring_kernel, n),
        out_shape=jax.ShapeDtypeStruct((rows, block), jnp.bfloat16),
        in_specs=[pl.BlockSpec(memory_space=pltpu.VMEM), pl.BlockSpec(memory_space=pl.ANY)],
        out_specs=pl.BlockSpec(memory_space=pltpu.VMEM),
        scratch_shapes=[
            pltpu.VMEM((2, half, width), jnp.bfloat16),
            pltpu.VMEM((2, rows, half), jnp.float32),
            pltpu.VMEM((2, rows, half), jnp.bfloat16),
            pltpu.VMEM((2, n - 1, rows, half), jnp.bfloat16),
            pltpu.SemaphoreType.DMA((2,)),
            pltpu.SemaphoreType.DMA((2,)),
            pltpu.SemaphoreType.DMA((2, n - 1)),
        ],
        compiler_params=pltpu.CompilerParams(
            collective_id=0, has_side_effects=True, vmem_limit_bytes=60 * 1024 * 1024
        ),
        cost_estimate=pl.CostEstimate(
            flops=2 * rows * width * whole_w.shape[0],
            bytes_accessed=2 * (whole_w.size + grad_proj.size + rows * block),
            transcendentals=0,
        ),
    )(grad_proj, whole_w)


def mode_sum(amp, rates, lag):
    total = amp[0] * jnp.exp(-rates[0] * lag)
    for r in range(1, rates.shape[0]):
        total = total + amp[r] * jnp.exp(-rates[r] * lag)
    return total


def local(tokens, proj_weight, residues, decay_rates, skip_gain, grad_out):
    tok_rows = tokens.shape[0]
    chan_count = skip_gain.shape[0]
    seq_count = lax.axis_size(SEQ)
    me = lax.axis_index(SEQ)
    flat_w = proj_weight.reshape(proj_weight.shape[0], 3 * chan_count)
    whole_w = gather_rows(flat_w, 1)
    projected = jnp.dot(tokens, whole_w, preferred_element_type=f32)
    proj_vals = (
        lax.optimization_barrier(projected.astype(bf16))
        .astype(f32)
        .reshape(tok_rows, 3, chan_count)
    )
    query_in = proj_vals[:, 0]
    key_in = proj_vals[:, 1]
    value_in = proj_vals[:, 2]
    mixed_in = key_in * value_in
    grad_gate = grad_out.astype(f32)
    grad_mix = grad_gate * query_in

    rates = decay_rates
    modes = rates.shape[0]
    mode_gain = residues * jnp.sqrt(-jnp.expm1(-2.0 * rates))
    steps = jnp.arange(tok_rows, dtype=f32)

    col = steps[:, None]
    end_fwd = jnp.stack(
        [jnp.sum(jnp.exp(-rates[r] * (tok_rows - 1 - col)) * mixed_in, axis=0) for r in range(modes)]
    )
    end_bwd = jnp.stack(
        [jnp.sum(jnp.exp(-rates[r] * col) * grad_mix, axis=0) for r in range(modes)]
    )
    states = jnp.stack([end_fwd, end_bwd])
    every = exchange_states(states.astype(bf16)).astype(f32)

    others = jnp.arange(seq_count, dtype=jnp.int32)
    gap_f = me - 1 - others
    gap_b = others - me - 1
    span = rates[None] * float(tok_rows)
    w_f = jnp.where(
        (gap_f >= 0)[:, None, None],
        jnp.exp(-span * jnp.maximum(gap_f, 0).astype(f32)[:, None, None]),
        0.0,
    )
    w_b = jnp.where(
        (gap_b >= 0)[:, None, None],
        jnp.exp(-span * jnp.maximum(gap_b, 0).astype(f32)[:, None, None]),
        0.0,
    )
    into_f = jnp.sum(w_f * every, axis=0) * mode_gain
    into_b = jnp.sum(w_b * every, axis=0) * mode_gain

    taps = mode_sum(mode_gain, rates, col)
    fwd, inv = dft_tables(tok_rows)
    fwd_b = fwd.astype(bf16)
    inv_b = inv.astype(bf16)
    fwd_r, inv_r = dft_tables(tok_rows, flip=True)
    spec = jnp.dot(fwd, taps, precision=lax.Precision.HIGHEST)
    row0 = (jnp.arange(tok_rows) == 0)[:, None]
    h_a = spec[:tok_rows]
    h_a2 = jnp.where(row0, spec[tok_rows:tok_rows + 1], h_a)
    h_b = jnp.where(row0, 0.0, spec[tok_rows:])

    local_f = spectral_conv(mixed_in, fwd_b, inv_b, h_a, h_a2, h_b)
    carry_f = mode_sum(into_f, rates, col + 1.0)
    filtered = local_f + carry_f + skip_gain[None, :] * mixed_in
    gated_output = (query_in * filtered).astype(bf16)
    grad_query = grad_gate * filtered

    local_b = spectral_conv(grad_mix, fwd_r.astype(bf16), inv_r.astype(bf16), h_a, h_a2, h_b)
    carry_b = mode_sum(into_b, rates, tok_rows - col)
    grad_conv = local_b + carry_b + skip_gain[None, :] * grad_mix

    grad_proj = jnp.stack([grad_query, grad_conv * value_in, grad_conv * key_in], axis=1).astype(bf16)
    grad_proj = grad_proj.reshape(tok_rows, 3 * chan_count)
    grad_tokens = ring_reduce(grad_proj, whole_w, lax.axis_size("chan"))
    return (gated_output, grad_tokens)


SEQ = ("x", "y", "core")


def solution(mesh):
    side, cores = 4, 2
    split = jax.sharding.Mesh(
        mesh.devices.reshape(side, mesh.shape["seq"] // (side * cores), cores, mesh.shape["chan"]),
        ("x", "y", "core", "chan"),
    )
    placed = (
        P(SEQ, None),
        P(SEQ, None, "chan"),
        P(None, "chan"),
        P(None, "chan"),
        P("chan"),
        P(SEQ, "chan"),
    )
    return jax.shard_map(
        local,
        mesh=split,
        in_specs=placed,
        out_specs=(P(SEQ, "chan"), P(SEQ, "chan")),
        check_vma=False,
    )
```
